32 devices in a mesh: blk: 8 (over z, x), rep: 4 (over y, core).
Axes of the slice: x: 2, y: 2, z: 4, core: 2. Of those that a mesh axis runs over, the one named last changes fastest.
Arguments:
- features: bfloat16 [32768, 128], P('blk'), may hold values from -6 to 6
- weight: bfloat16 [128, 256], replicated, may hold values from -0.5 to 0.5
- bias: float32 [256], replicated, may hold values from -3 to 3
- tile_values: bfloat16 [8, 8, 160, 128, 128], P('blk', 'rep'), may hold values from 0 to 0.041748047
- tile_place: int32 [8, 8, 160], P('blk', 'rep'), may hold values from 0 to 1023, as said below
- tile_count: int32 [8, 8], P('blk', 'rep'), may hold values from 1 to 160, as said below
Outputs:
- activations: bfloat16 [32768, 256], P('blk')
The draws below stay inside these ranges and needn't reach their ends.
Inputs may be any that keep to these rules, and one draw needn't show every extreme that they name: `tile_place`: within one pair of destination block and section the 160 positions are distinct. `tile_count`: some pair of destination block and section has all 160 slots occupied.
All inputs are finite; a program needn't handle non-finite values.
Results may differ from the reference program's by a relative error of at most 0.0046.
Values may be sent and summed in bfloat16 or wider, within the bound.
A program may use at most 128 MiB of HBM per device.

```python
import jax
import jax.numpy as jnp
from jax import lax

F_IN = 128
HIDDEN_SIZE = 256
TILE = 128
ROWS_BLK = 4096
SLOTS = 160
BLOCKS = 8
NODES = 32768


def draw_tile_count(key, part):
    base = jax.random.fold_in(key, 11)
    first_key, second_key, third_key = jax.random.split(base, 3)
    first_draw = jax.random.randint(first_key, (BLOCKS * BLOCKS,), 1, SLOTS + 1)
    second_draw = jax.random.randint(second_key, (BLOCKS * BLOCKS,), 1, SLOTS + 1)
    counts = jnp.minimum(first_draw, second_draw)
    chosen = jax.random.randint(third_key, (), 0, BLOCKS * BLOCKS)
    counts = jnp.where(jnp.arange(BLOCKS * BLOCKS, dtype=jnp.int32) == chosen, SLOTS, counts)
    return counts.reshape(BLOCKS, BLOCKS).astype(jnp.int32)


def draw_tile_place(key, part):
    base = jax.random.fold_in(key, 23)
    positions = ROWS_BLK // TILE * (ROWS_BLK // TILE)
    scores = jax.random.randint(base, (BLOCKS, BLOCKS, positions), 0, 2 ** 30 // positions)
    scores = scores * positions + jnp.arange(positions, dtype=jnp.int32)
    order = jnp.argsort(scores, axis=-1)
    return order[:, :, :SLOTS].astype(jnp.int32)


def block_scale(key, extent, shards, smallest, top_value):
    def one(dim, blocks):
        steps = jax.random.uniform(jax.random.fold_in(jax.random.fold_in(key, 6), dim), (blocks,), jnp.float32, smallest / len(shards), top_value / len(shards))
        return jnp.repeat(jnp.exp(steps), extent[dim] // blocks).reshape((-1,) + (1,) * (len(extent) - dim - 1))

    level = one(*shards[0])
    for cut in shards[1:]:
        level = level * one(*cut)
    return level


def centred(key, shape, spread, most, shards=(), kind=jnp.bfloat16):
    gain = block_scale(key, shape, shards, -0.22, 0.18) if shards else 1.0
    values = jax.random.normal(key, shape, jnp.float32) * spread * gain
    return jnp.minimum(jnp.maximum(values, -most), most).astype(kind)


def setup_inputs(seed: int = 0) -> dict:
    arg_keys = jax.random.split(jax.random.key(seed), 7)
    return {
        "features": centred(arg_keys[0], (NODES, F_IN), 1.0, 6.0, ((0, 8),)),
        "weight": centred(arg_keys[1], (F_IN, HIDDEN_SIZE), F_IN ** -0.5, 0.5),
        "bias": centred(arg_keys[2], (HIDDEN_SIZE,), 0.5, 3.0, (), jnp.float32),
        "tile_values": jnp.clip(0.041748047 * jax.random.uniform(arg_keys[3], (BLOCKS, BLOCKS, SLOTS, TILE, TILE), jnp.float32) ** block_scale(arg_keys[3], (BLOCKS, BLOCKS, SLOTS, TILE, TILE), ((0, 8), (1, 4)), -0.2, 0.2), 0.0, 0.041748047).astype(jnp.bfloat16),
        "tile_place": draw_tile_place(jax.random.fold_in(arg_keys[6], 71), 0),
        "tile_count": draw_tile_count(jax.random.fold_in(arg_keys[6], 71), 0),
    }


def reference(features, weight, bias, tile_values, tile_place, tile_count):
    row_tiles = ROWS_BLK // TILE
    blocked = features.reshape(BLOCKS, row_tiles, TILE, F_IN)
    section_ids = jnp.arange(BLOCKS, dtype=jnp.int32)
    slot_ids = jnp.arange(SLOTS, dtype=jnp.int32)
    tile_rows = jnp.arange(row_tiles, dtype=jnp.int32)

    def one_block(dest):
        sources = ((dest - section_ids) % BLOCKS).astype(jnp.int32)
        place = tile_place[dest]
        column = place % row_tiles
        target = place // row_tiles
        pieces = blocked[sources[:, None], column]
        products = jnp.einsum("skij,skjf->skif", tile_values[dest].astype(jnp.float32), pieces.astype(jnp.float32))
        live = (slot_ids[None, :] < tile_count[dest][:, None]).astype(jnp.float32)
        picker = (target[:, :, None] == tile_rows[None, None, :]).astype(jnp.float32) * live[:, :, None]
        summed = jnp.einsum("skr,skif->rif", picker, products, precision=lax.Precision.HIGHEST)
        return summed.reshape(ROWS_BLK, F_IN)

    summed = lax.map(one_block, jnp.arange(BLOCKS, dtype=jnp.int32)).reshape(NODES, F_IN)
    aggregated = summed.astype(jnp.bfloat16)
    output = jnp.dot(aggregated, weight, preferred_element_type=jnp.float32) + bias
    return jnp.maximum(output, 0.0).astype(jnp.bfloat16)
```

```python
import functools
import heapq

import jax
import jax.numpy as jnp
from jax import lax
from jax.experimental import pallas as pl
from jax.experimental.pallas import tpu as pltpu
from jax.sharding import PartitionSpec as P

MESH = pl.DeviceIdType.MESH
GROUP = 16
BLOCK = 80
CHUNKS = 4
PIECES = 16
HOP = 4
LEAD = 3
PASSES = 1024
ROWS_STEP = 4096
GRANT = 16 * 1024 * 1024


def largest_divisor(number, most):
    return max(d for d in range(1, most + 1) if number % d == 0)


def chip_grid(blocks, replicas):
    columns = 2
    planes = replicas // 2
    chips = [(z, x, y) for z in range(blocks // columns) for x in range(columns) for y in range(planes)]
    links = {}
    for z, x, y in chips:
        out = [(0, (z, columns - 1 - x, y)), (1, (z + 1, x, y)), (2, (z - 1, x, y))]
        out += [(3, (z, x, 1 - y))] if planes == 2 else [(3, (z, x, y + 1)), (4, (z, x, y - 1))]
        links[z, x, y] = [(way, chip) for way, chip in out if chip in set(chips)]
    return columns, planes, chips, links


def plan_trees(blocks, replicas, sections, pieces, hop, passes):
    columns, planes, chips, links = chip_grid(blocks, replicas)
    order = {chip: i for i, chip in enumerate(chips)}
    core_of = {}
    for b in range(blocks):
        for r in range(replicas):
            for i in range(sections):
                core_of[(b // columns, b % columns, r // 2), (b - r * sections - i) % blocks] = r % 2
    roots = {s: [(s // columns, s % columns, y) for y in range(planes)] for s in range(blocks)}
    wants = {s: [c for c in chips if (c, s) in core_of and c not in roots[s]] for s in range(blocks)}
    busy = {(chip, way): 0 for chip in chips for way, _ in links[chip]}
    load = dict.fromkeys(busy, 0)
    past = dict.fromkeys(busy, 0.0)
    trees, best = {}, None
    keys = [(s, p) for p in range(pieces) for s in range(blocks)]
    turn, random = list(keys), 1

    def grow(s, price):
        ready = dict.fromkeys(roots[s], 0)
        left, tree = set(wants[s]), []
        while left:
            cost, came, done = {}, {}, set()
            heap = [(0.1 * t, t, order[c], c) for c, t in ready.items()]
            heapq.heapify(heap)
            while True:
                c, t, _, chip = heapq.heappop(heap)
                if chip in done:
                    continue
                done.add(chip)
                if chip in left:
                    break
                for way, other in links[chip]:
                    if other in ready or other in done:
                        continue
                    taken = busy[chip, way] >> t
                    start = t + (~taken & (taken + 1)).bit_length() - 1
                    total = c + 0.1 * (start + hop - t) + price[chip, way]
                    if other not in cost or total < cost[other]:
                        cost[other] = total
                        came[other] = (chip, way, start)
                        heapq.heappush(heap, (total, start + hop, order[other], other))
            path = []
            while chip not in ready:
                path.append(came[chip] + (chip,))
                chip = came[chip][0]
            for chip, way, start, other in reversed(path):
                ready[other] = start + hop
                busy[chip, way] |= 1 << start
                load[chip, way] += 1
                tree.append((chip, way, start, other))
                left.discard(other)
        return tree

    for _ in range(passes):
        for key in turn:
            for chip, way, start, _ in trees.get(key, ()):
                busy[chip, way] &= ~(1 << start)
                load[chip, way] -= 1
            top = max(max(load.values()), 1)
            trees[key] = grow(key[0], {k: past[k] + (load[k] / top) ** 4 for k in load})
        last = {key: max(start for _, _, start, _ in tree) for key, tree in trees.items()}
        span = max(last.values())
        score = (span, sum(v >= span - 1 for v in last.values()), sum(load.values()))
        if best is None or score < best[0]:
            best = (score, {key: list(tree) for key, tree in trees.items()})
        top = max(load.values())
        for k in load:
            past[k] = past[k] * 0.9 + (0.2 if load[k] >= top - pieces * 0.05 else 0.0)
        ranks = []
        for key in keys:
            random = (random * 1103515245 + 12345) % (1 << 31)
            ranks.append(((random >> 8) % 1000 / 125 - last[key], key))
        turn = [key for _, key in sorted(ranks)]
    return best[1], core_of


def plan_gather(blocks, replicas, sections, pieces, hop, passes):
    trees, core_of = plan_trees(blocks, replicas, sections, pieces, hop, passes)
    columns, planes, chips, _ = chip_grid(blocks, replicas)
    devices = blocks * replicas
    actions = [[] for _ in range(devices)]
    arrived = [set() for _ in range(devices)]

    def core(chip, s, p):
        return core_of.get((chip, s), p % 2) if chip[:2] != (s // columns, s % columns) else p % 2

    def device(chip, c):
        return (chip[0] * columns + chip[1]) * replicas + chip[2] * 2 + c

    for (s, p), tree in sorted(trees.items()):
        for chip, way, start, other in tree:
            here, there = core(chip, s, p), core(other, s, p)
            own = chip[:2] == (s // columns, s % columns)
            actions[device(chip, here)].append((start - (LEAD if own else 0), not own, s * pieces + p, way, there))
            arrived[device(other, there)].add(s * pieces + p)
    plans = []
    for d in range(devices):
        slots, waited = [], set()
        for _, relay, piece, way, there in sorted(actions[d]):
            spot = None
            for j in range(len(slots) - 1, -1, -1):
                if slots[j][0] == piece:
                    spot = j
                    break
                if way in slots[j][2]:
                    break
            if spot is None:
                slots.append((piece, relay and piece not in waited, {}))
                spot = len(slots) - 1
                if relay:
                    waited.add(piece)
            slots[spot][2][way] = there
        leaves = arrived[d] - waited
        plans.append((slots, leaves))
    return plans


def gather_kernel(blocks, replicas, sections, pieces, plans, features_ref, tiles_ref, all_ref, held_ref,
                  recv_sem, send_sem, own_sem, held_sem):
    blk, rep = lax.axis_index("blk"), lax.axis_index("rep")
    columns, planes, _, _ = chip_grid(blocks, replicas)
    floors = blocks // columns
    rows = features_ref.shape[0]
    size = rows // pieces
    z, x = lax.div(blk, columns), lax.rem(blk, columns)
    y, me = lax.div(rep, 2), lax.rem(rep, 2)
    is_blk = [blk == b for b in range(blocks)]
    is_rep = [rep == r for r in range(replicas)]

    def choose(options, tests):
        value = jnp.int32(options[0])
        for option, test in zip(options[1:], tests[1:]):
            value = jnp.where(test, option, value)
        return value

    def pick(values):
        if len(set(values)) == 1:
            return jnp.int32(values[0])
        picked = []
        for b in range(blocks):
            row = values[b * replicas:(b + 1) * replicas]
            picked.append(row[0] if len(set(row)) == 1 else choose(row, is_rep))
        return choose(picked, is_blk)

    def target(way, c):
        if way == 0:
            return (z * columns + (columns - 1 - x), y * 2 + c)
        if way in (1, 2):
            return (blk + (columns if way == 1 else -columns), y * 2 + c)
        if planes == 2:
            return (blk, (1 - y) * 2 + c)
        return (blk, (y + (1 if way == 3 else -1)) * 2 + c)

    exists = {0: None, 1: z < floors - 1, 2: z > 0}
    exists.update({3: None} if planes == 2 else {3: y < planes - 1, 4: y > 0})

    own = pltpu.make_async_copy(features_ref, all_ref.at[blk], own_sem)
    own.start()
    barrier = pltpu.get_barrier_semaphore()
    count = jnp.int32(0)
    for way, test in exists.items():
        def greet(way=way):
            for c in range(2):
                pl.semaphore_signal(barrier, inc=1, device_id=target(way, c), device_id_type=MESH)
        if test is None:
            greet()
            count = count + 2
        else:
            pl.when(test)(greet)
            count = count + jnp.where(test, 2, 0)
    pl.semaphore_wait(barrier, count)

    def block(piece):
        return all_ref.at[lax.div(piece, pieces), pl.ds(pl.multiple_of(lax.rem(piece, pieces) * size, size), size)]

    def copy(piece, way, c, j):
        return pltpu.make_async_remote_copy(
            src_ref=block(piece), dst_ref=block(piece), send_sem=send_sem.at[j, way],
            recv_sem=recv_sem.at[piece], device_id=target(way, c), device_id_type=MESH)

    steps = max(len(slots) for slots, _ in plans)
    ways = len(exists)
    table = []
    for j in range(steps):
        values, used, relays = [], set(), False
        for slots, _ in plans:
            if j >= len(slots):
                values.append(0)
                continue
            piece, relay, sends = slots[j]
            value = piece * 2 + int(relay)
            for way in range(ways):
                value = value * 4 + (2 + sends[way] if way in sends else 0)
            used |= set(sends)
            relays = relays or relay
            values.append(value)
        table.append((pick(values), used, relays))

    def unpack(j):
        value, used, relays = table[j]
        head = lax.div(value, 4 ** ways)
        piece = lax.div(head, 2)
        sends = {}
        for way in sorted(used):
            field = lax.rem(lax.div(value, 4 ** (ways - 1 - way)), 4)
            sends[way] = (field >= 2, lax.rem(field, 2))
        return piece, lax.rem(head, 2) == 1, relays, sends

    own.wait()
    held = pltpu.make_async_copy(tiles_ref, held_ref, held_sem)
    for j in range(steps):
        piece, relay, relays, sends = unpack(j)
        if relays:
            pl.when(relay)(lambda piece=piece, j=j: copy(piece, 0, 0, j).wait_recv())
        for way, (test, c) in sends.items():
            pl.when(test)(lambda piece=piece, way=way, c=c, j=j: copy(piece, way, c, j).start())
        if j == 3:
            held.start()

    def drain(j):
        piece, _, _, sends = unpack(j)
        for way, (test, c) in sends.items():
            pl.when(test)(lambda piece=piece, way=way, c=c, j=j: copy(piece, way, c, j).wait_send())

    for j in range(steps * 3 // 4):
        drain(j)
    held.wait()
    for i in range(sections):
        source = lax.rem(blk - rep * sections - i + blocks, blocks)
        values = []
        for d, (_, leaves) in enumerate(plans):
            s = (d // replicas - d % replicas * sections - i) % blocks
            values.append(sum(1 << p for p in range(pieces) if s * pieces + p in leaves))
        mask = pick(values)
        for p in range(pieces):
            if any(v >> p & 1 for v in values):
                test = lax.rem(lax.div(mask, 1 << p), 2) == 1
                pl.when(test)(lambda p=p, source=source: copy(source * pieces + p, 0, 0, 0).wait_recv())
    for j in range(steps * 3 // 4, steps):
        drain(j)


def gather_sources(features, tile_values, blocks, replicas):
    sections = tile_values.shape[1]
    rows, width = features.shape
    pieces = largest_divisor(rows // 16, PIECES)
    plans = plan_gather(blocks, replicas, sections, pieces, HOP, max(2, PASSES // (blocks * replicas)))
    steps = max(len(slots) for slots, _ in plans)
    vmem = pl.BlockSpec(memory_space=pltpu.VMEM)
    hbm = pl.BlockSpec(memory_space=pl.ANY)
    dma = pltpu.SemaphoreType.DMA
    return pl.pallas_call(
        functools.partial(gather_kernel, blocks, replicas, sections, pieces, plans),
        out_shape=(
            jax.ShapeDtypeStruct((blocks, rows, width), features.dtype),
            jax.ShapeDtypeStruct(tile_values.shape, tile_values.dtype),
        ),
        in_specs=[hbm, hbm],
        out_specs=(vmem, vmem),
        scratch_shapes=[dma((blocks * pieces,)), dma((steps, 5)), dma(()), dma(())],
        compiler_params=pltpu.CompilerParams(collective_id=1, has_side_effects=True, vmem_limit_bytes=3 * GRANT),
        cost_estimate=pl.CostEstimate(
            flops=0, bytes_accessed=96 * rows * width * features.dtype.itemsize, transcendentals=0
        ),
        name="gather_sources",
    )(features, tile_values)


def sections_kernel(find, group, sections, place_ref, count_ref, source_ref, tiles_ref, acc_ref):
    step = pl.program_id(0)
    slots, tile = tiles_ref.shape[2], tiles_ref.shape[3]
    row_tiles = source_ref.shape[1] // tile
    blocks = source_ref.shape[0]
    section, chunk, active = find(step, count_ref)
    blk, rep = lax.axis_index("blk"), lax.axis_index("rep")
    source = lax.rem(blk - rep * sections - section + blocks, blocks)
    count = count_ref[0, section]
    base = chunk * slots

    @pl.when(step == 0)
    def _():
        acc_ref[...] = jnp.zeros_like(acc_ref)

    def body(g, carry):
        for u in range(group):
            k = g * group + u
            place = place_ref[0, section, base + k]
            column, target = lax.rem(place, row_tiles), lax.div(place, row_tiles)
            piece = source_ref[source, pl.ds(pl.multiple_of(column * tile, tile), tile), :]
            product = jnp.dot(tiles_ref[0, 0, k], piece, preferred_element_type=jnp.float32)
            rows = pl.ds(pl.multiple_of(target * tile, tile), tile)
            acc_ref[rows, :] += jnp.where(base + k < count, product, 0.0)
        return carry

    live = jnp.where(active, jnp.clip(count - base, 0, slots), 0)
    lax.fori_loop(0, (live + group - 1) // group, body, 0)


def section_sums(sources, tile_values, tile_place, tile_count):
    sections, slots, tile = tile_values.shape[1:4]
    rows, width = sources.shape[1:]
    block = largest_divisor(slots, BLOCK)
    group = largest_divisor(block, GROUP)

    def find(step, count_ref):
        section, chunk = jnp.int32(0), jnp.int32(0)
        start, active = jnp.int32(0), False
        for s in range(sections):
            steps = lax.div(count_ref[0, s] + block - 1, block)
            inside = step >= start
            section = jnp.where(inside, s, section)
            chunk = jnp.where(inside, jnp.minimum(step - start, steps - 1), chunk)
            start = start + steps
        return section, chunk, step < start

    def tiles_map(step, place_ref, count_ref):
        section, chunk, _ = find(step, count_ref)
        return (0, section, chunk, 0, 0)

    vmem = pl.BlockSpec(memory_space=pltpu.VMEM)
    return pl.pallas_call(
        functools.partial(sections_kernel, find, group, sections),
        out_shape=jax.ShapeDtypeStruct((rows, width), jnp.float32),
        grid_spec=pltpu.PrefetchScalarGridSpec(
            num_scalar_prefetch=2, grid=(sections * slots // block,),
            in_specs=[vmem, pl.BlockSpec((1, 1, block, tile, tile), tiles_map)], out_specs=vmem
        ),
        compiler_params=pltpu.CompilerParams(vmem_limit_bytes=GRANT),
        name="section_sums",
    )(tile_place, tile_count, sources, tile_values)


def reduce_kernel(chips, chunks, part_ref, agg_ref, core_in, send_buf, recv_buf,
                  s1, r1, s2, r2, s3, r3, s4, r4):
    blk, rep = lax.axis_index("blk"), lax.axis_index("rep")
    core, chip = lax.rem(rep, 2), lax.div(rep, 2)
    rows = part_ref.shape[0]
    half = rows // 2
    size = half // chips // chunks
    other = chip * 2 + (1 - core)

    def peer(d):
        return lax.rem(chip + d, chips)

    def local(piece, ch):
        return pl.ds(pl.multiple_of((piece * chunks + ch) * size, size), size)

    def place(which, piece, ch):
        return pl.ds(pl.multiple_of(which * half + (piece * chunks + ch) * size, size), size)

    barrier = pltpu.get_barrier_semaphore()
    pl.semaphore_signal(barrier, inc=1, device_id=(blk, other), device_id_type=MESH)
    for d in range(1, chips):
        pl.semaphore_signal(barrier, inc=1, device_id=(blk, peer(d) * 2 + core), device_id_type=MESH)
    pl.semaphore_wait(barrier, chips)

    order = [(ch, d) for ch in range(chunks) for d in list(range(1, chips)) + [0]]
    stage1, stage2, stage3, stage4 = {}, {}, {}, {}
    for ch, d in order:
        copy = pltpu.make_async_remote_copy(
            src_ref=part_ref.at[place(1 - core, peer(d), ch)], dst_ref=core_in.at[local(peer(d), ch)],
            send_sem=s1.at[d, ch], recv_sem=r1.at[d, ch], device_id=(blk, other), device_id_type=MESH)
        copy.start()
        stage1[ch, d] = copy
    for ch, d in order:
        if d == 0:
            continue
        stage1[ch, d].wait_recv()
        total = part_ref[place(core, peer(d), ch), :] + core_in[local(peer(d), ch), :]
        send_buf[d - 1, ch] = total.astype(jnp.bfloat16)
        copy = pltpu.make_async_remote_copy(
            src_ref=send_buf.at[d - 1, ch], dst_ref=recv_buf.at[d - 1, ch],
            send_sem=s2.at[d, ch], recv_sem=r2.at[d, ch],
            device_id=(blk, peer(d) * 2 + core), device_id_type=MESH)
        copy.start()
        stage2[ch, d] = copy
    for ch in range(chunks):
        stage1[ch, 0].wait_recv()
        total = part_ref[place(core, chip, ch), :] + core_in[local(chip, ch), :]
        for d in range(1, chips):
            stage2[ch, d].wait_recv()
            total = total + recv_buf[d - 1, ch].astype(jnp.float32)
        mine = place(core, chip, ch)
        agg_ref[mine, :] = total.astype(jnp.bfloat16)
        for d in list(range(1, chips)) + [0]:
            target = other if d == 0 else peer(d) * 2 + core
            copy = pltpu.make_async_remote_copy(
                src_ref=agg_ref.at[mine], dst_ref=agg_ref.at[mine],
                send_sem=s3.at[d, ch], recv_sem=r3.at[d, ch],
                device_id=(blk, target), device_id_type=MESH)
            copy.start()
            stage3[ch, d] = copy
    for ch in range(chunks):
        for d in range(1, chips):
            stage3[ch, d].wait_recv()
            came = place(core, lax.rem(chip + chips - d, chips), ch)
            copy = pltpu.make_async_remote_copy(
                src_ref=agg_ref.at[came], dst_ref=agg_ref.at[came],
                send_sem=s4.at[d, ch], recv_sem=r4.at[d, ch],
                device_id=(blk, other), device_id_type=MESH)
            copy.start()
            stage4[ch, d] = copy
    for ch, d in order:
        stage1[ch, d].wait_send()
        stage3[ch, d].wait_send()
        if d == 0:
            stage3[ch, d].wait_recv()
        else:
            stage2[ch, d].wait_send()
            stage4[ch, d].wait()


def replica_sum(part, replicas):
    rows, width = part.shape
    chips = replicas // 2
    chunks = largest_divisor(rows // 2 // chips // 16, CHUNKS)
    size = rows // 2 // chips // chunks
    dma = pltpu.SemaphoreType.DMA((chips, chunks))
    vmem = pl.BlockSpec(memory_space=pltpu.VMEM)
    return pl.pallas_call(
        functools.partial(reduce_kernel, chips, chunks),
        out_shape=jax.ShapeDtypeStruct((rows, width), jnp.bfloat16),
        in_specs=[vmem],
        out_specs=vmem,
        scratch_shapes=[
            pltpu.VMEM((rows // 2, width), jnp.float32),
            pltpu.VMEM((chips - 1, chunks, size, width), jnp.bfloat16),
            pltpu.VMEM((chips - 1, chunks, size, width), jnp.bfloat16),
        ] + [dma] * 8,
        compiler_params=pltpu.CompilerParams(collective_id=0, has_side_effects=True, vmem_limit_bytes=GRANT),
        name="replica_sum",
    )(part)


def activate_kernel(agg_ref, weight_ref, bias_ref, out_ref):
    output = jnp.dot(agg_ref[...], weight_ref[...], preferred_element_type=jnp.float32) + bias_ref[...]
    out_ref[...] = jnp.maximum(output, 0.0).astype(out_ref.dtype)


def activate(aggregated, weight, bias):
    rows, width = aggregated.shape
    hidden = weight.shape[1]
    step = largest_divisor(rows, ROWS_STEP)
    return pl.pallas_call(
        activate_kernel,
        out_shape=jax.ShapeDtypeStruct((rows, hidden), jnp.bfloat16),
        grid=(rows // step,),
        in_specs=[
            pl.BlockSpec((step, width), lambda i: (i, 0)),
            pl.BlockSpec((width, hidden), lambda i: (0, 0)),
            pl.BlockSpec((1, hidden), lambda i: (0, 0)),
        ],
        out_specs=pl.BlockSpec((step, hidden), lambda i: (i, 0)),
        compiler_params=pltpu.CompilerParams(vmem_limit_bytes=GRANT),
        name="activate",
    )(aggregated, weight, bias[None, :])


def shards(blocks, replicas, features, weight, bias, tile_values, tile_place, tile_count):
    sources, held = gather_sources(features, tile_values, blocks, replicas)
    part = section_sums(sources, held, tile_place, tile_count)
    aggregated = replica_sum(part, replicas)
    return activate(aggregated, weight, bias)


def solution(mesh):
    in_specs = (
        P("blk", None),
        P(),
        P(),
        P("blk", "rep", None, None, None),
        P("blk", "rep", None),
        P("blk", "rep"),
    )
    body = functools.partial(shards, mesh.shape["blk"], mesh.shape["rep"])
    return jax.shard_map(body, mesh=mesh, in_specs=in_specs, out_specs=P("blk", None), check_vma=False)
```

```python
import functools
import heapq

import jax
import jax.numpy as jnp
from jax import lax
from jax.experimental import pallas as pl
from jax.experimental.pallas import tpu as pltpu
from jax.sharding import PartitionSpec as P

MESH = pl.DeviceIdType.MESH
GROUP = 16
BLOCK = 80
CHUNKS = 4
PIECES = 16
HOP = 4
LEAD = 3
PASSES = 1024
ROWS_STEP = 4096
GRANT = 16 * 1024 * 1024


def largest_divisor(number, most):
    return max(d for d in range(1, most + 1) if number % d == 0)


def chip_grid(blocks, replicas):
    columns = 2
    planes = replicas // 2
    chips = [(z, x, y) for z in range(blocks // columns) for x in range(columns) for y in range(planes)]
    links = {}
    for z, x, y in chips:
        out = [(0, (z, columns - 1 - x, y)), (1, (z + 1, x, y)), (2, (z - 1, x, y))]
        out += [(3, (z, x, 1 - y))] if planes == 2 else [(3, (z, x, y + 1)), (4, (z, x, y - 1))]
        links[z, x, y] = [(way, chip) for way, chip in out if chip in set(chips)]
    return columns, planes, chips, links


def plan_trees(blocks, replicas, sections, pieces, hop, passes):
    columns, planes, chips, links = chip_grid(blocks, replicas)
    order = {chip: i for i, chip in enumerate(chips)}
    core_of = {}
    for b in range(blocks):
        for r in range(replicas):
            for i in range(sections):
                core_of[(b // columns, b % columns, r // 2), (b - r * sections - i) % blocks] = r % 2
    roots = {s: [(s // columns, s % columns, y) for y in range(planes)] for s in range(blocks)}
    wants = {s: [c for c in chips if (c, s) in core_of and c not in roots[s]] for s in range(blocks)}
    busy = {(chip, way): 0 for chip in chips for way, _ in links[chip]}
    load = dict.fromkeys(busy, 0)
    past = dict.fromkeys(busy, 0.0)
    trees, best = {}, None
    keys = [(s, p) for p in range(pieces) for s in range(blocks)]
    turn, random = list(keys), 1

    def grow(s, price):
        ready = dict.fromkeys(roots[s], 0)
        left, tree = set(wants[s]), []
        while left:
            cost, came, done = {}, {}, set()
            heap = [(0.1 * t, t, order[c], c) for c, t in ready.items()]
            heapq.heapify(heap)
            while True:
                c, t, _, chip = heapq.heappop(heap)
                if chip in done:
                    continue
                done.add(chip)
                if chip in left:
                    break
                for way, other in links[chip]:
                    if other in ready or other in done:
                        continue
                    taken = busy[chip, way] >> t
                    start = t + (~taken & (taken + 1)).bit_length() - 1
                    total = c + 0.1 * (start + hop - t) + price[chip, way]
                    if other not in cost or total < cost[other]:
                        cost[other] = total
                        came[other] = (chip, way, start)
                        heapq.heappush(heap, (total, start + hop, order[other], other))
            path = []
            while chip not in ready:
                path.append(came[chip] + (chip,))
                chip = came[chip][0]
            for chip, way, start, other in reversed(path):
                ready[other] = start + hop
                busy[chip, way] |= 1 << start
                load[chip, way] += 1
                tree.append((chip, way, start, other))
                left.discard(other)
        return tree

    for _ in range(passes):
        for key in turn:
            for chip, way, start, _ in trees.get(key, ()):
                busy[chip, way] &= ~(1 << start)
                load[chip, way] -= 1
            top = max(max(load.values()), 1)
            trees[key] = grow(key[0], {k: past[k] + (load[k] / top) ** 4 for k in load})
        last = {key: max(start for _, _, start, _ in tree) for key, tree in trees.items()}
        span = max(last.values())
        score = (span, sum(v >= span - 1 for v in last.values()), sum(load.values()))
        if best is None or score < best[0]:
            best = (score, {key: list(tree) for key, tree in trees.items()})
        top = max(load.values())
        for k in load:
            past[k] = past[k] * 0.9 + (0.2 if load[k] >= top - pieces * 0.05 else 0.0)
        ranks = []
        for key in keys:
            random = (random * 1103515245 + 12345) % (1 << 31)
            ranks.append(((random >> 8) % 1000 / 125 - last[key], key))
        turn = [key for _, key in sorted(ranks)]
    return best[1], core_of


def plan_gather(blocks, replicas, sections, pieces, hop, passes):
    trees, core_of = plan_trees(blocks, replicas, sections, pieces, hop, passes)
    columns, planes, chips, _ = chip_grid(blocks, replicas)
    devices = blocks * replicas
    actions = [[] for _ in range(devices)]
    arrived = [set() for _ in range(devices)]

    def core(chip, s, p):
        return core_of.get((chip, s), p % 2) if chip[:2] != (s // columns, s % columns) else p % 2

    def device(chip, c):
        return (chip[0] * columns + chip[1]) * replicas + chip[2] * 2 + c

    for (s, p), tree in sorted(trees.items()):
        for chip, way, start, other in tree:
            here, there = core(chip, s, p), core(other, s, p)
            own = chip[:2] == (s // columns, s % columns)
            actions[device(chip, here)].append((start - (LEAD if own else 0), not own, s * pieces + p, way, there))
            arrived[device(other, there)].add(s * pieces + p)
    plans = []
    for d in range(devices):
        slots, waited = [], set()
        for _, relay, piece, way, there in sorted(actions[d]):
            spot = None
            for j in range(len(slots) - 1, -1, -1):
                if slots[j][0] == piece:
                    spot = j
                    break
                if way in slots[j][2]:
                    break
            if spot is None:
                slots.append((piece, relay and piece not in waited, {}))
                spot = len(slots) - 1
                if relay:
                    waited.add(piece)
            slots[spot][2][way] = there
        leaves = arrived[d] - waited
        plans.append((slots, leaves))
    return plans


def gather_kernel(blocks, replicas, sections, pieces, plans, features_ref, tiles_ref, all_ref, held_ref,
                  recv_sem, send_sem, own_sem, held_sem):
    blk, rep = lax.axis_index("blk"), lax.axis_index("rep")
    columns, planes, _, _ = chip_grid(blocks, replicas)
    floors = blocks // columns
    rows = features_ref.shape[0]
    size = rows // pieces
    z, x = lax.div(blk, columns), lax.rem(blk, columns)
    y, me = lax.div(rep, 2), lax.rem(rep, 2)
    is_blk = [blk == b for b in range(blocks)]
    is_rep = [rep == r for r in range(replicas)]

    def choose(options, tests):
        value = jnp.int32(options[0])
        for option, test in zip(options[1:], tests[1:]):
            value = jnp.where(test, option, value)
        return value

    def pick(values):
        if len(set(values)) == 1:
            return jnp.int32(values[0])
        picked = []
        for b in range(blocks):
            row = values[b * replicas:(b + 1) * replicas]
            picked.append(row[0] if len(set(row)) == 1 else choose(row, is_rep))
        return choose(picked, is_blk)

    def target(way, c):
        if way == 0:
            return (z * columns + (columns - 1 - x), y * 2 + c)
        if way in (1, 2):
            return (blk + (columns if way == 1 else -columns), y * 2 + c)
        if planes == 2:
            return (blk, (1 - y) * 2 + c)
        return (blk, (y + (1 if way == 3 else -1)) * 2 + c)

    exists = {0: None, 1: z < floors - 1, 2: z > 0}
    exists.update({3: None} if planes == 2 else {3: y < planes - 1, 4: y > 0})

    own = pltpu.make_async_copy(features_ref, all_ref.at[blk], own_sem)
    own.start()
    barrier = pltpu.get_barrier_semaphore()
    count = jnp.int32(0)
    for way, test in exists.items():
        def greet(way=way):
            for c in range(2):
                pl.semaphore_signal(barrier, inc=1, device_id=target(way, c), device_id_type=MESH)
        if test is None:
            greet()
            count = count + 2
        else:
            pl.when(test)(greet)
            count = count + jnp.where(test, 2, 0)
    pl.semaphore_wait(barrier, count)

    def block(piece):
        return all_ref.at[lax.div(piece, pieces), pl.ds(pl.multiple_of(lax.rem(piece, pieces) * size, size), size)]

    def copy(piece, way, c, j):
        return pltpu.make_async_remote_copy(
            src_ref=block(piece), dst_ref=block(piece), send_sem=send_sem.at[j, way],
            recv_sem=recv_sem.at[piece], device_id=target(way, c), device_id_type=MESH)

    steps = max(len(slots) for slots, _ in plans)
    ways = len(exists)
    table = []
    for j in range(steps):
        values, used, relays = [], set(), False
        for slots, _ in plans:
            if j >= len(slots):
                values.append(0)
                continue
            piece, relay, sends = slots[j]
            value = piece * 2 + int(relay)
            for way in range(ways):
                value = value * 4 + (2 + sends[way] if way in sends else 0)
            used |= set(sends)
            relays = relays or relay
            values.append(value)
        table.append((pick(values), used, relays))

    def unpack(j):
        value, used, relays = table[j]
        head = lax.div(value, 4 ** ways)
        piece = lax.div(head, 2)
        sends = {}
        for way in sorted(used):
            field = lax.rem(lax.div(value, 4 ** (ways - 1 - way)), 4)
            sends[way] = (field >= 2, lax.rem(field, 2))
        return piece, lax.rem(head, 2) == 1, relays, sends

    own.wait()
    held = pltpu.make_async_copy(tiles_ref, held_ref, held_sem)
    for j in range(steps):
        piece, relay, relays, sends = unpack(j)
        if relays:
            pl.when(relay)(lambda piece=piece, j=j: copy(piece, 0, 0, j).wait_recv())
        for way, (test, c) in sends.items():
            pl.when(test)(lambda piece=piece, way=way, c=c, j=j: copy(piece, way, c, j).start())
        if j == 3:
            held.start()

    def drain(j):
        piece, _, _, sends = unpack(j)
        for way, (test, c) in sends.items():
            pl.when(test)(lambda piece=piece, way=way, c=c, j=j: copy(piece, way, c, j).wait_send())

    for j in range(steps * 3 // 4):
        drain(j)
    held.wait()
    for i in range(sections):
        source = lax.rem(blk - rep * sections - i + blocks, blocks)
        values = []
        for d, (_, leaves) in enumerate(plans):
            s = (d // replicas - d % replicas * sections - i) % blocks
            values.append(sum(1 << p for p in range(pieces) if s * pieces + p in leaves))
        mask = pick(values)
        for p in range(pieces):
            if any(v >> p & 1 for v in values):
                test = lax.rem(lax.div(mask, 1 << p), 2) == 1
                pl.when(test)(lambda p=p, source=source: copy(source * pieces + p, 0, 0, 0).wait_recv())
    for j in range(steps * 3 // 4, steps):
        drain(j)


def gather_sources(features, tile_values, blocks, replicas):
    sections = tile_values.shape[1]
    rows, width = features.shape
    pieces = largest_divisor(rows // 16, PIECES)
    plans = plan_gather(blocks, replicas, sections, pieces, HOP, max(2, PASSES // (blocks * replicas)))
    steps = max(len(slots) for slots, _ in plans)
    vmem = pl.BlockSpec(memory_space=pltpu.VMEM)
    hbm = pl.BlockSpec(memory_space=pltpu.HBM)
    dma = pltpu.SemaphoreType.DMA
    return pl.pallas_call(
        functools.partial(gather_kernel, blocks, replicas, sections, pieces, plans),
        out_shape=(
            jax.ShapeDtypeStruct((blocks, rows, width), features.dtype),
            jax.ShapeDtypeStruct(tile_values.shape, tile_values.dtype),
        ),
        in_specs=[hbm, hbm],
        out_specs=(vmem, vmem),
        scratch_shapes=[dma((blocks * pieces,)), dma((steps, 5)), dma(()), dma(())],
        compiler_params=pltpu.CompilerParams(collective_id=1, has_side_effects=True, vmem_limit_bytes=2 * GRANT),
        cost_estimate=pl.CostEstimate(
            flops=0, bytes_accessed=96 * rows * width * features.dtype.itemsize, transcendentals=0
        ),
        name="gather_sources",
    )(features, tile_values)


def sections_kernel(find, group, sections, place_ref, count_ref, source_ref, tiles_ref, acc_ref):
    step = pl.program_id(0)
    slots, tile = tiles_ref.shape[2], tiles_ref.shape[3]
    row_tiles = source_ref.shape[1] // tile
    blocks = source_ref.shape[0]
    section, chunk, active = find(step, count_ref)
    blk, rep = lax.axis_index("blk"), lax.axis_index("rep")
    source = lax.rem(blk - rep * sections - section + blocks, blocks)
    count = count_ref[0, section]
    base = chunk * slots

    @pl.when(step == 0)
    def _():
        acc_ref[...] = jnp.zeros_like(acc_ref)

    def body(g, carry):
        for u in range(group):
            k = g * group + u
            place = place_ref[0, section, base + k]
            column, target = lax.rem(place, row_tiles), lax.div(place, row_tiles)
            piece = source_ref[source, pl.ds(pl.multiple_of(column * tile, tile), tile), :]
            product = jnp.dot(tiles_ref[0, 0, k], piece, preferred_element_type=jnp.float32)
            rows = pl.ds(pl.multiple_of(target * tile, tile), tile)
            acc_ref[rows, :] += jnp.where(base + k < count, product, 0.0)
        return carry

    live = jnp.where(active, jnp.clip(count - base, 0, slots), 0)
    lax.fori_loop(0, (live + group - 1) // group, body, 0)


def section_sums(sources, tile_values, tile_place, tile_count):
    sections, slots, tile = tile_values.shape[1:4]
    rows, width = sources.shape[1:]
    block = largest_divisor(slots, BLOCK)
    group = largest_divisor(block, GROUP)

    def find(step, count_ref):
        section, chunk = jnp.int32(0), jnp.int32(0)
        start, active = jnp.int32(0), False
        for s in range(sections):
            steps = lax.div(count_ref[0, s] + block - 1, block)
            inside = step >= start
            section = jnp.where(inside, s, section)
            chunk = jnp.where(inside, jnp.minimum(step - start, steps - 1), chunk)
            start = start + steps
        return section, chunk, step < start

    def tiles_map(step, place_ref, count_ref):
        section, chunk, _ = find(step, count_ref)
        return (0, section, chunk, 0, 0)

    vmem = pl.BlockSpec(memory_space=pltpu.VMEM)
    return pl.pallas_call(
        functools.partial(sections_kernel, find, group, sections),
        out_shape=jax.ShapeDtypeStruct((rows, width), jnp.float32),
        grid_spec=pltpu.PrefetchScalarGridSpec(
            num_scalar_prefetch=2, grid=(sections * slots // block,),
            in_specs=[vmem, pl.BlockSpec((1, 1, block, tile, tile), tiles_map)], out_specs=vmem
        ),
        compiler_params=pltpu.CompilerParams(vmem_limit_bytes=GRANT),
        name="section_sums",
    )(tile_place, tile_count, sources, tile_values)


def reduce_kernel(chips, chunks, part_ref, agg_ref, core_in, send_buf, recv_buf,
                  s1, r1, s2, r2, s3, r3, s4, r4):
    blk, rep = lax.axis_index("blk"), lax.axis_index("rep")
    core, chip = lax.rem(rep, 2), lax.div(rep, 2)
    rows = part_ref.shape[0]
    half = rows // 2
    size = half // chips // chunks
    other = chip * 2 + (1 - core)

    def peer(d):
        return lax.rem(chip + d, chips)

    def local(piece, ch):
        return pl.ds(pl.multiple_of((piece * chunks + ch) * size, size), size)

    def place(which, piece, ch):
        return pl.ds(pl.multiple_of(which * half + (piece * chunks + ch) * size, size), size)

    barrier = pltpu.get_barrier_semaphore()
    pl.semaphore_signal(barrier, inc=1, device_id=(blk, other), device_id_type=MESH)
    for d in range(1, chips):
        pl.semaphore_signal(barrier, inc=1, device_id=(blk, peer(d) * 2 + core), device_id_type=MESH)
    pl.semaphore_wait(barrier, chips)

    order = [(ch, d) for ch in range(chunks) for d in list(range(1, chips)) + [0]]
    stage1, stage2, stage3, stage4 = {}, {}, {}, {}
    for ch, d in order:
        copy = pltpu.make_async_remote_copy(
            src_ref=part_ref.at[place(1 - core, peer(d), ch)], dst_ref=core_in.at[local(peer(d), ch)],
            send_sem=s1.at[d, ch], recv_sem=r1.at[d, ch], device_id=(blk, other), device_id_type=MESH)
        copy.start()
        stage1[ch, d] = copy
    for ch, d in order:
        if d == 0:
            continue
        stage1[ch, d].wait_recv()
        total = part_ref[place(core, peer(d), ch), :] + core_in[local(peer(d), ch), :]
        send_buf[d - 1, ch] = total.astype(jnp.bfloat16)
        copy = pltpu.make_async_remote_copy(
            src_ref=send_buf.at[d - 1, ch], dst_ref=recv_buf.at[d - 1, ch],
            send_sem=s2.at[d, ch], recv_sem=r2.at[d, ch],
            device_id=(blk, peer(d) * 2 + core), device_id_type=MESH)
        copy.start()
        stage2[ch, d] = copy
    for ch in range(chunks):
        stage1[ch, 0].wait_recv()
        total = part_ref[place(core, chip, ch), :] + core_in[local(chip, ch), :]
        for d in range(1, chips):
            stage2[ch, d].wait_recv()
            total = total + recv_buf[d - 1, ch].astype(jnp.float32)
        mine = place(core, chip, ch)
        agg_ref[mine, :] = total.astype(jnp.bfloat16)
        for d in list(range(1, chips)) + [0]:
            target = other if d == 0 else peer(d) * 2 + core
            copy = pltpu.make_async_remote_copy(
                src_ref=agg_ref.at[mine], dst_ref=agg_ref.at[mine],
                send_sem=s3.at[d, ch], recv_sem=r3.at[d, ch],
                device_id=(blk, target), device_id_type=MESH)
            copy.start()
            stage3[ch, d] = copy
    for ch in range(chunks):
        for d in range(1, chips):
            stage3[ch, d].wait_recv()
            came = place(core, lax.rem(chip + chips - d, chips), ch)
            copy = pltpu.make_async_remote_copy(
                src_ref=agg_ref.at[came], dst_ref=agg_ref.at[came],
                send_sem=s4.at[d, ch], recv_sem=r4.at[d, ch],
                device_id=(blk, other), device_id_type=MESH)
            copy.start()
            stage4[ch, d] = copy
    for ch, d in order:
        stage1[ch, d].wait_send()
        stage3[ch, d].wait_send()
        if d == 0:
            stage3[ch, d].wait_recv()
        else:
            stage2[ch, d].wait_send()
            stage4[ch, d].wait()


def replica_sum(part, replicas):
    rows, width = part.shape
    chips = replicas // 2
    chunks = largest_divisor(rows // 2 // chips // 16, CHUNKS)
    size = rows // 2 // chips // chunks
    dma = pltpu.SemaphoreType.DMA((chips, chunks))
    vmem = pl.BlockSpec(memory_space=pltpu.VMEM)
    return pl.pallas_call(
        functools.partial(reduce_kernel, chips, chunks),
        out_shape=jax.ShapeDtypeStruct((rows, width), jnp.bfloat16),
        in_specs=[vmem],
        out_specs=vmem,
        scratch_shapes=[
            pltpu.VMEM((rows // 2, width), jnp.float32),
            pltpu.VMEM((chips - 1, chunks, size, width), jnp.bfloat16),
            pltpu.VMEM((chips - 1, chunks, size, width), jnp.bfloat16),
        ] + [dma] * 8,
        compiler_params=pltpu.CompilerParams(collective_id=0, has_side_effects=True, vmem_limit_bytes=GRANT),
        name="replica_sum",
    )(part)


def activate_kernel(agg_ref, weight_ref, bias_ref, out_ref):
    output = jnp.dot(agg_ref[...], weight_ref[...], preferred_element_type=jnp.float32) + bias_ref[...]
    out_ref[...] = jnp.maximum(output, 0.0).astype(out_ref.dtype)


def activate(aggregated, weight, bias):
    rows, width = aggregated.shape
    hidden = weight.shape[1]
    step = largest_divisor(rows, ROWS_STEP)
    return pl.pallas_call(
        activate_kernel,
        out_shape=jax.ShapeDtypeStruct((rows, hidden), jnp.bfloat16),
        grid=(rows // step,),
        in_specs=[
            pl.BlockSpec((step, width), lambda i: (i, 0)),
            pl.BlockSpec((width, hidden), lambda i: (0, 0)),
            pl.BlockSpec((1, hidden), lambda i: (0, 0)),
        ],
        out_specs=pl.BlockSpec((step, hidden), lambda i: (i, 0)),
        compiler_params=pltpu.CompilerParams(vmem_limit_bytes=GRANT),
        name="activate",
    )(aggregated, weight, bias[None, :])


def shards(blocks, replicas, features, weight, bias, tile_values, tile_place, tile_count):
    sources, held = gather_sources(features, tile_values, blocks, replicas)
    part = section_sums(sources, held, tile_place, tile_count)
    aggregated = replica_sum(part, replicas)
    return activate(aggregated, weight, bias)


def solution(mesh):
    in_specs = (
        P("blk", None),
        P(),
        P(),
        P("blk", "rep", None, None, None),
        P("blk", "rep", None),
        P("blk", "rep"),
    )
    body = functools.partial(shards, mesh.shape["blk"], mesh.shape["rep"])
    return jax.shard_map(body, mesh=mesh, in_specs=in_specs, out_specs=P("blk", None), check_vma=False)
```

```python
import functools
import heapq

import jax
import jax.numpy as jnp
from jax import lax
from jax.experimental import pallas as pl
from jax.experimental.pallas import tpu as pltpu
from jax.sharding import PartitionSpec as P

MESH = pl.DeviceIdType.MESH
GROUP = 16
BLOCK = 80
CHUNKS = 4
PIECES = 16
HOP = 4
LEAD = 3
PASSES = 1024
ROWS_STEP = 1024
SWAPS = 8
GRANT = 16 * 1024 * 1024


def largest_divisor(number, most):
    return max(d for d in range(1, most + 1) if number % d == 0)


def chip_grid(blocks, replicas):
    columns = 2
    planes = replicas // 2
    chips = [(z, x, y) for z in range(blocks // columns) for x in range(columns) for y in range(planes)]
    links = {}
    for z, x, y in chips:
        out = [(0, (z, columns - 1 - x, y)), (1, (z + 1, x, y)), (2, (z - 1, x, y))]
        out += [(3, (z, x, 1 - y))] if planes == 2 else [(3, (z, x, y + 1)), (4, (z, x, y - 1))]
        links[z, x, y] = [(way, chip) for way, chip in out if chip in set(chips)]
    return columns, planes, chips, links


def plan_trees(blocks, replicas, sections, pieces, hop, passes):
    columns, planes, chips, links = chip_grid(blocks, replicas)
    order = {chip: i for i, chip in enumerate(chips)}
    core_of = {}
    for b in range(blocks):
        for r in range(replicas):
            for i in range(sections):
                core_of[(b // columns, b % columns, r // 2), (b - r * sections - i) % blocks] = r % 2
    roots = {s: [(s // columns, s % columns, y) for y in range(planes)] for s in range(blocks)}
    wants = {s: [c for c in chips if (c, s) in core_of and c not in roots[s]] for s in range(blocks)}
    busy = {(chip, way): 0 for chip in chips for way, _ in links[chip]}
    load = dict.fromkeys(busy, 0)
    past = dict.fromkeys(busy, 0.0)
    trees, best = {}, None
    keys = [(s, p) for p in range(pieces) for s in range(blocks)]
    turn, random = list(keys), 1

    def grow(s, price):
        ready = dict.fromkeys(roots[s], 0)
        left, tree = set(wants[s]), []
        while left:
            cost, came, done = {}, {}, set()
            heap = [(0.1 * t, t, order[c], c) for c, t in ready.items()]
            heapq.heapify(heap)
            while True:
                c, t, _, chip = heapq.heappop(heap)
                if chip in done:
                    continue
                done.add(chip)
                if chip in left:
                    break
                for way, other in links[chip]:
                    if other in ready or other in done:
                        continue
                    taken = busy[chip, way] >> t
                    start = t + (~taken & (taken + 1)).bit_length() - 1
                    total = c + 0.1 * (start + hop - t) + price[chip, way]
                    if other not in cost or total < cost[other]:
                        cost[other] = total
                        came[other] = (chip, way, start)
                        heapq.heappush(heap, (total, start + hop, order[other], other))
            path = []
            while chip not in ready:
                path.append(came[chip] + (chip,))
                chip = came[chip][0]
            for chip, way, start, other in reversed(path):
                ready[other] = start + hop
                busy[chip, way] |= 1 << start
                load[chip, way] += 1
                tree.append((chip, way, start, other))
                left.discard(other)
        return tree

    for _ in range(passes):
        for key in turn:
            for chip, way, start, _ in trees.get(key, ()):
                busy[chip, way] &= ~(1 << start)
                load[chip, way] -= 1
            top = max(max(load.values()), 1)
            trees[key] = grow(key[0], {k: past[k] + (load[k] / top) ** 4 for k in load})
        last = {key: max(start for _, _, start, _ in tree) for key, tree in trees.items()}
        span = max(last.values())
        score = (span, sum(v >= span - 1 for v in last.values()), sum(load.values()))
        if best is None or score < best[0]:
            best = (score, {key: list(tree) for key, tree in trees.items()})
        top = max(load.values())
        for k in load:
            past[k] = past[k] * 0.9 + (0.2 if load[k] >= top - pieces * 0.05 else 0.0)
        ranks = []
        for key in keys:
            random = (random * 1103515245 + 12345) % (1 << 31)
            ranks.append(((random >> 8) % 1000 / 125 - last[key], key))
        turn = [key for _, key in sorted(ranks)]
    return best[1], core_of


def plan_gather(blocks, replicas, sections, pieces, hop, passes):
    trees, core_of = plan_trees(blocks, replicas, sections, pieces, hop, passes)
    columns, planes, chips, _ = chip_grid(blocks, replicas)
    devices = blocks * replicas
    actions = [[] for _ in range(devices)]
    arrived = [set() for _ in range(devices)]

    def core(chip, s, p):
        return core_of.get((chip, s), p % 2) if chip[:2] != (s // columns, s % columns) else p % 2

    def device(chip, c):
        return (chip[0] * columns + chip[1]) * replicas + chip[2] * 2 + c

    for (s, p), tree in sorted(trees.items()):
        for chip, way, start, other in tree:
            here, there = core(chip, s, p), core(other, s, p)
            own = chip[:2] == (s // columns, s % columns)
            actions[device(chip, here)].append((start - (LEAD if own else 0), not own, s * pieces + p, way, there))
            arrived[device(other, there)].add(s * pieces + p)
    plans = []
    for d in range(devices):
        slots, waited = [], set()
        for _, relay, piece, way, there in sorted(actions[d]):
            spot = None
            for j in range(len(slots) - 1, -1, -1):
                if slots[j][0] == piece:
                    spot = j
                    break
                if way in slots[j][2]:
                    break
            if spot is None:
                slots.append((piece, relay and piece not in waited, {}))
                spot = len(slots) - 1
                if relay:
                    waited.add(piece)
            slots[spot][2][way] = there
        leaves = arrived[d] - waited
        plans.append((slots, leaves))
    return plans


def gather_kernel(blocks, replicas, sections, pieces, plans, features_ref, tiles_ref, all_ref, held_ref,
                  recv_sem, send_sem, own_sem, held_sem):
    blk, rep = lax.axis_index("blk"), lax.axis_index("rep")
    columns, planes, _, _ = chip_grid(blocks, replicas)
    floors = blocks // columns
    rows = features_ref.shape[0]
    size = rows // pieces
    z, x = lax.div(blk, columns), lax.rem(blk, columns)
    y, me = lax.div(rep, 2), lax.rem(rep, 2)
    is_blk = [blk == b for b in range(blocks)]
    is_rep = [rep == r for r in range(replicas)]

    def choose(options, tests):
        value = jnp.int32(options[0])
        for option, test in zip(options[1:], tests[1:]):
            value = jnp.where(test, option, value)
        return value

    def pick(values):
        if len(set(values)) == 1:
            return jnp.int32(values[0])
        picked = []
        for b in range(blocks):
            row = values[b * replicas:(b + 1) * replicas]
            picked.append(row[0] if len(set(row)) == 1 else choose(row, is_rep))
        return choose(picked, is_blk)

    def target(way, c):
        if way == 0:
            return (z * columns + (columns - 1 - x), y * 2 + c)
        if way in (1, 2):
            return (blk + (columns if way == 1 else -columns), y * 2 + c)
        if planes == 2:
            return (blk, (1 - y) * 2 + c)
        return (blk, (y + (1 if way == 3 else -1)) * 2 + c)

    exists = {0: None, 1: z < floors - 1, 2: z > 0}
    exists.update({3: None} if planes == 2 else {3: y < planes - 1, 4: y > 0})

    own = pltpu.make_async_copy(features_ref, all_ref.at[blk], own_sem)
    own.start()
    barrier = pltpu.get_barrier_semaphore()
    count = jnp.int32(0)
    for way, test in exists.items():
        def greet(way=way):
            for c in range(2):
                pl.semaphore_signal(barrier, inc=1, device_id=target(way, c), device_id_type=MESH)
        if test is None:
            greet()
            count = count + 2
        else:
            pl.when(test)(greet)
            count = count + jnp.where(test, 2, 0)
    pl.semaphore_wait(barrier, count)

    def block(piece):
        return all_ref.at[lax.div(piece, pieces), pl.ds(pl.multiple_of(lax.rem(piece, pieces) * size, size), size)]

    def copy(piece, way, c, j):
        return pltpu.make_async_remote_copy(
            src_ref=block(piece), dst_ref=block(piece), send_sem=send_sem.at[j, way],
            recv_sem=recv_sem.at[piece], device_id=target(way, c), device_id_type=MESH)

    steps = max(len(slots) for slots, _ in plans)
    ways = len(exists)
    table = []
    for j in range(steps):
        values, used, relays = [], set(), False
        for slots, _ in plans:
            if j >= len(slots):
                values.append(0)
                continue
            piece, relay, sends = slots[j]
            value = piece * 2 + int(relay)
            for way in range(ways):
                value = value * 4 + (2 + sends[way] if way in sends else 0)
            used |= set(sends)
            relays = relays or relay
            values.append(value)
        table.append((pick(values), used, relays))

    def unpack(j):
        value, used, relays = table[j]
        head = lax.div(value, 4 ** ways)
        piece = lax.div(head, 2)
        sends = {}
        for way in sorted(used):
            field = lax.rem(lax.div(value, 4 ** (ways - 1 - way)), 4)
            sends[way] = (field >= 2, lax.rem(field, 2))
        return piece, lax.rem(head, 2) == 1, relays, sends

    own.wait()
    held = pltpu.make_async_copy(tiles_ref, held_ref, held_sem)
    for j in range(steps):
        piece, relay, relays, sends = unpack(j)
        if relays:
            pl.when(relay)(lambda piece=piece, j=j: copy(piece, 0, 0, j).wait_recv())
        for way, (test, c) in sends.items():
            pl.when(test)(lambda piece=piece, way=way, c=c, j=j: copy(piece, way, c, j).start())
        if j == 3:
            held.start()

    def drain(j):
        piece, _, _, sends = unpack(j)
        for way, (test, c) in sends.items():
            pl.when(test)(lambda piece=piece, way=way, c=c, j=j: copy(piece, way, c, j).wait_send())

    for j in range(steps * 3 // 4):
        drain(j)
    held.wait()
    for i in range(sections):
        source = lax.rem(blk - rep * sections - i + blocks, blocks)
        values = []
        for d, (_, leaves) in enumerate(plans):
            s = (d // replicas - d % replicas * sections - i) % blocks
            values.append(sum(1 << p for p in range(pieces) if s * pieces + p in leaves))
        mask = pick(values)
        for p in range(pieces):
            if any(v >> p & 1 for v in values):
                test = lax.rem(lax.div(mask, 1 << p), 2) == 1
                pl.when(test)(lambda p=p, source=source: copy(source * pieces + p, 0, 0, 0).wait_recv())
    for j in range(steps * 3 // 4, steps):
        drain(j)


def gather_sources(features, tile_values, blocks, replicas):
    sections = tile_values.shape[1]
    rows, width = features.shape
    pieces = largest_divisor(rows // 16, PIECES)
    plans = plan_gather(blocks, replicas, sections, pieces, HOP, max(2, PASSES // (blocks * replicas)))
    steps = max(len(slots) for slots, _ in plans)
    vmem = pl.BlockSpec(memory_space=pltpu.VMEM)
    hbm = pl.BlockSpec(memory_space=pltpu.HBM)
    dma = pltpu.SemaphoreType.DMA
    return pl.pallas_call(
        functools.partial(gather_kernel, blocks, replicas, sections, pieces, plans),
        out_shape=(
            jax.ShapeDtypeStruct((blocks, rows, width), features.dtype),
            jax.ShapeDtypeStruct(tile_values.shape, tile_values.dtype),
        ),
        in_specs=[hbm, hbm],
        out_specs=(vmem, vmem),
        scratch_shapes=[dma((blocks * pieces,)), dma((steps, 5)), dma(()), dma(())],
        compiler_params=pltpu.CompilerParams(collective_id=1, has_side_effects=True, vmem_limit_bytes=2 * GRANT),
        cost_estimate=pl.CostEstimate(
            flops=0, bytes_accessed=96 * rows * width * features.dtype.itemsize, transcendentals=0
        ),
        name="gather_sources",
    )(pltpu.with_memory_space_constraint(features, pltpu.HBM), tile_values)


def sections_kernel(find, group, sections, place_ref, count_ref, source_ref, tiles_ref, acc_ref):
    step = pl.program_id(0)
    slots, tile = tiles_ref.shape[2], tiles_ref.shape[3]
    row_tiles = source_ref.shape[1] // tile
    blocks = source_ref.shape[0]
    section, chunk, active = find(step, count_ref)
    blk, rep = lax.axis_index("blk"), lax.axis_index("rep")
    source = lax.rem(blk - rep * sections - section + blocks, blocks)
    count = count_ref[0, section]
    base = chunk * slots

    @pl.when(step == 0)
    def _():
        acc_ref[...] = jnp.zeros_like(acc_ref)

    def body(g, carry):
        for u in range(group):
            k = g * group + u
            place = place_ref[0, section, base + k]
            column, target = lax.rem(place, row_tiles), lax.div(place, row_tiles)
            piece = source_ref[source, pl.ds(pl.multiple_of(column * tile, tile), tile), :]
            product = jnp.dot(tiles_ref[0, 0, k], piece, preferred_element_type=jnp.float32)
            rows = pl.ds(pl.multiple_of(target * tile, tile), tile)
            acc_ref[rows, :] += jnp.where(base + k < count, product, 0.0)
        return carry

    live = jnp.where(active, jnp.clip(count - base, 0, slots), 0)
    lax.fori_loop(0, (live + group - 1) // group, body, 0)


def section_sums(sources, tile_values, tile_place, tile_count):
    sections, slots, tile = tile_values.shape[1:4]
    rows, width = sources.shape[1:]
    block = largest_divisor(slots, BLOCK)
    group = largest_divisor(block, GROUP)

    def find(step, count_ref):
        section, chunk = jnp.int32(0), jnp.int32(0)
        start, active = jnp.int32(0), False
        for s in range(sections):
            steps = lax.div(count_ref[0, s] + block - 1, block)
            inside = step >= start
            section = jnp.where(inside, s, section)
            chunk = jnp.where(inside, jnp.minimum(step - start, steps - 1), chunk)
            start = start + steps
        return section, chunk, step < start

    def tiles_map(step, place_ref, count_ref):
        section, chunk, _ = find(step, count_ref)
        return (0, section, chunk, 0, 0)

    vmem = pl.BlockSpec(memory_space=pltpu.VMEM)
    return pl.pallas_call(
        functools.partial(sections_kernel, find, group, sections),
        out_shape=jax.ShapeDtypeStruct((rows, width), jnp.float32),
        grid_spec=pltpu.PrefetchScalarGridSpec(
            num_scalar_prefetch=2, grid=(sections * slots // block,),
            in_specs=[vmem, pl.BlockSpec((1, 1, block, tile, tile), tiles_map)], out_specs=vmem
        ),
        compiler_params=pltpu.CompilerParams(vmem_limit_bytes=GRANT),
        name="section_sums",
    )(tile_place, tile_count, sources, tile_values)


def swap_kernel(chunks, part_ref, agg_ref, core_in, send_buf, recv_buf, s1, r1, s2, r2, s3, r3):
    blk, rep = lax.axis_index("blk"), lax.axis_index("rep")
    core, chip = lax.rem(rep, 2), lax.div(rep, 2)
    half = part_ref.shape[0] // 2
    size = half // chunks
    other, across = chip * 2 + (1 - core), (1 - chip) * 2 + core

    def place(which, ch):
        return pl.ds(pl.multiple_of(which * half + ch * size, size), size)

    barrier = pltpu.get_barrier_semaphore()
    for target in (other, across):
        pl.semaphore_signal(barrier, inc=1, device_id=(blk, target), device_id_type=MESH)
    pl.semaphore_wait(barrier, 2)

    stage1, stage2, stage3 = [], [], []
    for ch in range(chunks):
        stage1.append(pltpu.make_async_remote_copy(
            src_ref=part_ref.at[place(1 - core, ch)], dst_ref=core_in.at[ch],
            send_sem=s1.at[ch], recv_sem=r1.at[ch], device_id=(blk, other), device_id_type=MESH))
        stage1[ch].start()
    for ch in range(chunks):
        stage1[ch].wait_recv()
        send_buf[ch] = (part_ref[place(core, ch), :] + core_in[ch]).astype(send_buf.dtype)
        stage2.append(pltpu.make_async_remote_copy(
            src_ref=send_buf.at[ch], dst_ref=recv_buf.at[ch],
            send_sem=s2.at[ch], recv_sem=r2.at[ch], device_id=(blk, across), device_id_type=MESH))
        stage2[ch].start()
    for ch in range(chunks):
        stage2[ch].wait_recv()
        mine = place(core, ch)
        total = send_buf[ch].astype(jnp.float32) + recv_buf[ch].astype(jnp.float32)
        agg_ref[mine, :] = total.astype(agg_ref.dtype)
        stage3.append(pltpu.make_async_remote_copy(
            src_ref=agg_ref.at[mine], dst_ref=agg_ref.at[mine],
            send_sem=s3.at[ch], recv_sem=r3.at[ch], device_id=(blk, other), device_id_type=MESH))
        stage3[ch].start()
    for ch in range(chunks):
        stage1[ch].wait_send()
        stage2[ch].wait_send()
        stage3[ch].wait()


def pair_sum(part):
    rows, width = part.shape
    chunks = largest_divisor(rows // 2 // 16, SWAPS)
    size = rows // 2 // chunks
    dma = pltpu.SemaphoreType.DMA((chunks,))
    vmem = pl.BlockSpec(memory_space=pltpu.VMEM)
    return pl.pallas_call(
        functools.partial(swap_kernel, chunks),
        out_shape=jax.ShapeDtypeStruct((rows, width), jnp.bfloat16),
        in_specs=[vmem],
        out_specs=vmem,
        scratch_shapes=[
            pltpu.VMEM((chunks, size, width), jnp.float32),
            pltpu.VMEM((chunks, size, width), jnp.bfloat16),
            pltpu.VMEM((chunks, size, width), jnp.bfloat16),
        ] + [dma] * 6,
        compiler_params=pltpu.CompilerParams(collective_id=0, has_side_effects=True, vmem_limit_bytes=GRANT),
        name="replica_sum",
    )(part)


def reduce_kernel(chips, chunks, part_ref, agg_ref, core_in, send_buf, recv_buf,
                  s1, r1, s2, r2, s3, r3, s4, r4):
    blk, rep = lax.axis_index("blk"), lax.axis_index("rep")
    core, chip = lax.rem(rep, 2), lax.div(rep, 2)
    rows = part_ref.shape[0]
    half = rows // 2
    size = half // chips // chunks
    other = chip * 2 + (1 - core)

    def peer(d):
        return lax.rem(chip + d, chips)

    def local(piece, ch):
        return pl.ds(pl.multiple_of((piece * chunks + ch) * size, size), size)

    def place(which, piece, ch):
        return pl.ds(pl.multiple_of(which * half + (piece * chunks + ch) * size, size), size)

    barrier = pltpu.get_barrier_semaphore()
    pl.semaphore_signal(barrier, inc=1, device_id=(blk, other), device_id_type=MESH)
    for d in range(1, chips):
        pl.semaphore_signal(barrier, inc=1, device_id=(blk, peer(d) * 2 + core), device_id_type=MESH)
    pl.semaphore_wait(barrier, chips)

    order = [(ch, d) for ch in range(chunks) for d in list(range(1, chips)) + [0]]
    stage1, stage2, stage3, stage4 = {}, {}, {}, {}
    for ch, d in order:
        copy = pltpu.make_async_remote_copy(
            src_ref=part_ref.at[place(1 - core, peer(d), ch)], dst_ref=core_in.at[local(peer(d), ch)],
            send_sem=s1.at[d, ch], recv_sem=r1.at[d, ch], device_id=(blk, other), device_id_type=MESH)
        copy.start()
        stage1[ch, d] = copy
    for ch, d in order:
        if d == 0:
            continue
        stage1[ch, d].wait_recv()
        total = part_ref[place(core, peer(d), ch), :] + core_in[local(peer(d), ch), :]
        send_buf[d - 1, ch] = total.astype(jnp.bfloat16)
        copy = pltpu.make_async_remote_copy(
            src_ref=send_buf.at[d - 1, ch], dst_ref=recv_buf.at[d - 1, ch],
            send_sem=s2.at[d, ch], recv_sem=r2.at[d, ch],
            device_id=(blk, peer(d) * 2 + core), device_id_type=MESH)
        copy.start()
        stage2[ch, d] = copy
    for ch in range(chunks):
        stage1[ch, 0].wait_recv()
        total = part_ref[place(core, chip, ch), :] + core_in[local(chip, ch), :]
        for d in range(1, chips):
            stage2[ch, d].wait_recv()
            total = total + recv_buf[d - 1, ch].astype(jnp.float32)
        mine = place(core, chip, ch)
        agg_ref[mine, :] = total.astype(jnp.bfloat16)
        for d in list(range(1, chips)) + [0]:
            target = other if d == 0 else peer(d) * 2 + core
            copy = pltpu.make_async_remote_copy(
                src_ref=agg_ref.at[mine], dst_ref=agg_ref.at[mine],
                send_sem=s3.at[d, ch], recv_sem=r3.at[d, ch],
                device_id=(blk, target), device_id_type=MESH)
            copy.start()
            stage3[ch, d] = copy
    for ch in range(chunks):
        for d in range(1, chips):
            stage3[ch, d].wait_recv()
            came = place(core, lax.rem(chip + chips - d, chips), ch)
            copy = pltpu.make_async_remote_copy(
                src_ref=agg_ref.at[came], dst_ref=agg_ref.at[came],
                send_sem=s4.at[d, ch], recv_sem=r4.at[d, ch],
                device_id=(blk, other), device_id_type=MESH)
            copy.start()
            stage4[ch, d] = copy
    for ch, d in order:
        stage1[ch, d].wait_send()
        stage3[ch, d].wait_send()
        if d == 0:
            stage3[ch, d].wait_recv()
        else:
            stage2[ch, d].wait_send()
            stage4[ch, d].wait()


def replica_sum(part, replicas):
    rows, width = part.shape
    chips = replicas // 2
    chunks = largest_divisor(rows // 2 // chips // 16, CHUNKS)
    size = rows // 2 // chips // chunks
    dma = pltpu.SemaphoreType.DMA((chips, chunks))
    vmem = pl.BlockSpec(memory_space=pltpu.VMEM)
    return pl.pallas_call(
        functools.partial(reduce_kernel, chips, chunks),
        out_shape=jax.ShapeDtypeStruct((rows, width), jnp.bfloat16),
        in_specs=[vmem],
        out_specs=vmem,
        scratch_shapes=[
            pltpu.VMEM((rows // 2, width), jnp.float32),
            pltpu.VMEM((chips - 1, chunks, size, width), jnp.bfloat16),
            pltpu.VMEM((chips - 1, chunks, size, width), jnp.bfloat16),
        ] + [dma] * 8,
        compiler_params=pltpu.CompilerParams(collective_id=0, has_side_effects=True, vmem_limit_bytes=GRANT),
        name="replica_sum",
    )(part)


def activate_kernel(agg_ref, weight_ref, bias_ref, out_ref):
    output = jnp.dot(agg_ref[...], weight_ref[...], preferred_element_type=jnp.float32) + bias_ref[...]
    out_ref[...] = jnp.maximum(output, 0.0).astype(out_ref.dtype)


def activate(aggregated, weight, bias):
    rows, width = aggregated.shape
    hidden = weight.shape[1]
    step = largest_divisor(rows, ROWS_STEP)
    return pl.pallas_call(
        activate_kernel,
        out_shape=jax.ShapeDtypeStruct((rows, hidden), jnp.bfloat16),
        grid=(rows // step,),
        in_specs=[
            pl.BlockSpec((step, width), lambda i: (i, 0)),
            pl.BlockSpec((width, hidden), lambda i: (0, 0)),
            pl.BlockSpec((1, hidden), lambda i: (0, 0)),
        ],
        out_specs=pl.BlockSpec((step, hidden), lambda i: (i, 0)),
        compiler_params=pltpu.CompilerParams(vmem_limit_bytes=GRANT),
        name="activate",
    )(aggregated, weight, bias[None, :])


def shards(blocks, replicas, features, weight, bias, tile_values, tile_place, tile_count):
    sources, held = gather_sources(features, tile_values, blocks, replicas)
    part = section_sums(sources, held, tile_place, tile_count)
    aggregated = pair_sum(part) if replicas == 4 else replica_sum(part, replicas)
    return activate(aggregated, weight, bias)


def solution(mesh):
    in_specs = (
        P("blk", None),
        P(),
        P(),
        P("blk", "rep", None, None, None),
        P("blk", "rep", None),
        P("blk", "rep"),
    )
    body = functools.partial(shards, mesh.shape["blk"], mesh.shape["rep"])
    return jax.shard_map(body, mesh=mesh, in_specs=in_specs, out_specs=P("blk", None), check_vma=False)
```

```python
import functools
import heapq

import jax
import jax.numpy as jnp
from jax import lax
from jax.experimental import pallas as pl
from jax.experimental.pallas import tpu as pltpu
from jax.sharding import PartitionSpec as P

MESH = pl.DeviceIdType.MESH
GROUP = 16
BLOCK = 80
CHUNKS = 4
PIECES = 16
HOP = 6
LEAD = 0
PASSES = 1024
SEED = 11
EXPRESS = 1
URGENCY = 0.1
TOLL = 1.0
OUT_STEPS = 8
SWAPS = 8
GRANT = 16 * 1024 * 1024


def largest_divisor(number, most):
    return max(d for d in range(1, most + 1) if number % d == 0)


def chip_grid(blocks, replicas):
    columns = 2
    floors, planes = blocks // columns, replicas // 2
    chips = [(z, x, y) for z in range(floors) for x in range(columns) for y in range(planes)]
    ways = {}
    for z, x, y in chips:
        out = [(0, (z, columns - 1 - x, y), [(z, x, y, 0)])]
        out += [(3, (z, x, 1 - y), [(z, x, y, 3)])] if planes == 2 else [
            (3 + (side < 0), (z, x, y + side), [(z, x, y, 3 + (side < 0))])
            for side in (1, -1) if 0 <= y + side < planes]
        for far in range(1, EXPRESS + 1):
            for side in (1, -1):
                if 0 <= z + side * far < floors:
                    first = 1 if far == 1 else 2 * far + 1
                    crossed = [(z + side * k, x, y, 1 + (side < 0)) for k in range(far)]
                    out.append((first + (side < 0), (z + side * far, x, y), crossed))
        ways[z, x, y] = out
    return columns, planes, chips, ways


def plan_trees(blocks, replicas, sections, pieces, hop, passes):
    columns, planes, chips, ways = chip_grid(blocks, replicas)
    order = {chip: i for i, chip in enumerate(chips)}
    core_of = {}
    for b in range(blocks):
        for r in range(replicas):
            for i in range(sections):
                core_of[(b // columns, b % columns, r // 2), (b - r * sections - i) % blocks] = r % 2
    roots = {s: [(s // columns, s % columns, y) for y in range(planes)] for s in range(blocks)}
    wants = {s: [c for c in chips if (c, s) in core_of and c not in roots[s]] for s in range(blocks)}
    busy = {link: 0 for chip in chips for _, _, crossed in ways[chip] for link in crossed}
    load = dict.fromkeys(busy, 0)
    past = dict.fromkeys(busy, 0.0)
    trees, best = {}, None
    keys = [(s, p) for p in range(pieces) for s in range(blocks)]
    turn, random = list(keys), SEED

    def grow(s, price):
        ready = dict.fromkeys(roots[s], 0)
        left, tree = set(wants[s]), []
        while left:
            cost, came, done = {}, {}, set()
            heap = [(URGENCY * t, t, order[c], c) for c, t in ready.items()]
            heapq.heapify(heap)
            while True:
                c, t, _, chip = heapq.heappop(heap)
                if chip in done:
                    continue
                done.add(chip)
                if chip in left:
                    break
                for way, other, crossed in ways[chip]:
                    if other in ready or other in done:
                        continue
                    taken, toll = 0, 0.0
                    for link in crossed:
                        taken |= busy[link]
                        toll += price[link]
                    taken >>= t
                    start = t + (~taken & (taken + 1)).bit_length() - 1
                    there = start + hop + len(crossed) - 1
                    total = c + URGENCY * (there - t) + toll
                    if other not in cost or total < cost[other]:
                        cost[other] = total
                        came[other] = (chip, way, start, crossed, there)
                        heapq.heappush(heap, (total, there, order[other], other))
            path = []
            while chip not in ready:
                path.append(came[chip] + (chip,))
                chip = came[chip][0]
            for chip, way, start, crossed, there, other in reversed(path):
                ready[other] = there
                for link in crossed:
                    busy[link] |= 1 << start
                    load[link] += 1
                tree.append((chip, way, start, other, crossed))
                left.discard(other)
        return tree

    for _ in range(passes):
        for key in turn:
            for _, _, start, _, crossed in trees.get(key, ()):
                for link in crossed:
                    busy[link] &= ~(1 << start)
                    load[link] -= 1
            top = max(max(load.values()), 1)
            trees[key] = grow(key[0], {k: TOLL * (past[k] + (load[k] / top) ** 4) for k in load})
        last = {key: max(start for _, _, start, _, _ in tree) for key, tree in trees.items()}
        span = max(last.values())
        score = (span, sum(v >= span - 1 for v in last.values()), sum(load.values()))
        if best is None or score < best[0]:
            best = (score, {key: list(tree) for key, tree in trees.items()})
        top = max(load.values())
        for k in load:
            past[k] = past[k] * 0.9 + (0.2 if load[k] >= top - pieces * 0.05 else 0.0)
        ranks = []
        for key in keys:
            random = (random * 1103515245 + 12345) % (1 << 31)
            ranks.append(((random >> 8) % 1000 / 125 - last[key], key))
        turn = [key for _, key in sorted(ranks)]
    return best[1], core_of


def plan_gather(blocks, replicas, sections, pieces, hop, passes):
    trees, core_of = plan_trees(blocks, replicas, sections, pieces, hop, passes)
    columns, planes, chips, _ = chip_grid(blocks, replicas)
    devices = blocks * replicas
    actions = [[] for _ in range(devices)]
    arrived = [set() for _ in range(devices)]

    def core(chip, s, p):
        return core_of.get((chip, s), p % 2) if chip[:2] != (s // columns, s % columns) else p % 2

    def device(chip, c):
        return (chip[0] * columns + chip[1]) * replicas + chip[2] * 2 + c

    for (s, p), tree in sorted(trees.items()):
        for chip, way, start, other, _ in tree:
            here, there = core(chip, s, p), core(other, s, p)
            own = chip[:2] == (s // columns, s % columns)
            actions[device(chip, here)].append((start - (LEAD if own else 0), not own, s * pieces + p, way, there))
            arrived[device(other, there)].add(s * pieces + p)
    plans = []
    for d in range(devices):
        slots, waited = [], set()
        for _, relay, piece, way, there in sorted(actions[d]):
            spot = None
            for j in range(len(slots) - 1, -1, -1):
                if slots[j][0] == piece:
                    spot = j
                    break
                if way in slots[j][2]:
                    break
            if spot is None:
                slots.append((piece, relay and piece not in waited, {}))
                spot = len(slots) - 1
                if relay:
                    waited.add(piece)
            slots[spot][2][way] = there
        leaves = arrived[d] - waited
        plans.append((slots, leaves))
    return plans


def used_ways(plans):
    used = {way for slots, _ in plans for _, _, sends in slots for way in sends}
    pairs = {1: 2, 2: 1, 3: 3, 4: 3}
    return sorted(used | {0 if w == 0 else pairs.get(w, w + 1 if w % 2 else w - 1) for w in used})


def gather_kernel(blocks, replicas, sections, pieces, plans, features_ref, tiles_ref, all_ref, held_ref,
                  table_ref, recv_sem, send_sem, own_sem, held_sem):
    blk, rep = lax.axis_index("blk"), lax.axis_index("rep")
    columns, planes, _, _ = chip_grid(blocks, replicas)
    floors = blocks // columns
    rows = features_ref.shape[0]
    size = rows // pieces
    z, x = lax.div(blk, columns), lax.rem(blk, columns)
    y, me = lax.div(rep, 2), lax.rem(rep, 2)
    is_blk = [blk == b for b in range(blocks)]
    is_rep = [rep == r for r in range(replicas)]

    def choose(options, tests):
        value = jnp.int32(options[0])
        for option, test in zip(options[1:], tests[1:]):
            value = jnp.where(test, option, value)
        return value

    def pick(values):
        if len(set(values)) == 1:
            return jnp.int32(values[0])
        picked = []
        for b in range(blocks):
            row = values[b * replicas:(b + 1) * replicas]
            picked.append(row[0] if len(set(row)) == 1 else choose(row, is_rep))
        return choose(picked, is_blk)

    def target(way, c):
        if way == 0:
            return (z * columns + (columns - 1 - x), y * 2 + c)
        if way in (3, 4):
            return (blk, (1 - y if planes == 2 else y + (1 if way == 3 else -1)) * 2 + c)
        far = 1 if way < 3 else (way - 1) // 2
        return (blk + (far if way % 2 else -far) * columns, y * 2 + c)

    exists = {}
    for way in used_ways(plans):
        if way == 0 or (way == 3 and planes == 2):
            exists[way] = None
        elif way in (3, 4):
            exists[way] = y < planes - 1 if way == 3 else y > 0
        else:
            far = 1 if way < 3 else (way - 1) // 2
            exists[way] = z < floors - far if way % 2 else z >= far

    own = pltpu.make_async_copy(features_ref, all_ref.at[blk], own_sem)
    own.start()
    steps = max(len(slots) for slots, _ in plans)
    ways = sorted(exists)
    shift = pieces.bit_length() - 1
    for j in range(steps):
        values = []
        for slots, _ in plans:
            piece, relay, sends = slots[j] if j < len(slots) else (0, False, {})
            values.append((piece * 2 + int(relay) << 2 * len(ways)) + sum(2 + sends[w] << 2 * k for k, w in enumerate(ways) if w in sends))
        table_ref[j] = pick(values)
    run = min(pieces, 16)
    words = [(i, first) for i in range(sections) for first in range(0, pieces, run)]
    for n, (i, first) in enumerate(words):
        values = []
        for d, (_, leaves) in enumerate(plans):
            s = (d // replicas - d % replicas * sections - i) % blocks
            values.append(sum(1 << p for p in range(run) if s * pieces + first + p in leaves))
        table_ref[steps + n] = pick(values)

    barrier = pltpu.get_barrier_semaphore()
    count = jnp.int32(0)
    for way, test in exists.items():
        def greet(way=way):
            for c in range(2):
                pl.semaphore_signal(barrier, inc=1, device_id=target(way, c), device_id_type=MESH)
        if test is None:
            greet()
            count = count + 2
        else:
            pl.when(test)(greet)
            count = count + jnp.where(test, 2, 0)
    pl.semaphore_wait(barrier, count)

    def block(piece):
        return all_ref.at[piece >> shift, pl.ds(pl.multiple_of((piece & (pieces - 1)) * size, size), size)]

    def copy(piece, way, c, j):
        return pltpu.make_async_remote_copy(
            src_ref=block(piece), dst_ref=block(piece), send_sem=send_sem.at[j, ways.index(way)],
            recv_sem=recv_sem.at[piece], device_id=target(way, c), device_id_type=MESH)

    def unpack(j):
        value = table_ref[j]
        return value >> (2 * len(ways) + 1), (value >> (2 * len(ways))) & 1 == 1, [
            (way, (value >> (2 * k + 1)) & 1 == 1, (value >> (2 * k)) & 1) for k, way in enumerate(ways)]

    own.wait()
    held = pltpu.make_async_copy(tiles_ref, held_ref, held_sem)
    held.start()

    def step(j, carry):
        piece, relay, sends = unpack(j)
        pl.when(relay)(lambda: copy(piece, 0, 0, j).wait_recv())
        for way, test, c in sends:
            pl.when(test)(lambda way=way, c=c: copy(piece, way, c, j).start())
        return carry

    def drain(j, carry):
        piece, _, sends = unpack(j)
        for way, test, c in sends:
            pl.when(test)(lambda way=way, c=c: copy(piece, way, c, j).wait_send())
        return carry

    lax.fori_loop(0, steps, step, 0)
    lax.fori_loop(0, steps * 3 // 4, drain, 0)
    for n, (i, first) in enumerate(words):
        source = lax.rem(blk - rep * sections - i + blocks, blocks)
        mask = table_ref[steps + n]

        def leaf(p, carry, start=source * pieces + first, mask=mask):
            pl.when((mask >> p) & 1 == 1)(lambda: copy(start + p, 0, 0, 0).wait_recv())
            return carry

        lax.fori_loop(0, run, leaf, 0)
    lax.fori_loop(steps * 3 // 4, steps, drain, 0)
    held.wait()


def gather_sources(features, tile_values, blocks, replicas):
    sections = tile_values.shape[1]
    rows, width = features.shape
    pieces = PIECES
    while rows % (16 * pieces):
        pieces //= 2
    plans = plan_gather(blocks, replicas, sections, pieces, HOP, max(2, PASSES // (blocks * replicas)))
    steps = max(len(slots) for slots, _ in plans)
    ways = len(used_ways(plans))
    vmem = pl.BlockSpec(memory_space=pltpu.VMEM)
    hbm = pl.BlockSpec(memory_space=pltpu.HBM)
    dma = pltpu.SemaphoreType.DMA
    return pl.pallas_call(
        functools.partial(gather_kernel, blocks, replicas, sections, pieces, plans),
        out_shape=(
            jax.ShapeDtypeStruct((blocks, rows, width), features.dtype),
            jax.ShapeDtypeStruct(tile_values.shape, tile_values.dtype),
        ),
        in_specs=[hbm, hbm],
        out_specs=(vmem, vmem),
        scratch_shapes=[
            pltpu.SMEM((steps + sections * pl.cdiv(pieces, 16),), jnp.int32), dma((blocks * pieces,)), dma((steps, ways)), dma(()), dma(())
        ],
        compiler_params=pltpu.CompilerParams(collective_id=1, has_side_effects=True, vmem_limit_bytes=2 * GRANT),
        cost_estimate=pl.CostEstimate(
            flops=0, bytes_accessed=96 * rows * width * features.dtype.itemsize, transcendentals=0
        ),
        name="gather_sources",
    )(pltpu.with_memory_space_constraint(features, pltpu.HBM), tile_values)


def sections_kernel(find, group, sections, place_ref, count_ref, source_ref, tiles_ref, acc_ref):
    step = pl.program_id(0)
    slots, tile = tiles_ref.shape[2], tiles_ref.shape[3]
    row_tiles = source_ref.shape[1] // tile
    blocks = source_ref.shape[0]
    section, chunk, active = find(step, count_ref)
    blk, rep = lax.axis_index("blk"), lax.axis_index("rep")
    source = lax.rem(blk - rep * sections - section + blocks, blocks)
    count = count_ref[0, section]
    base = chunk * slots

    @pl.when(step == 0)
    def _():
        acc_ref[...] = jnp.zeros_like(acc_ref)

    def body(g, carry):
        for u in range(group):
            k = g * group + u
            place = place_ref[0, section, base + k]
            column, target = lax.rem(place, row_tiles), lax.div(place, row_tiles)
            piece = source_ref[source, pl.ds(pl.multiple_of(column * tile, tile), tile), :]
            product = jnp.dot(tiles_ref[0, 0, k], piece, preferred_element_type=jnp.float32)
            rows = pl.ds(pl.multiple_of(target * tile, tile), tile)
            acc_ref[rows, :] += jnp.where(base + k < count, product, 0.0)
        return carry

    live = jnp.where(active, jnp.clip(count - base, 0, slots), 0)
    lax.fori_loop(0, (live + group - 1) // group, body, 0)


def section_sums(sources, tile_values, tile_place, tile_count):
    sections, slots, tile = tile_values.shape[1:4]
    rows, width = sources.shape[1:]
    block = largest_divisor(slots, BLOCK)
    group = largest_divisor(block, GROUP)

    def find(step, count_ref):
        section, chunk = jnp.int32(0), jnp.int32(0)
        start, active = jnp.int32(0), False
        for s in range(sections):
            steps = lax.div(count_ref[0, s] + block - 1, block)
            inside = step >= start
            section = jnp.where(inside, s, section)
            chunk = jnp.where(inside, jnp.minimum(step - start, steps - 1), chunk)
            start = start + steps
        return section, chunk, step < start

    def tiles_map(step, place_ref, count_ref):
        section, chunk, _ = find(step, count_ref)
        return (0, section, chunk, 0, 0)

    vmem = pl.BlockSpec(memory_space=pltpu.VMEM)
    return pl.pallas_call(
        functools.partial(sections_kernel, find, group, sections),
        out_shape=jax.ShapeDtypeStruct((rows, width), jnp.float32),
        grid_spec=pltpu.PrefetchScalarGridSpec(
            num_scalar_prefetch=2, grid=(sections * slots // block,),
            in_specs=[vmem, pl.BlockSpec((1, 1, block, tile, tile), tiles_map)], out_specs=vmem
        ),
        compiler_params=pltpu.CompilerParams(vmem_limit_bytes=GRANT),
        name="section_sums",
    )(tile_place, tile_count, sources, tile_values)


def swap_kernel(chunks, part_ref, agg_ref, core_in, send_buf, recv_buf, s1, r1, s2, r2, s3, r3):
    blk, rep = lax.axis_index("blk"), lax.axis_index("rep")
    core, chip = lax.rem(rep, 2), lax.div(rep, 2)
    half = part_ref.shape[0] // 2
    size = half // chunks
    other, across = chip * 2 + (1 - core), (1 - chip) * 2 + core

    def place(which, ch):
        return pl.ds(pl.multiple_of(which * half + ch * size, size), size)

    barrier = pltpu.get_barrier_semaphore()
    for target in (other, across):
        pl.semaphore_signal(barrier, inc=1, device_id=(blk, target), device_id_type=MESH)
    pl.semaphore_wait(barrier, 2)

    stage1, stage2, stage3 = [], [], []
    for ch in range(chunks):
        stage1.append(pltpu.make_async_remote_copy(
            src_ref=part_ref.at[place(1 - core, ch)], dst_ref=core_in.at[ch],
            send_sem=s1.at[ch], recv_sem=r1.at[ch], device_id=(blk, other), device_id_type=MESH))
        stage1[ch].start()
    for ch in range(chunks):
        stage1[ch].wait_recv()
        send_buf[ch] = (part_ref[place(core, ch), :] + core_in[ch]).astype(send_buf.dtype)
        stage2.append(pltpu.make_async_remote_copy(
            src_ref=send_buf.at[ch], dst_ref=recv_buf.at[ch],
            send_sem=s2.at[ch], recv_sem=r2.at[ch], device_id=(blk, across), device_id_type=MESH))
        stage2[ch].start()
    for ch in range(chunks):
        stage2[ch].wait_recv()
        mine = place(core, ch)
        total = send_buf[ch].astype(jnp.float32) + recv_buf[ch].astype(jnp.float32)
        agg_ref[mine, :] = total.astype(agg_ref.dtype)
        stage3.append(pltpu.make_async_remote_copy(
            src_ref=agg_ref.at[mine], dst_ref=agg_ref.at[mine],
            send_sem=s3.at[ch], recv_sem=r3.at[ch], device_id=(blk, other), device_id_type=MESH))
        stage3[ch].start()
    for ch in range(chunks):
        stage1[ch].wait_send()
        stage2[ch].wait_send()
        stage3[ch].wait()


def pair_sum(part):
    rows, width = part.shape
    chunks = largest_divisor(rows // 2 // 16, SWAPS)
    size = rows // 2 // chunks
    dma = pltpu.SemaphoreType.DMA((chunks,))
    vmem = pl.BlockSpec(memory_space=pltpu.VMEM)
    return pl.pallas_call(
        functools.partial(swap_kernel, chunks),
        out_shape=jax.ShapeDtypeStruct((rows, width), jnp.bfloat16),
        in_specs=[vmem],
        out_specs=vmem,
        scratch_shapes=[
            pltpu.VMEM((chunks, size, width), jnp.float32),
            pltpu.VMEM((chunks, size, width), jnp.bfloat16),
            pltpu.VMEM((chunks, size, width), jnp.bfloat16),
        ] + [dma] * 6,
        compiler_params=pltpu.CompilerParams(collective_id=0, has_side_effects=True, vmem_limit_bytes=GRANT),
        name="replica_sum",
    )(part)


def reduce_kernel(chips, chunks, part_ref, agg_ref, core_in, send_buf, recv_buf,
                  s1, r1, s2, r2, s3, r3, s4, r4):
    blk, rep = lax.axis_index("blk"), lax.axis_index("rep")
    core, chip = lax.rem(rep, 2), lax.div(rep, 2)
    rows = part_ref.shape[0]
    half = rows // 2
    size = half // chips // chunks
    other = chip * 2 + (1 - core)

    def peer(d):
        return lax.rem(chip + d, chips)

    def local(piece, ch):
        return pl.ds(pl.multiple_of((piece * chunks + ch) * size, size), size)

    def place(which, piece, ch):
        return pl.ds(pl.multiple_of(which * half + (piece * chunks + ch) * size, size), size)

    barrier = pltpu.get_barrier_semaphore()
    pl.semaphore_signal(barrier, inc=1, device_id=(blk, other), device_id_type=MESH)
    for d in range(1, chips):
        pl.semaphore_signal(barrier, inc=1, device_id=(blk, peer(d) * 2 + core), device_id_type=MESH)
    pl.semaphore_wait(barrier, chips)

    order = [(ch, d) for ch in range(chunks) for d in list(range(1, chips)) + [0]]
    stage1, stage2, stage3, stage4 = {}, {}, {}, {}
    for ch, d in order:
        copy = pltpu.make_async_remote_copy(
            src_ref=part_ref.at[place(1 - core, peer(d), ch)], dst_ref=core_in.at[local(peer(d), ch)],
            send_sem=s1.at[d, ch], recv_sem=r1.at[d, ch], device_id=(blk, other), device_id_type=MESH)
        copy.start()
        stage1[ch, d] = copy
    for ch, d in order:
        if d == 0:
            continue
        stage1[ch, d].wait_recv()
        total = part_ref[place(core, peer(d), ch), :] + core_in[local(peer(d), ch), :]
        send_buf[d - 1, ch] = total.astype(jnp.bfloat16)
        copy = pltpu.make_async_remote_copy(
            src_ref=send_buf.at[d - 1, ch], dst_ref=recv_buf.at[d - 1, ch],
            send_sem=s2.at[d, ch], recv_sem=r2.at[d, ch],
            device_id=(blk, peer(d) * 2 + core), device_id_type=MESH)
        copy.start()
        stage2[ch, d] = copy
    for ch in range(chunks):
        stage1[ch, 0].wait_recv()
        total = part_ref[place(core, chip, ch), :] + core_in[local(chip, ch), :]
        for d in range(1, chips):
            stage2[ch, d].wait_recv()
            total = total + recv_buf[d - 1, ch].astype(jnp.float32)
        mine = place(core, chip, ch)
        agg_ref[mine, :] = total.astype(jnp.bfloat16)
        for d in list(range(1, chips)) + [0]:
            target = other if d == 0 else peer(d) * 2 + core
            copy = pltpu.make_async_remote_copy(
                src_ref=agg_ref.at[mine], dst_ref=agg_ref.at[mine],
                send_sem=s3.at[d, ch], recv_sem=r3.at[d, ch],
                device_id=(blk, target), device_id_type=MESH)
            copy.start()
            stage3[ch, d] = copy
    for ch in range(chunks):
        for d in range(1, chips):
            stage3[ch, d].wait_recv()
            came = place(core, lax.rem(chip + chips - d, chips), ch)
            copy = pltpu.make_async_remote_copy(
                src_ref=agg_ref.at[came], dst_ref=agg_ref.at[came],
                send_sem=s4.at[d, ch], recv_sem=r4.at[d, ch],
                device_id=(blk, other), device_id_type=MESH)
            copy.start()
            stage4[ch, d] = copy
    for ch, d in order:
        stage1[ch, d].wait_send()
        stage3[ch, d].wait_send()
        if d == 0:
            stage3[ch, d].wait_recv()
        else:
            stage2[ch, d].wait_send()
            stage4[ch, d].wait()


def replica_sum(part, replicas):
    rows, width = part.shape
    chips = replicas // 2
    chunks = largest_divisor(rows // 2 // chips // 16, CHUNKS)
    size = rows // 2 // chips // chunks
    dma = pltpu.SemaphoreType.DMA((chips, chunks))
    vmem = pl.BlockSpec(memory_space=pltpu.VMEM)
    return pl.pallas_call(
        functools.partial(reduce_kernel, chips, chunks),
        out_shape=jax.ShapeDtypeStruct((rows, width), jnp.bfloat16),
        in_specs=[vmem],
        out_specs=vmem,
        scratch_shapes=[
            pltpu.VMEM((rows // 2, width), jnp.float32),
            pltpu.VMEM((chips - 1, chunks, size, width), jnp.bfloat16),
            pltpu.VMEM((chips - 1, chunks, size, width), jnp.bfloat16),
        ] + [dma] * 8,
        compiler_params=pltpu.CompilerParams(collective_id=0, has_side_effects=True, vmem_limit_bytes=GRANT),
        name="replica_sum",
    )(part)


def activate_kernel(steps, agg_ref, weight_ref, bias_ref, out_ref, buffer, sems):
    size = agg_ref.shape[0] // steps
    copies = []
    for i in range(steps):
        span = pl.ds(i * size, size)
        output = jnp.dot(agg_ref[span, :], weight_ref[...], preferred_element_type=jnp.float32) + bias_ref[...]
        buffer[span, :] = jnp.maximum(output, 0.0).astype(buffer.dtype)
        copies.append(pltpu.make_async_copy(buffer.at[span], out_ref.at[span], sems.at[i]))
        copies[i].start()
    for copy in copies:
        copy.wait()


def activate(aggregated, weight, bias):
    rows, width = aggregated.shape
    hidden = weight.shape[1]
    steps = largest_divisor(rows // 16, OUT_STEPS)
    vmem = pl.BlockSpec(memory_space=pltpu.VMEM)
    return pl.pallas_call(
        functools.partial(activate_kernel, steps),
        out_shape=jax.ShapeDtypeStruct((rows, hidden), jnp.bfloat16),
        in_specs=[vmem, vmem, vmem],
        out_specs=pl.BlockSpec(memory_space=pltpu.HBM),
        scratch_shapes=[pltpu.VMEM((rows, hidden), jnp.bfloat16), pltpu.SemaphoreType.DMA((steps,))],
        compiler_params=pltpu.CompilerParams(vmem_limit_bytes=GRANT),
        name="activate",
    )(aggregated, weight, bias[None, :])


def shards(blocks, replicas, features, weight, bias, tile_values, tile_place, tile_count):
    sources, held = gather_sources(features, tile_values, blocks, replicas)
    part = section_sums(sources, held, tile_place, tile_count)
    aggregated = pair_sum(part) if replicas == 4 else replica_sum(part, replicas)
    return activate(aggregated, weight, bias)


def solution(mesh):
    in_specs = (
        P("blk", None),
        P(),
        P(),
        P("blk", "rep", None, None, None),
        P("blk", "rep", None),
        P("blk", "rep"),
    )
    body = functools.partial(shards, mesh.shape["blk"], mesh.shape["rep"])
    return jax.shard_map(body, mesh=mesh, in_specs=in_specs, out_specs=P("blk", None), check_vma=False)
```

```python
import functools
import heapq
import random

import jax
import jax.numpy as jnp
from jax import lax
from jax.experimental import pallas as pl
from jax.experimental.pallas import tpu as pltpu
from jax.sharding import PartitionSpec as P

MESH = pl.DeviceIdType.MESH
GROUP = 80
CHUNKS = 4
PIECES = 16
HOP = 6
WAIT = 7
ROUNDS = 40
LEAD = 0
PASSES = 768
SEED = 63485
EXPRESS = 1
URGENCY = 0.1
TOLL = 1.0
OUT_STEPS = 8
SWAPS = 8
GRANT = 16 * 1024 * 1024


def largest_divisor(number, most):
    return max(d for d in range(1, most + 1) if number % d == 0)


def chip_grid(blocks, replicas):
    columns = 2
    floors, planes = blocks // columns, replicas // 2
    chips = [(z, x, y) for z in range(floors) for x in range(columns) for y in range(planes)]
    ways = {}
    for z, x, y in chips:
        out = [(0, (z, columns - 1 - x, y), [(z, x, y, 0)])]
        out += [(3, (z, x, 1 - y), [(z, x, y, 3)])] if planes == 2 else [
            (3 + (side < 0), (z, x, y + side), [(z, x, y, 3 + (side < 0))])
            for side in (1, -1) if 0 <= y + side < planes]
        for far in range(1, EXPRESS + 1):
            for side in (1, -1):
                if 0 <= z + side * far < floors:
                    first = 1 if far == 1 else 2 * far + 1
                    crossed = [(z + side * k, x, y, 1 + (side < 0)) for k in range(far)]
                    out.append((first + (side < 0), (z + side * far, x, y), crossed))
        ways[z, x, y] = out
    return columns, planes, chips, ways


def plan_trees(blocks, replicas, sections, pieces, hop, passes):
    columns, planes, chips, ways = chip_grid(blocks, replicas)
    order = {chip: i for i, chip in enumerate(chips)}
    core_of = {}
    for b in range(blocks):
        for r in range(replicas):
            for i in range(sections):
                core_of[(b // columns, b % columns, r // 2), (b - r * sections - i) % blocks] = r % 2
    roots = {s: [(s // columns, s % columns, y) for y in range(planes)] for s in range(blocks)}
    wants = {s: [c for c in chips if (c, s) in core_of and c not in roots[s]] for s in range(blocks)}
    busy = {link: 0 for chip in chips for _, _, crossed in ways[chip] for link in crossed}
    load = dict.fromkeys(busy, 0)
    past = dict.fromkeys(busy, 0.0)
    trees, best = {}, None
    keys = [(s, p) for p in range(pieces) for s in range(blocks)]
    turn, draw = list(keys), SEED

    def grow(s, price):
        ready = dict.fromkeys(roots[s], 0)
        left, tree = set(wants[s]), []
        while left:
            cost, came, done = {}, {}, set()
            heap = [(URGENCY * t, t, order[c], c) for c, t in ready.items()]
            heapq.heapify(heap)
            while True:
                c, t, _, chip = heapq.heappop(heap)
                if chip in done:
                    continue
                done.add(chip)
                if chip in left:
                    break
                for way, other, crossed in ways[chip]:
                    if other in ready or other in done:
                        continue
                    taken, toll = 0, 0.0
                    for link in crossed:
                        taken |= busy[link]
                        toll += price[link]
                    taken >>= t
                    start = t + (~taken & (taken + 1)).bit_length() - 1
                    there = start + hop + len(crossed) - 1
                    total = c + URGENCY * (there - t) + toll
                    if other not in cost or total < cost[other]:
                        cost[other] = total
                        came[other] = (chip, way, start, crossed, there)
                        heapq.heappush(heap, (total, there, order[other], other))
            path = []
            while chip not in ready:
                path.append(came[chip] + (chip,))
                chip = came[chip][0]
            for chip, way, start, crossed, there, other in reversed(path):
                ready[other] = there
                for link in crossed:
                    busy[link] |= 1 << start
                    load[link] += 1
                tree.append((chip, way, start, other, crossed))
                left.discard(other)
        return tree

    for _ in range(passes):
        for key in turn:
            for _, _, start, _, crossed in trees.get(key, ()):
                for link in crossed:
                    busy[link] &= ~(1 << start)
                    load[link] -= 1
            top = max(max(load.values()), 1)
            trees[key] = grow(key[0], {k: TOLL * (past[k] + (load[k] / top) ** 4) for k in load})
        last = {key: max(start for _, _, start, _, _ in tree) for key, tree in trees.items()}
        span = max(last.values())
        score = (span, sum(v >= span - 1 for v in last.values()), sum(load.values()))
        if best is None or score < best[0]:
            best = (score, {key: list(tree) for key, tree in trees.items()})
        top = max(load.values())
        for k in load:
            past[k] = past[k] * 0.9 + (0.2 if load[k] >= top - pieces * 0.05 else 0.0)
        ranks = []
        for key in keys:
            draw = (draw * 1103515245 + 12345) % (1 << 31)
            ranks.append(((draw >> 8) % 1000 / 125 - last[key], key))
        turn = [key for _, key in sorted(ranks)]
    return best[1], core_of


def list_times(trees, hop, bonus):
    kids, to_go, queues, arrivals = {}, {}, {}, {}
    starts, last, number, slot = {}, dict.fromkeys(trees, 0), 0, 0
    left = sum(len(tree) for tree in trees.values())

    def enqueue(key, i):
        nonlocal number
        chip, way = trees[key][i][:2]
        heapq.heappush(queues.setdefault((chip, way), []), (-(to_go[key][i] * hop + bonus[key]), number, key, i))
        number += 1

    for key, tree in trees.items():
        kids[key], to_go[key] = {}, {}
        for i, (chip, _, _, _, _) in enumerate(tree):
            kids[key].setdefault(chip, []).append(i)
        for i in reversed(range(len(tree))):
            to_go[key][i] = 1 + max([to_go[key][j] for j in kids[key].get(tree[i][3], [])], default=0)
        reached = {other for _, _, _, other, _ in tree}
        for i, (chip, _, _, _, _) in enumerate(tree):
            if chip not in reached:
                enqueue(key, i)
    while left:
        for key, i in arrivals.pop(slot, []):
            for j in kids[key].get(trees[key][i][3], []):
                enqueue(key, j)
        for queue in queues.values():
            if queue:
                _, _, key, i = heapq.heappop(queue)
                starts[key, i] = slot
                arrivals.setdefault(slot + hop, []).append((key, i))
                last[key] = max(last[key], slot + hop)
                left -= 1
        slot += 1
    return starts, last


def retime(trees, hop, rounds):
    draw, bonus, best = random.Random(1), dict.fromkeys(trees, 0.0), None
    for _ in range(rounds):
        starts, last = list_times(trees, hop, bonus)
        span = max(last.values())
        score = (span, sum(v >= span - 1 for v in last.values()))
        if best is None or score < best[0]:
            best = (score, starts)
        for key in bonus:
            late = 1.0 if last[key] >= span - 1 else 0.3 if last[key] >= span - 3 else 0.0
            bonus[key] = bonus[key] * 0.95 + late * draw.random() * 2
    return {
        key: [(chip, way, best[1][key, i], other, crossed) for i, (chip, way, _, other, crossed) in enumerate(tree)]
        for key, tree in trees.items()}


def plan_gather(blocks, replicas, sections, pieces, hop, passes):
    trees, core_of = plan_trees(blocks, replicas, sections, pieces, hop, passes)
    trees = retime(trees, WAIT, ROUNDS)
    columns, planes, chips, _ = chip_grid(blocks, replicas)
    devices = blocks * replicas
    actions = [[] for _ in range(devices)]
    arrived = [set() for _ in range(devices)]

    def core(chip, s, p):
        return core_of.get((chip, s), p % 2) if chip[:2] != (s // columns, s % columns) else p % 2

    def device(chip, c):
        return (chip[0] * columns + chip[1]) * replicas + chip[2] * 2 + c

    for (s, p), tree in sorted(trees.items()):
        for chip, way, start, other, _ in tree:
            here, there = core(chip, s, p), core(other, s, p)
            own = chip[:2] == (s // columns, s % columns)
            actions[device(chip, here)].append((start - (LEAD if own else 0), not own, s * pieces + p, way, there))
            arrived[device(other, there)].add(s * pieces + p)
    plans = []
    for d in range(devices):
        slots, waited = [], set()
        for _, relay, piece, way, there in sorted(actions[d]):
            spot = None
            for j in range(len(slots) - 1, -1, -1):
                if slots[j][0] == piece:
                    spot = j
                    break
                if way in slots[j][2]:
                    break
            if spot is None:
                slots.append((piece, relay and piece not in waited, {}))
                spot = len(slots) - 1
                if relay:
                    waited.add(piece)
            slots[spot][2][way] = there
        leaves = arrived[d] - waited
        plans.append((slots, leaves))
    return plans


def used_ways(plans):
    used = {way for slots, _ in plans for _, _, sends in slots for way in sends}
    pairs = {1: 2, 2: 1, 3: 3, 4: 3}
    return sorted(used | {0 if w == 0 else pairs.get(w, w + 1 if w % 2 else w - 1) for w in used})


def gather_kernel(blocks, replicas, sections, pieces, plans, features_ref, tiles_ref, all_ref, held_ref,
                  table_ref, recv_sem, send_sem, own_sem, held_sem):
    blk, rep = lax.axis_index("blk"), lax.axis_index("rep")
    columns, planes, _, _ = chip_grid(blocks, replicas)
    floors = blocks // columns
    rows = features_ref.shape[0]
    size = rows // pieces
    z, x = lax.div(blk, columns), lax.rem(blk, columns)
    y, me = lax.div(rep, 2), lax.rem(rep, 2)
    is_blk = [blk == b for b in range(blocks)]
    is_rep = [rep == r for r in range(replicas)]

    def choose(options, tests):
        value = jnp.int32(options[0])
        for option, test in zip(options[1:], tests[1:]):
            value = jnp.where(test, option, value)
        return value

    def pick(values):
        if len(set(values)) == 1:
            return jnp.int32(values[0])
        picked = []
        for b in range(blocks):
            row = values[b * replicas:(b + 1) * replicas]
            picked.append(row[0] if len(set(row)) == 1 else choose(row, is_rep))
        return choose(picked, is_blk)

    def target(way, c):
        if way == 0:
            return (z * columns + (columns - 1 - x), y * 2 + c)
        if way in (3, 4):
            return (blk, (1 - y if planes == 2 else y + (1 if way == 3 else -1)) * 2 + c)
        far = 1 if way < 3 else (way - 1) // 2
        return (blk + (far if way % 2 else -far) * columns, y * 2 + c)

    exists = {}
    for way in used_ways(plans):
        if way == 0 or (way == 3 and planes == 2):
            exists[way] = None
        elif way in (3, 4):
            exists[way] = y < planes - 1 if way == 3 else y > 0
        else:
            far = 1 if way < 3 else (way - 1) // 2
            exists[way] = z < floors - far if way % 2 else z >= far

    own = pltpu.make_async_copy(features_ref, all_ref.at[blk], own_sem)
    own.start()
    steps = max(len(slots) for slots, _ in plans)
    ways = sorted(exists)
    shift = pieces.bit_length() - 1
    for j in range(steps):
        values = []
        for slots, _ in plans:
            piece, relay, sends = slots[j] if j < len(slots) else (0, False, {})
            values.append((piece * 2 + int(relay) << 2 * len(ways)) + sum(2 + sends[w] << 2 * k for k, w in enumerate(ways) if w in sends))
        table_ref[j] = pick(values)
    run = min(pieces, 16)
    words = [(i, first) for i in range(sections) for first in range(0, pieces, run)]
    for n, (i, first) in enumerate(words):
        values = []
        for d, (_, leaves) in enumerate(plans):
            s = (d // replicas - d % replicas * sections - i) % blocks
            values.append(sum(1 << p for p in range(run) if s * pieces + first + p in leaves))
        table_ref[steps + n] = pick(values)

    barrier = pltpu.get_barrier_semaphore()
    count = jnp.int32(0)
    for way, test in exists.items():
        def greet(way=way):
            for c in range(2):
                pl.semaphore_signal(barrier, inc=1, device_id=target(way, c), device_id_type=MESH)
        if test is None:
            greet()
            count = count + 2
        else:
            pl.when(test)(greet)
            count = count + jnp.where(test, 2, 0)
    pl.semaphore_wait(barrier, count)

    def block(piece):
        return all_ref.at[piece >> shift, pl.ds(pl.multiple_of((piece & (pieces - 1)) * size, size), size)]

    def copy(piece, way, c, j):
        return pltpu.make_async_remote_copy(
            src_ref=block(piece), dst_ref=block(piece), send_sem=send_sem.at[j, ways.index(way)],
            recv_sem=recv_sem.at[piece], device_id=target(way, c), device_id_type=MESH)

    def unpack(j):
        value = table_ref[j]
        return value >> (2 * len(ways) + 1), (value >> (2 * len(ways))) & 1 == 1, [
            (way, (value >> (2 * k + 1)) & 1 == 1, (value >> (2 * k)) & 1) for k, way in enumerate(ways)]

    own.wait()
    held = pltpu.make_async_copy(tiles_ref, held_ref, held_sem)
    held.start()

    def step(j, carry):
        piece, relay, sends = unpack(j)
        pl.when(relay)(lambda: copy(piece, 0, 0, j).wait_recv())
        for way, test, c in sends:
            pl.when(test)(lambda way=way, c=c: copy(piece, way, c, j).start())
        return carry

    def drain(j, carry):
        piece, _, sends = unpack(j)
        for way, test, c in sends:
            pl.when(test)(lambda way=way, c=c: copy(piece, way, c, j).wait_send())
        return carry

    lax.fori_loop(0, steps, step, 0)
    lax.fori_loop(0, steps * 3 // 4, drain, 0)
    for n, (i, first) in enumerate(words):
        source = lax.rem(blk - rep * sections - i + blocks, blocks)
        mask = table_ref[steps + n]

        def leaf(p, carry, start=source * pieces + first, mask=mask):
            pl.when((mask >> p) & 1 == 1)(lambda: copy(start + p, 0, 0, 0).wait_recv())
            return carry

        lax.fori_loop(0, run, leaf, 0)
    lax.fori_loop(steps * 3 // 4, steps, drain, 0)
    held.wait()


def gather_sources(features, tile_values, blocks, replicas):
    sections = tile_values.shape[1]
    rows, width = features.shape
    pieces = PIECES
    while rows % (16 * pieces):
        pieces //= 2
    plans = plan_gather(blocks, replicas, sections, pieces, HOP, max(2, PASSES // (blocks * replicas)))
    steps = max(len(slots) for slots, _ in plans)
    ways = len(used_ways(plans))
    vmem = pl.BlockSpec(memory_space=pltpu.VMEM)
    hbm = pl.BlockSpec(memory_space=pltpu.HBM)
    dma = pltpu.SemaphoreType.DMA
    return pl.pallas_call(
        functools.partial(gather_kernel, blocks, replicas, sections, pieces, plans),
        out_shape=(
            jax.ShapeDtypeStruct((blocks, rows, width), features.dtype),
            jax.ShapeDtypeStruct(tile_values.shape, tile_values.dtype),
        ),
        in_specs=[hbm, hbm],
        out_specs=(vmem, vmem),
        scratch_shapes=[
            pltpu.SMEM((steps + sections * pl.cdiv(pieces, 16),), jnp.int32), dma((blocks * pieces,)), dma((steps, ways)), dma(()), dma(())
        ],
        compiler_params=pltpu.CompilerParams(collective_id=1, has_side_effects=True, vmem_limit_bytes=2 * GRANT),
        cost_estimate=pl.CostEstimate(
            flops=0, bytes_accessed=96 * rows * width * features.dtype.itemsize, transcendentals=0
        ),
        name="gather_sources",
    )(pltpu.with_memory_space_constraint(features, pltpu.HBM), tile_values)


def sections_kernel(group, place_ref, count_ref, source_ref, tiles_ref, acc_ref):
    sections, slots, tile = tiles_ref.shape[1:4]
    blocks, row_tiles = source_ref.shape[0], source_ref.shape[1] // tile
    blk, rep = lax.axis_index("blk"), lax.axis_index("rep")
    acc_ref[...] = jnp.zeros_like(acc_ref)
    for section in range(sections):
        source = lax.rem(blk - rep * sections - section + blocks, blocks)
        count = count_ref[0, section]

        def body(g, carry, section=section, source=source, count=count):
            for u in range(group):
                k = g * group + u
                place = place_ref[0, section, k]
                column, target = lax.rem(place, row_tiles), lax.div(place, row_tiles)
                piece = source_ref[source, pl.ds(pl.multiple_of(column * tile, tile), tile), :]
                product = jnp.dot(tiles_ref[0, section, k], piece, preferred_element_type=jnp.float32)
                rows = pl.ds(pl.multiple_of(target * tile, tile), tile)
                acc_ref[rows, :] += jnp.where(k < count, product, 0.0)
            return carry

        lax.fori_loop(0, lax.div(count + group - 1, group), body, 0)


def section_sums(sources, tile_values, tile_place, tile_count):
    slots = tile_values.shape[2]
    rows, width = sources.shape[1:]
    vmem = pl.BlockSpec(memory_space=pltpu.VMEM)
    smem = pl.BlockSpec(memory_space=pltpu.SMEM)
    return pl.pallas_call(
        functools.partial(sections_kernel, largest_divisor(slots, GROUP)),
        out_shape=jax.ShapeDtypeStruct((rows, width), jnp.float32),
        in_specs=[smem, smem, vmem, vmem],
        out_specs=vmem,
        compiler_params=pltpu.CompilerParams(vmem_limit_bytes=2 * GRANT),
        name="section_sums",
    )(tile_place, tile_count, sources, tile_values)


def swap_kernel(chunks, part_ref, agg_ref, core_in, send_buf, recv_buf, s1, r1, s2, r2, s3, r3):
    blk, rep = lax.axis_index("blk"), lax.axis_index("rep")
    core, chip = lax.rem(rep, 2), lax.div(rep, 2)
    half = part_ref.shape[0] // 2
    size = half // chunks
    other, across = chip * 2 + (1 - core), (1 - chip) * 2 + core

    def place(which, ch):
        return pl.ds(pl.multiple_of(which * half + ch * size, size), size)

    barrier = pltpu.get_barrier_semaphore()
    for target in (other, across):
        pl.semaphore_signal(barrier, inc=1, device_id=(blk, target), device_id_type=MESH)
    pl.semaphore_wait(barrier, 2)

    stage1, stage2, stage3 = [], [], []
    for ch in range(chunks):
        stage1.append(pltpu.make_async_remote_copy(
            src_ref=part_ref.at[place(1 - core, ch)], dst_ref=core_in.at[ch],
            send_sem=s1.at[ch], recv_sem=r1.at[ch], device_id=(blk, other), device_id_type=MESH))
        stage1[ch].start()
    for ch in range(chunks):
        stage1[ch].wait_recv()
        send_buf[ch] = (part_ref[place(core, ch), :] + core_in[ch]).astype(send_buf.dtype)
        stage2.append(pltpu.make_async_remote_copy(
            src_ref=send_buf.at[ch], dst_ref=recv_buf.at[ch],
            send_sem=s2.at[ch], recv_sem=r2.at[ch], device_id=(blk, across), device_id_type=MESH))
        stage2[ch].start()
    for ch in range(chunks):
        stage2[ch].wait_recv()
        mine = place(core, ch)
        total = send_buf[ch].astype(jnp.float32) + recv_buf[ch].astype(jnp.float32)
        agg_ref[mine, :] = total.astype(agg_ref.dtype)
        stage3.append(pltpu.make_async_remote_copy(
            src_ref=agg_ref.at[mine], dst_ref=agg_ref.at[mine],
            send_sem=s3.at[ch], recv_sem=r3.at[ch], device_id=(blk, other), device_id_type=MESH))
        stage3[ch].start()
    for ch in range(chunks):
        stage1[ch].wait_send()
        stage2[ch].wait_send()
        stage3[ch].wait()


def pair_sum(part):
    rows, width = part.shape
    chunks = largest_divisor(rows // 2 // 16, SWAPS)
    size = rows // 2 // chunks
    dma = pltpu.SemaphoreType.DMA((chunks,))
    vmem = pl.BlockSpec(memory_space=pltpu.VMEM)
    return pl.pallas_call(
        functools.partial(swap_kernel, chunks),
        out_shape=jax.ShapeDtypeStruct((rows, width), jnp.bfloat16),
        in_specs=[vmem],
        out_specs=vmem,
        scratch_shapes=[
            pltpu.VMEM((chunks, size, width), jnp.float32),
            pltpu.VMEM((chunks, size, width), jnp.bfloat16),
            pltpu.VMEM((chunks, size, width), jnp.bfloat16),
        ] + [dma] * 6,
        compiler_params=pltpu.CompilerParams(collective_id=0, has_side_effects=True, vmem_limit_bytes=GRANT),
        name="replica_sum",
    )(part)


def reduce_kernel(chips, chunks, part_ref, agg_ref, core_in, send_buf, recv_buf,
                  s1, r1, s2, r2, s3, r3, s4, r4):
    blk, rep = lax.axis_index("blk"), lax.axis_index("rep")
    core, chip = lax.rem(rep, 2), lax.div(rep, 2)
    rows = part_ref.shape[0]
    half = rows // 2
    size = half // chips // chunks
    other = chip * 2 + (1 - core)

    def peer(d):
        return lax.rem(chip + d, chips)

    def local(piece, ch):
        return pl.ds(pl.multiple_of((piece * chunks + ch) * size, size), size)

    def place(which, piece, ch):
        return pl.ds(pl.multiple_of(which * half + (piece * chunks + ch) * size, size), size)

    barrier = pltpu.get_barrier_semaphore()
    pl.semaphore_signal(barrier, inc=1, device_id=(blk, other), device_id_type=MESH)
    for d in range(1, chips):
        pl.semaphore_signal(barrier, inc=1, device_id=(blk, peer(d) * 2 + core), device_id_type=MESH)
    pl.semaphore_wait(barrier, chips)

    order = [(ch, d) for ch in range(chunks) for d in list(range(1, chips)) + [0]]
    stage1, stage2, stage3, stage4 = {}, {}, {}, {}
    for ch, d in order:
        copy = pltpu.make_async_remote_copy(
            src_ref=part_ref.at[place(1 - core, peer(d), ch)], dst_ref=core_in.at[local(peer(d), ch)],
            send_sem=s1.at[d, ch], recv_sem=r1.at[d, ch], device_id=(blk, other), device_id_type=MESH)
        copy.start()
        stage1[ch, d] = copy
    for ch, d in order:
        if d == 0:
            continue
        stage1[ch, d].wait_recv()
        total = part_ref[place(core, peer(d), ch), :] + core_in[local(peer(d), ch), :]
        send_buf[d - 1, ch] = total.astype(jnp.bfloat16)
        copy = pltpu.make_async_remote_copy(
            src_ref=send_buf.at[d - 1, ch], dst_ref=recv_buf.at[d - 1, ch],
            send_sem=s2.at[d, ch], recv_sem=r2.at[d, ch],
            device_id=(blk, peer(d) * 2 + core), device_id_type=MESH)
        copy.start()
        stage2[ch, d] = copy
    for ch in range(chunks):
        stage1[ch, 0].wait_recv()
        total = part_ref[place(core, chip, ch), :] + core_in[local(chip, ch), :]
        for d in range(1, chips):
            stage2[ch, d].wait_recv()
            total = total + recv_buf[d - 1, ch].astype(jnp.float32)
        mine = place(core, chip, ch)
        agg_ref[mine, :] = total.astype(jnp.bfloat16)
        for d in list(range(1, chips)) + [0]:
            target = other if d == 0 else peer(d) * 2 + core
            copy = pltpu.make_async_remote_copy(
                src_ref=agg_ref.at[mine], dst_ref=agg_ref.at[mine],
                send_sem=s3.at[d, ch], recv_sem=r3.at[d, ch],
                device_id=(blk, target), device_id_type=MESH)
            copy.start()
            stage3[ch, d] = copy
    for ch in range(chunks):
        for d in range(1, chips):
            stage3[ch, d].wait_recv()
            came = place(core, lax.rem(chip + chips - d, chips), ch)
            copy = pltpu.make_async_remote_copy(
                src_ref=agg_ref.at[came], dst_ref=agg_ref.at[came],
                send_sem=s4.at[d, ch], recv_sem=r4.at[d, ch],
                device_id=(blk, other), device_id_type=MESH)
            copy.start()
            stage4[ch, d] = copy
    for ch, d in order:
        stage1[ch, d].wait_send()
        stage3[ch, d].wait_send()
        if d == 0:
            stage3[ch, d].wait_recv()
        else:
            stage2[ch, d].wait_send()
            stage4[ch, d].wait()


def replica_sum(part, replicas):
    rows, width = part.shape
    chips = replicas // 2
    chunks = largest_divisor(rows // 2 // chips // 16, CHUNKS)
    size = rows // 2 // chips // chunks
    dma = pltpu.SemaphoreType.DMA((chips, chunks))
    vmem = pl.BlockSpec(memory_space=pltpu.VMEM)
    return pl.pallas_call(
        functools.partial(reduce_kernel, chips, chunks),
        out_shape=jax.ShapeDtypeStruct((rows, width), jnp.bfloat16),
        in_specs=[vmem],
        out_specs=vmem,
        scratch_shapes=[
            pltpu.VMEM((rows // 2, width), jnp.float32),
            pltpu.VMEM((chips - 1, chunks, size, width), jnp.bfloat16),
            pltpu.VMEM((chips - 1, chunks, size, width), jnp.bfloat16),
        ] + [dma] * 8,
        compiler_params=pltpu.CompilerParams(collective_id=0, has_side_effects=True, vmem_limit_bytes=GRANT),
        name="replica_sum",
    )(part)


def activate_kernel(steps, agg_ref, weight_ref, bias_ref, out_ref, buffer, sems):
    size = agg_ref.shape[0] // steps
    copies = []
    for i in range(steps):
        span = pl.ds(i * size, size)
        output = jnp.dot(agg_ref[span, :], weight_ref[...], preferred_element_type=jnp.float32) + bias_ref[...]
        buffer[span, :] = jnp.maximum(output, 0.0).astype(buffer.dtype)
        copies.append(pltpu.make_async_copy(buffer.at[span], out_ref.at[span], sems.at[i]))
        copies[i].start()
    for copy in copies:
        copy.wait()


def activate(aggregated, weight, bias):
    rows, width = aggregated.shape
    hidden = weight.shape[1]
    steps = largest_divisor(rows // 16, OUT_STEPS)
    vmem = pl.BlockSpec(memory_space=pltpu.VMEM)
    return pl.pallas_call(
        functools.partial(activate_kernel, steps),
        out_shape=jax.ShapeDtypeStruct((rows, hidden), jnp.bfloat16),
        in_specs=[vmem, vmem, vmem],
        out_specs=pl.BlockSpec(memory_space=pltpu.HBM),
        scratch_shapes=[pltpu.VMEM((rows, hidden), jnp.bfloat16), pltpu.SemaphoreType.DMA((steps,))],
        compiler_params=pltpu.CompilerParams(vmem_limit_bytes=GRANT),
        name="activate",
    )(aggregated, weight, bias[None, :])


def shards(blocks, replicas, features, weight, bias, tile_values, tile_place, tile_count):
    sources, held = gather_sources(features, tile_values, blocks, replicas)
    part = section_sums(sources, held, tile_place, tile_count)
    aggregated = pair_sum(part) if replicas == 4 else replica_sum(part, replicas)
    return activate(aggregated, weight, bias)


def solution(mesh):
    in_specs = (
        P("blk", None),
        P(),
        P(),
        P("blk", "rep", None, None, None),
        P("blk", "rep", None),
        P("blk", "rep"),
    )
    body = functools.partial(shards, mesh.shape["blk"], mesh.shape["rep"])
    return jax.shard_map(body, mesh=mesh, in_specs=in_specs, out_specs=P("blk", None), check_vma=False)
```

```python
import functools
import heapq
import random

import jax
import jax.numpy as jnp
from jax import lax
from jax.experimental import pallas as pl
from jax.experimental.pallas import tpu as pltpu
from jax.sharding import PartitionSpec as P

MESH = pl.DeviceIdType.MESH
GROUP = 80
CHUNKS = 4
PIECES = 16
HOP = 6
WAIT = 7
ROUNDS = 40
LEAD = 0
PASSES = 768
SEED = 63485
EXPRESS = 1
URGENCY = 0.1
TOLL = 1.0
OUT_STEPS = 8
SWAPS = (1,) * 8
GRANT = 16 * 1024 * 1024


def largest_divisor(number, most):
    return max(d for d in range(1, most + 1) if number % d == 0)


def chip_grid(blocks, replicas):
    columns = 2
    floors, planes = blocks // columns, replicas // 2
    chips = [(z, x, y) for z in range(floors) for x in range(columns) for y in range(planes)]
    ways = {}
    for z, x, y in chips:
        out = [(0, (z, columns - 1 - x, y), [(z, x, y, 0)])]
        out += [(3, (z, x, 1 - y), [(z, x, y, 3)])] if planes == 2 else [
            (3 + (side < 0), (z, x, y + side), [(z, x, y, 3 + (side < 0))])
            for side in (1, -1) if 0 <= y + side < planes]
        for far in range(1, EXPRESS + 1):
            for side in (1, -1):
                if 0 <= z + side * far < floors:
                    first = 1 if far == 1 else 2 * far + 1
                    crossed = [(z + side * k, x, y, 1 + (side < 0)) for k in range(far)]
                    out.append((first + (side < 0), (z + side * far, x, y), crossed))
        ways[z, x, y] = out
    return columns, planes, chips, ways


def plan_trees(blocks, replicas, sections, pieces, hop, passes):
    columns, planes, chips, ways = chip_grid(blocks, replicas)
    order = {chip: i for i, chip in enumerate(chips)}
    core_of = {}
    for b in range(blocks):
        for r in range(replicas):
            for i in range(sections):
                core_of[(b // columns, b % columns, r // 2), (b - r * sections - i) % blocks] = r % 2
    roots = {s: [(s // columns, s % columns, y) for y in range(planes)] for s in range(blocks)}
    wants = {s: [c for c in chips if (c, s) in core_of and c not in roots[s]] for s in range(blocks)}
    busy = {link: 0 for chip in chips for _, _, crossed in ways[chip] for link in crossed}
    load = dict.fromkeys(busy, 0)
    past = dict.fromkeys(busy, 0.0)
    trees, best = {}, None
    keys = [(s, p) for p in range(pieces) for s in range(blocks)]
    turn, draw = list(keys), SEED

    def grow(s, price):
        ready = dict.fromkeys(roots[s], 0)
        left, tree = set(wants[s]), []
        while left:
            cost, came, done = {}, {}, set()
            heap = [(URGENCY * t, t, order[c], c) for c, t in ready.items()]
            heapq.heapify(heap)
            while True:
                c, t, _, chip = heapq.heappop(heap)
                if chip in done:
                    continue
                done.add(chip)
                if chip in left:
                    break
                for way, other, crossed in ways[chip]:
                    if other in ready or other in done:
                        continue
                    taken, toll = 0, 0.0
                    for link in crossed:
                        taken |= busy[link]
                        toll += price[link]
                    taken >>= t
                    start = t + (~taken & (taken + 1)).bit_length() - 1
                    there = start + hop + len(crossed) - 1
                    total = c + URGENCY * (there - t) + toll
                    if other not in cost or total < cost[other]:
                        cost[other] = total
                        came[other] = (chip, way, start, crossed, there)
                        heapq.heappush(heap, (total, there, order[other], other))
            path = []
            while chip not in ready:
                path.append(came[chip] + (chip,))
                chip = came[chip][0]
            for chip, way, start, crossed, there, other in reversed(path):
                ready[other] = there
                for link in crossed:
                    busy[link] |= 1 << start
                    load[link] += 1
                tree.append((chip, way, start, other, crossed))
                left.discard(other)
        return tree

    for _ in range(passes):
        for key in turn:
            for _, _, start, _, crossed in trees.get(key, ()):
                for link in crossed:
                    busy[link] &= ~(1 << start)
                    load[link] -= 1
            top = max(max(load.values()), 1)
            trees[key] = grow(key[0], {k: TOLL * (past[k] + (load[k] / top) ** 4) for k in load})
        last = {key: max(start for _, _, start, _, _ in tree) for key, tree in trees.items()}
        span = max(last.values())
        score = (span, sum(v >= span - 1 for v in last.values()), sum(load.values()))
        if best is None or score < best[0]:
            best = (score, {key: list(tree) for key, tree in trees.items()})
        top = max(load.values())
        for k in load:
            past[k] = past[k] * 0.9 + (0.2 if load[k] >= top - pieces * 0.05 else 0.0)
        ranks = []
        for key in keys:
            draw = (draw * 1103515245 + 12345) % (1 << 31)
            ranks.append(((draw >> 8) % 1000 / 125 - last[key], key))
        turn = [key for _, key in sorted(ranks)]
    return best[1], core_of


def list_times(trees, hop, bonus):
    kids, to_go, queues, arrivals = {}, {}, {}, {}
    starts, last, number, slot = {}, dict.fromkeys(trees, 0), 0, 0
    left = sum(len(tree) for tree in trees.values())

    def enqueue(key, i):
        nonlocal number
        chip, way = trees[key][i][:2]
        heapq.heappush(queues.setdefault((chip, way), []), (-(to_go[key][i] * hop + bonus[key]), number, key, i))
        number += 1

    for key, tree in trees.items():
        kids[key], to_go[key] = {}, {}
        for i, (chip, _, _, _, _) in enumerate(tree):
            kids[key].setdefault(chip, []).append(i)
        for i in reversed(range(len(tree))):
            to_go[key][i] = 1 + max([to_go[key][j] for j in kids[key].get(tree[i][3], [])], default=0)
        reached = {other for _, _, _, other, _ in tree}
        for i, (chip, _, _, _, _) in enumerate(tree):
            if chip not in reached:
                enqueue(key, i)
    while left:
        for key, i in arrivals.pop(slot, []):
            for j in kids[key].get(trees[key][i][3], []):
                enqueue(key, j)
        for queue in queues.values():
            if queue:
                _, _, key, i = heapq.heappop(queue)
                starts[key, i] = slot
                arrivals.setdefault(slot + hop, []).append((key, i))
                last[key] = max(last[key], slot + hop)
                left -= 1
        slot += 1
    return starts, last


def retime(trees, hop, rounds):
    draw, bonus, best = random.Random(1), dict.fromkeys(trees, 0.0), None
    for _ in range(rounds):
        starts, last = list_times(trees, hop, bonus)
        span = max(last.values())
        score = (span, sum(v >= span - 1 for v in last.values()))
        if best is None or score < best[0]:
            best = (score, starts)
        for key in bonus:
            late = 1.0 if last[key] >= span - 1 else 0.3 if last[key] >= span - 3 else 0.0
            bonus[key] = bonus[key] * 0.95 + late * draw.random() * 2
    return {
        key: [(chip, way, best[1][key, i], other, crossed) for i, (chip, way, _, other, crossed) in enumerate(tree)]
        for key, tree in trees.items()}


def plan_gather(blocks, replicas, sections, pieces, hop, passes):
    trees, core_of = plan_trees(blocks, replicas, sections, pieces, hop, passes)
    trees = retime(trees, WAIT, ROUNDS)
    columns, planes, chips, _ = chip_grid(blocks, replicas)
    devices = blocks * replicas
    actions = [[] for _ in range(devices)]
    arrived = [set() for _ in range(devices)]

    def core(chip, s, p):
        return core_of.get((chip, s), p % 2) if chip[:2] != (s // columns, s % columns) else p % 2

    def device(chip, c):
        return (chip[0] * columns + chip[1]) * replicas + chip[2] * 2 + c

    for (s, p), tree in sorted(trees.items()):
        for chip, way, start, other, _ in tree:
            here, there = core(chip, s, p), core(other, s, p)
            own = chip[:2] == (s // columns, s % columns)
            actions[device(chip, here)].append((start - (LEAD if own else 0), not own, s * pieces + p, way, there))
            arrived[device(other, there)].add(s * pieces + p)
    plans = []
    for d in range(devices):
        slots, waited = [], set()
        for _, relay, piece, way, there in sorted(actions[d]):
            spot = None
            for j in range(len(slots) - 1, -1, -1):
                if slots[j][0] == piece:
                    spot = j
                    break
                if way in slots[j][2]:
                    break
            if spot is None:
                slots.append((piece, relay and piece not in waited, {}))
                spot = len(slots) - 1
                if relay:
                    waited.add(piece)
            slots[spot][2][way] = there
        leaves = arrived[d] - waited
        plans.append((slots, leaves))
    return plans


def used_ways(plans):
    used = {way for slots, _ in plans for _, _, sends in slots for way in sends}
    pairs = {1: 2, 2: 1, 3: 3, 4: 3}
    return sorted(used | {0 if w == 0 else pairs.get(w, w + 1 if w % 2 else w - 1) for w in used})


def gather_kernel(blocks, replicas, sections, pieces, plans, features_ref, tiles_ref, all_ref, held_ref,
                  table_ref, recv_sem, send_sem, own_sem, held_sem):
    blk, rep = lax.axis_index("blk"), lax.axis_index("rep")
    columns, planes, _, _ = chip_grid(blocks, replicas)
    floors = blocks // columns
    rows = features_ref.shape[0]
    size = rows // pieces
    z, x = lax.div(blk, columns), lax.rem(blk, columns)
    y, me = lax.div(rep, 2), lax.rem(rep, 2)
    is_blk = [blk == b for b in range(blocks)]
    is_rep = [rep == r for r in range(replicas)]

    def choose(options, tests):
        value = jnp.int32(options[0])
        for option, test in zip(options[1:], tests[1:]):
            value = jnp.where(test, option, value)
        return value

    def pick(values):
        if len(set(values)) == 1:
            return jnp.int32(values[0])
        picked = []
        for b in range(blocks):
            row = values[b * replicas:(b + 1) * replicas]
            picked.append(row[0] if len(set(row)) == 1 else choose(row, is_rep))
        return choose(picked, is_blk)

    def target(way, c):
        if way == 0:
            return (z * columns + (columns - 1 - x), y * 2 + c)
        if way in (3, 4):
            return (blk, (1 - y if planes == 2 else y + (1 if way == 3 else -1)) * 2 + c)
        far = 1 if way < 3 else (way - 1) // 2
        return (blk + (far if way % 2 else -far) * columns, y * 2 + c)

    exists = {}
    for way in used_ways(plans):
        if way == 0 or (way == 3 and planes == 2):
            exists[way] = None
        elif way in (3, 4):
            exists[way] = y < planes - 1 if way == 3 else y > 0
        else:
            far = 1 if way < 3 else (way - 1) // 2
            exists[way] = z < floors - far if way % 2 else z >= far

    own = pltpu.make_async_copy(features_ref, all_ref.at[blk], own_sem)
    own.start()
    barrier = pltpu.get_barrier_semaphore()
    count = jnp.int32(0)
    for way, test in exists.items():
        def greet(way=way):
            for c in range(2):
                pl.semaphore_signal(barrier, inc=1, device_id=target(way, c), device_id_type=MESH)
        if test is None:
            greet()
            count = count + 2
        else:
            pl.when(test)(greet)
            count = count + jnp.where(test, 2, 0)
    steps = max(len(slots) for slots, _ in plans)
    ways = sorted(exists)
    shift = pieces.bit_length() - 1
    for j in range(steps):
        values = []
        for slots, _ in plans:
            piece, relay, sends = slots[j] if j < len(slots) else (0, False, {})
            values.append((piece * 2 + int(relay) << 2 * len(ways)) + sum(2 + sends[w] << 2 * k for k, w in enumerate(ways) if w in sends))
        table_ref[j] = pick(values)
    run = min(pieces, 16)
    words = [(i, first) for i in range(sections) for first in range(0, pieces, run)]
    for n, (i, first) in enumerate(words):
        values = []
        for d, (_, leaves) in enumerate(plans):
            s = (d // replicas - d % replicas * sections - i) % blocks
            values.append(sum(1 << p for p in range(run) if s * pieces + first + p in leaves))
        table_ref[steps + n] = pick(values)
    pl.semaphore_wait(barrier, count)

    def block(piece):
        return all_ref.at[piece >> shift, pl.ds(pl.multiple_of((piece & (pieces - 1)) * size, size), size)]

    def copy(piece, way, c, j):
        return pltpu.make_async_remote_copy(
            src_ref=block(piece), dst_ref=block(piece), send_sem=send_sem.at[j, ways.index(way)],
            recv_sem=recv_sem.at[piece], device_id=target(way, c), device_id_type=MESH)

    def unpack(j):
        value = table_ref[j]
        return value >> (2 * len(ways) + 1), (value >> (2 * len(ways))) & 1 == 1, [
            (way, (value >> (2 * k + 1)) & 1 == 1, (value >> (2 * k)) & 1) for k, way in enumerate(ways)]

    own.wait()
    held = pltpu.make_async_copy(tiles_ref, held_ref, held_sem)
    held.start()

    def step(j, carry):
        piece, relay, sends = unpack(j)
        pl.when(relay)(lambda: copy(piece, 0, 0, j).wait_recv())
        for way, test, c in sends:
            pl.when(test)(lambda way=way, c=c: copy(piece, way, c, j).start())
        return carry

    def drain(j, carry):
        piece, _, sends = unpack(j)
        for way, test, c in sends:
            pl.when(test)(lambda way=way, c=c: copy(piece, way, c, j).wait_send())
        return carry

    lax.fori_loop(0, steps, step, 0)
    lax.fori_loop(0, steps * 3 // 4, drain, 0)
    for n, (i, first) in enumerate(words):
        source = lax.rem(blk - rep * sections - i + blocks, blocks)
        mask = table_ref[steps + n]

        def leaf(p, carry, start=source * pieces + first, mask=mask):
            pl.when((mask >> p) & 1 == 1)(lambda: copy(start + p, 0, 0, 0).wait_recv())
            return carry

        lax.fori_loop(0, run, leaf, 0)
    lax.fori_loop(steps * 3 // 4, steps, drain, 0)
    held.wait()


def gather_sources(features, tile_values, blocks, replicas):
    sections = tile_values.shape[1]
    rows, width = features.shape
    pieces = PIECES
    while rows % (16 * pieces):
        pieces //= 2
    plans = plan_gather(blocks, replicas, sections, pieces, HOP, max(2, PASSES // (blocks * replicas)))
    steps = max(len(slots) for slots, _ in plans)
    ways = len(used_ways(plans))
    vmem = pl.BlockSpec(memory_space=pltpu.VMEM)
    hbm = pl.BlockSpec(memory_space=pltpu.HBM)
    dma = pltpu.SemaphoreType.DMA
    return pl.pallas_call(
        functools.partial(gather_kernel, blocks, replicas, sections, pieces, plans),
        out_shape=(
            jax.ShapeDtypeStruct((blocks, rows, width), features.dtype),
            jax.ShapeDtypeStruct(tile_values.shape, tile_values.dtype),
        ),
        in_specs=[hbm, hbm],
        out_specs=(vmem, vmem),
        scratch_shapes=[
            pltpu.SMEM((steps + sections * pl.cdiv(pieces, 16),), jnp.int32), dma((blocks * pieces,)), dma((steps, ways)), dma(()), dma(())
        ],
        compiler_params=pltpu.CompilerParams(collective_id=1, has_side_effects=True, vmem_limit_bytes=2 * GRANT),
        cost_estimate=pl.CostEstimate(
            flops=0, bytes_accessed=96 * rows * width * features.dtype.itemsize, transcendentals=0
        ),
        name="gather_sources",
    )(pltpu.with_memory_space_constraint(features, pltpu.HBM), tile_values)


def sections_kernel(group, place_ref, count_ref, source_ref, tiles_ref, acc_ref):
    sections, slots, tile = tiles_ref.shape[1:4]
    blocks, row_tiles = source_ref.shape[0], source_ref.shape[1] // tile
    blk, rep = lax.axis_index("blk"), lax.axis_index("rep")
    acc_ref[...] = jnp.zeros_like(acc_ref)
    for section in range(sections):
        source = lax.rem(blk - rep * sections - section + blocks, blocks)
        count = count_ref[0, section]

        def body(g, carry, size=group, first=0, section=section, source=source, count=count):
            for u in range(size):
                k = first + g * size + u
                place = place_ref[0, section, k]
                column, target = lax.rem(place, row_tiles), lax.div(place, row_tiles)
                piece = source_ref[source, pl.ds(pl.multiple_of(column * tile, tile), tile), :]
                product = jnp.dot(tiles_ref[0, section, k], piece, preferred_element_type=jnp.float32)
                rows = pl.ds(pl.multiple_of(target * tile, tile), tile)
                acc_ref[rows, :] += jnp.where(k < count, product, 0.0)
            return carry

        half = group // 2 if group % 2 == 0 else group
        full = lax.div(count + group - half - 1, group)
        lax.fori_loop(0, full, body, 0)
        if half < group:
            left = count - full * group
            lax.fori_loop(0, jnp.where(left > 0, 1, 0), functools.partial(body, size=half, first=full * group), 0)


def section_sums(sources, tile_values, tile_place, tile_count):
    slots = tile_values.shape[2]
    rows, width = sources.shape[1:]
    vmem = pl.BlockSpec(memory_space=pltpu.VMEM)
    smem = pl.BlockSpec(memory_space=pltpu.SMEM)
    return pl.pallas_call(
        functools.partial(sections_kernel, largest_divisor(slots, GROUP)),
        out_shape=jax.ShapeDtypeStruct((rows, width), jnp.float32),
        in_specs=[smem, smem, vmem, vmem],
        out_specs=vmem,
        compiler_params=pltpu.CompilerParams(vmem_limit_bytes=2 * GRANT),
        name="section_sums",
    )(tile_place, tile_count, sources, tile_values)


def swap_kernel(sizes, part_ref, weight_ref, bias_ref, act_ref, agg_ref, core_in, send_buf, recv_buf,
                s1, r1, s2, r2, s3, r3):
    blk, rep = lax.axis_index("blk"), lax.axis_index("rep")
    core, chip = lax.rem(rep, 2), lax.div(rep, 2)
    half = part_ref.shape[0] // 2
    other, across = chip * 2 + (1 - core), (1 - chip) * 2 + core
    chunks = len(sizes)
    spans = [pl.ds(sum(sizes[:ch]), sizes[ch]) for ch in range(chunks)]

    def place(which, ch):
        return pl.ds(pl.multiple_of(which * half + sum(sizes[:ch]), min(sizes)), sizes[ch])

    def finish(which, ch):
        span = place(which, ch)
        output = jnp.dot(agg_ref[span, :], weight_ref[...], preferred_element_type=jnp.float32) + bias_ref[...]
        act_ref[span, :] = jnp.maximum(output, 0.0).astype(act_ref.dtype)

    barrier = pltpu.get_barrier_semaphore()
    for target in (other, across):
        pl.semaphore_signal(barrier, inc=1, device_id=(blk, target), device_id_type=MESH)
    pl.semaphore_wait(barrier, 2)

    stage1, stage2, stage3 = [], [], []
    for ch, span in enumerate(spans):
        stage1.append(pltpu.make_async_remote_copy(
            src_ref=part_ref.at[place(1 - core, ch)], dst_ref=core_in.at[span],
            send_sem=s1.at[ch], recv_sem=r1.at[ch], device_id=(blk, other), device_id_type=MESH))
        stage1[ch].start()
    for ch, span in enumerate(spans):
        stage1[ch].wait_recv()
        send_buf[span, :] = (part_ref[place(core, ch), :] + core_in[span, :]).astype(send_buf.dtype)
        stage2.append(pltpu.make_async_remote_copy(
            src_ref=send_buf.at[span], dst_ref=recv_buf.at[span],
            send_sem=s2.at[ch], recv_sem=r2.at[ch], device_id=(blk, across), device_id_type=MESH))
        stage2[ch].start()
    for ch, span in enumerate(spans):
        stage2[ch].wait_recv()
        mine = place(core, ch)
        total = send_buf[span, :].astype(jnp.float32) + recv_buf[span, :].astype(jnp.float32)
        agg_ref[mine, :] = total.astype(agg_ref.dtype)
        stage3.append(pltpu.make_async_remote_copy(
            src_ref=agg_ref.at[mine], dst_ref=agg_ref.at[mine],
            send_sem=s3.at[ch], recv_sem=r3.at[ch], device_id=(blk, other), device_id_type=MESH))
        stage3[ch].start()
        finish(core, ch)
        if ch:
            stage3[ch - 1].wait_recv()
            finish(1 - core, ch - 1)
    for ch in range(chunks):
        stage1[ch].wait_send()
        stage2[ch].wait_send()
    stage3[chunks - 1].wait_recv()
    finish(1 - core, chunks - 1)
    for ch in range(chunks):
        stage3[ch].wait_send()


def swap_and_activate(part, weight, bias):
    rows, width = part.shape
    hidden = weight.shape[1]
    half = rows // 2
    unit = half // sum(SWAPS)
    sizes = [unit * share for share in SWAPS] if unit * sum(SWAPS) == half and unit % 16 == 0 else [half]
    dma = pltpu.SemaphoreType.DMA((len(sizes),))
    vmem = pl.BlockSpec(memory_space=pltpu.VMEM)
    return pl.pallas_call(
        functools.partial(swap_kernel, sizes),
        out_shape=jax.ShapeDtypeStruct((rows, hidden), jnp.bfloat16),
        in_specs=[vmem, vmem, vmem],
        out_specs=vmem,
        scratch_shapes=[
            pltpu.VMEM((rows, width), jnp.bfloat16),
            pltpu.VMEM((half, width), jnp.float32),
            pltpu.VMEM((half, width), jnp.bfloat16),
            pltpu.VMEM((half, width), jnp.bfloat16),
        ] + [dma] * 6,
        compiler_params=pltpu.CompilerParams(collective_id=0, has_side_effects=True, vmem_limit_bytes=GRANT),
        name="swap_and_activate",
    )(part, weight, bias[None, :])


def flush_kernel(steps, act_ref, out_ref, sems):
    size = act_ref.shape[0] // steps
    spans = [pl.ds(i * size, size) for i in range(steps)]
    copies = [pltpu.make_async_copy(act_ref.at[span], out_ref.at[span], sems.at[i]) for i, span in enumerate(spans)]
    for copy in copies:
        copy.start()
    for copy in copies:
        copy.wait()


def flush(activations):
    steps = largest_divisor(activations.shape[0] // 16, OUT_STEPS)
    return pl.pallas_call(
        functools.partial(flush_kernel, steps),
        out_shape=jax.ShapeDtypeStruct(activations.shape, activations.dtype),
        in_specs=[pl.BlockSpec(memory_space=pltpu.VMEM)],
        out_specs=pl.BlockSpec(memory_space=pltpu.HBM),
        scratch_shapes=[pltpu.SemaphoreType.DMA((steps,))],
        compiler_params=pltpu.CompilerParams(vmem_limit_bytes=GRANT),
        name="flush",
    )(activations)


def reduce_kernel(chips, chunks, part_ref, agg_ref, core_in, send_buf, recv_buf,
                  s1, r1, s2, r2, s3, r3, s4, r4):
    blk, rep = lax.axis_index("blk"), lax.axis_index("rep")
    core, chip = lax.rem(rep, 2), lax.div(rep, 2)
    rows = part_ref.shape[0]
    half = rows // 2
    size = half // chips // chunks
    other = chip * 2 + (1 - core)

    def peer(d):
        return lax.rem(chip + d, chips)

    def local(piece, ch):
        return pl.ds(pl.multiple_of((piece * chunks + ch) * size, size), size)

    def place(which, piece, ch):
        return pl.ds(pl.multiple_of(which * half + (piece * chunks + ch) * size, size), size)

    barrier = pltpu.get_barrier_semaphore()
    pl.semaphore_signal(barrier, inc=1, device_id=(blk, other), device_id_type=MESH)
    for d in range(1, chips):
        pl.semaphore_signal(barrier, inc=1, device_id=(blk, peer(d) * 2 + core), device_id_type=MESH)
    pl.semaphore_wait(barrier, chips)

    order = [(ch, d) for ch in range(chunks) for d in list(range(1, chips)) + [0]]
    stage1, stage2, stage3, stage4 = {}, {}, {}, {}
    for ch, d in order:
        copy = pltpu.make_async_remote_copy(
            src_ref=part_ref.at[place(1 - core, peer(d), ch)], dst_ref=core_in.at[local(peer(d), ch)],
            send_sem=s1.at[d, ch], recv_sem=r1.at[d, ch], device_id=(blk, other), device_id_type=MESH)
        copy.start()
        stage1[ch, d] = copy
    for ch, d in order:
        if d == 0:
            continue
        stage1[ch, d].wait_recv()
        total = part_ref[place(core, peer(d), ch), :] + core_in[local(peer(d), ch), :]
        send_buf[d - 1, ch] = total.astype(jnp.bfloat16)
        copy = pltpu.make_async_remote_copy(
            src_ref=send_buf.at[d - 1, ch], dst_ref=recv_buf.at[d - 1, ch],
            send_sem=s2.at[d, ch], recv_sem=r2.at[d, ch],
            device_id=(blk, peer(d) * 2 + core), device_id_type=MESH)
        copy.start()
        stage2[ch, d] = copy
    for ch in range(chunks):
        stage1[ch, 0].wait_recv()
        total = part_ref[place(core, chip, ch), :] + core_in[local(chip, ch), :]
        for d in range(1, chips):
            stage2[ch, d].wait_recv()
            total = total + recv_buf[d - 1, ch].astype(jnp.float32)
        mine = place(core, chip, ch)
        agg_ref[mine, :] = total.astype(jnp.bfloat16)
        for d in list(range(1, chips)) + [0]:
            target = other if d == 0 else peer(d) * 2 + core
            copy = pltpu.make_async_remote_copy(
                src_ref=agg_ref.at[mine], dst_ref=agg_ref.at[mine],
                send_sem=s3.at[d, ch], recv_sem=r3.at[d, ch],
                device_id=(blk, target), device_id_type=MESH)
            copy.start()
            stage3[ch, d] = copy
    for ch in range(chunks):
        for d in range(1, chips):
            stage3[ch, d].wait_recv()
            came = place(core, lax.rem(chip + chips - d, chips), ch)
            copy = pltpu.make_async_remote_copy(
                src_ref=agg_ref.at[came], dst_ref=agg_ref.at[came],
                send_sem=s4.at[d, ch], recv_sem=r4.at[d, ch],
                device_id=(blk, other), device_id_type=MESH)
            copy.start()
            stage4[ch, d] = copy
    for ch, d in order:
        stage1[ch, d].wait_send()
        stage3[ch, d].wait_send()
        if d == 0:
            stage3[ch, d].wait_recv()
        else:
            stage2[ch, d].wait_send()
            stage4[ch, d].wait()


def replica_sum(part, replicas):
    rows, width = part.shape
    chips = replicas // 2
    chunks = largest_divisor(rows // 2 // chips // 16, CHUNKS)
    size = rows // 2 // chips // chunks
    dma = pltpu.SemaphoreType.DMA((chips, chunks))
    vmem = pl.BlockSpec(memory_space=pltpu.VMEM)
    return pl.pallas_call(
        functools.partial(reduce_kernel, chips, chunks),
        out_shape=jax.ShapeDtypeStruct((rows, width), jnp.bfloat16),
        in_specs=[vmem],
        out_specs=vmem,
        scratch_shapes=[
            pltpu.VMEM((rows // 2, width), jnp.float32),
            pltpu.VMEM((chips - 1, chunks, size, width), jnp.bfloat16),
            pltpu.VMEM((chips - 1, chunks, size, width), jnp.bfloat16),
        ] + [dma] * 8,
        compiler_params=pltpu.CompilerParams(collective_id=0, has_side_effects=True, vmem_limit_bytes=GRANT),
        name="replica_sum",
    )(part)


def activate_kernel(steps, agg_ref, weight_ref, bias_ref, out_ref, buffer, sems):
    size = agg_ref.shape[0] // steps
    copies = []
    for i in range(steps):
        span = pl.ds(i * size, size)
        output = jnp.dot(agg_ref[span, :], weight_ref[...], preferred_element_type=jnp.float32) + bias_ref[...]
        buffer[span, :] = jnp.maximum(output, 0.0).astype(buffer.dtype)
        copies.append(pltpu.make_async_copy(buffer.at[span], out_ref.at[span], sems.at[i]))
        copies[i].start()
    for copy in copies:
        copy.wait()


def activate(aggregated, weight, bias):
    rows, width = aggregated.shape
    hidden = weight.shape[1]
    steps = largest_divisor(rows // 16, OUT_STEPS)
    vmem = pl.BlockSpec(memory_space=pltpu.VMEM)
    return pl.pallas_call(
        functools.partial(activate_kernel, steps),
        out_shape=jax.ShapeDtypeStruct((rows, hidden), jnp.bfloat16),
        in_specs=[vmem, vmem, vmem],
        out_specs=pl.BlockSpec(memory_space=pltpu.HBM),
        scratch_shapes=[pltpu.VMEM((rows, hidden), jnp.bfloat16), pltpu.SemaphoreType.DMA((steps,))],
        compiler_params=pltpu.CompilerParams(vmem_limit_bytes=GRANT),
        name="activate",
    )(aggregated, weight, bias[None, :])


def shards(blocks, replicas, features, weight, bias, tile_values, tile_place, tile_count):
    sources, held = gather_sources(features, tile_values, blocks, replicas)
    part = section_sums(sources, held, tile_place, tile_count)
    if replicas == 4:
        return flush(swap_and_activate(part, weight, bias))
    return activate(replica_sum(part, replicas), weight, bias)


def solution(mesh):
    in_specs = (
        P("blk", None),
        P(),
        P(),
        P("blk", "rep", None, None, None),
        P("blk", "rep", None),
        P("blk", "rep"),
    )
    body = functools.partial(shards, mesh.shape["blk"], mesh.shape["rep"])
    return jax.shard_map(body, mesh=mesh, in_specs=in_specs, out_specs=P("blk", None), check_vma=False)
```

```python
import functools
import heapq
import random

import jax
import jax.numpy as jnp
from jax import lax
from jax.experimental import pallas as pl
from jax.experimental.pallas import tpu as pltpu
from jax.sharding import PartitionSpec as P

MESH = pl.DeviceIdType.MESH
GROUP = 80
CHUNKS = 4
PIECES = 16
HOP = 7
WAIT = 5
ROUNDS = 40
LEAD = 0
PASSES = 768
SEED = 36660
EXPRESS = 1
URGENCY = 0.2
TOLL = 1.0
SPREAD = 4.0
OUT_STEPS = 8
SWAPS = (1,) * 8
GRANT = 16 * 1024 * 1024


def largest_divisor(number, most):
    return max(d for d in range(1, most + 1) if number % d == 0)


def chip_grid(blocks, replicas):
    columns = 2
    floors, planes = blocks // columns, replicas // 2
    chips = [(z, x, y) for z in range(floors) for x in range(columns) for y in range(planes)]
    ways = {}
    for z, x, y in chips:
        out = [(0, (z, columns - 1 - x, y), [(z, x, y, 0)])]
        out += [(3, (z, x, 1 - y), [(z, x, y, 3)])] if planes == 2 else [
            (3 + (side < 0), (z, x, y + side), [(z, x, y, 3 + (side < 0))])
            for side in (1, -1) if 0 <= y + side < planes]
        for far in range(1, EXPRESS + 1):
            for side in (1, -1):
                if 0 <= z + side * far < floors:
                    first = 1 if far == 1 else 2 * far + 1
                    crossed = [(z + side * k, x, y, 1 + (side < 0)) for k in range(far)]
                    out.append((first + (side < 0), (z + side * far, x, y), crossed))
        ways[z, x, y] = out
    return columns, planes, chips, ways


def plan_trees(blocks, replicas, sections, pieces, hop, passes):
    columns, planes, chips, ways = chip_grid(blocks, replicas)
    order = {chip: i for i, chip in enumerate(chips)}
    core_of = {}
    for b in range(blocks):
        for r in range(replicas):
            for i in range(sections):
                core_of[(b // columns, b % columns, r // 2), (b - r * sections - i) % blocks] = r % 2
    roots = {s: [(s // columns, s % columns, y) for y in range(planes)] for s in range(blocks)}
    wants = {s: [c for c in chips if (c, s) in core_of and c not in roots[s]] for s in range(blocks)}
    busy = {link: 0 for chip in chips for _, _, crossed in ways[chip] for link in crossed}
    load = dict.fromkeys(busy, 0)
    past = dict.fromkeys(busy, 0.0)
    trees, best, mine = {}, None, {}
    keys = [(s, p) for p in range(pieces) for s in range(blocks)]
    turn, draw = list(keys), SEED

    def grow(s, price):
        ready = dict.fromkeys(roots[s], 0)
        left, tree = set(wants[s]), []
        while left:
            cost, came, done = {}, {}, set()
            heap = [(URGENCY * t, t, order[c], c) for c, t in ready.items()]
            heapq.heapify(heap)
            while True:
                c, t, _, chip = heapq.heappop(heap)
                if chip in done:
                    continue
                done.add(chip)
                if chip in left:
                    break
                for way, other, crossed in ways[chip]:
                    if other in ready or other in done:
                        continue
                    taken, toll = 0, 0.0
                    for link in crossed:
                        taken |= busy[link]
                        toll += price[link] + SPREAD * mine.get((s, link), 0) / pieces
                    taken >>= t
                    start = t + (~taken & (taken + 1)).bit_length() - 1
                    there = start + hop + len(crossed) - 1
                    total = c + URGENCY * (there - t) + toll
                    if other not in cost or total < cost[other]:
                        cost[other] = total
                        came[other] = (chip, way, start, crossed, there)
                        heapq.heappush(heap, (total, there, order[other], other))
            path = []
            while chip not in ready:
                path.append(came[chip] + (chip,))
                chip = came[chip][0]
            for chip, way, start, crossed, there, other in reversed(path):
                ready[other] = there
                for link in crossed:
                    busy[link] |= 1 << start
                    load[link] += 1
                    mine[s, link] = mine.get((s, link), 0) + 1
                tree.append((chip, way, start, other, crossed))
                left.discard(other)
        return tree

    for _ in range(passes):
        for key in turn:
            for _, _, start, _, crossed in trees.get(key, ()):
                for link in crossed:
                    busy[link] &= ~(1 << start)
                    load[link] -= 1
                    mine[key[0], link] -= 1
            top = max(max(load.values()), 1)
            trees[key] = grow(key[0], {k: TOLL * (past[k] + (load[k] / top) ** 4) for k in load})
        last = {key: max(start for _, _, start, _, _ in tree) for key, tree in trees.items()}
        span = max(last.values())
        score = (span, sum(v >= span - 1 for v in last.values()), sum(load.values()))
        if best is None or score < best[0]:
            best = (score, {key: list(tree) for key, tree in trees.items()})
        top = max(load.values())
        for k in load:
            past[k] = past[k] * 0.9 + (0.2 if load[k] >= top - pieces * 0.05 else 0.0)
        ranks = []
        for key in keys:
            draw = (draw * 1103515245 + 12345) % (1 << 31)
            ranks.append(((draw >> 8) % 1000 / 125 - last[key], key))
        turn = [key for _, key in sorted(ranks)]
    return best[1], core_of


def list_times(trees, hop, bonus):
    kids, to_go, queues, arrivals = {}, {}, {}, {}
    starts, last, number, slot = {}, dict.fromkeys(trees, 0), 0, 0
    left = sum(len(tree) for tree in trees.values())

    def enqueue(key, i):
        nonlocal number
        chip, way = trees[key][i][:2]
        heapq.heappush(queues.setdefault((chip, way), []), (-(to_go[key][i] * hop + bonus[key]), number, key, i))
        number += 1

    for key, tree in trees.items():
        kids[key], to_go[key] = {}, {}
        for i, (chip, _, _, _, _) in enumerate(tree):
            kids[key].setdefault(chip, []).append(i)
        for i in reversed(range(len(tree))):
            to_go[key][i] = 1 + max([to_go[key][j] for j in kids[key].get(tree[i][3], [])], default=0)
        reached = {other for _, _, _, other, _ in tree}
        for i, (chip, _, _, _, _) in enumerate(tree):
            if chip not in reached:
                enqueue(key, i)
    while left:
        for key, i in arrivals.pop(slot, []):
            for j in kids[key].get(trees[key][i][3], []):
                enqueue(key, j)
        for queue in queues.values():
            if queue:
                _, _, key, i = heapq.heappop(queue)
                starts[key, i] = slot
                arrivals.setdefault(slot + hop, []).append((key, i))
                last[key] = max(last[key], slot + hop)
                left -= 1
        slot += 1
    return starts, last


def retime(trees, hop, rounds):
    draw, bonus, best = random.Random(1), dict.fromkeys(trees, 0.0), None
    for _ in range(rounds):
        starts, last = list_times(trees, hop, bonus)
        span = max(last.values())
        score = (span, sum(v >= span - 1 for v in last.values()))
        if best is None or score < best[0]:
            best = (score, starts)
        for key in bonus:
            late = 1.0 if last[key] >= span - 1 else 0.3 if last[key] >= span - 3 else 0.0
            bonus[key] = bonus[key] * 0.95 + late * draw.random() * 2
    return {
        key: [(chip, way, best[1][key, i], other, crossed) for i, (chip, way, _, other, crossed) in enumerate(tree)]
        for key, tree in trees.items()}


def plan_gather(blocks, replicas, sections, pieces, hop, passes):
    trees, core_of = plan_trees(blocks, replicas, sections, pieces, hop, passes)
    trees = retime(trees, WAIT, ROUNDS)
    columns, planes, chips, _ = chip_grid(blocks, replicas)
    devices = blocks * replicas
    actions = [[] for _ in range(devices)]
    arrived = [set() for _ in range(devices)]

    def core(chip, s, p):
        return core_of.get((chip, s), p % 2) if chip[:2] != (s // columns, s % columns) else p % 2

    def device(chip, c):
        return (chip[0] * columns + chip[1]) * replicas + chip[2] * 2 + c

    for (s, p), tree in sorted(trees.items()):
        for chip, way, start, other, _ in tree:
            here, there = core(chip, s, p), core(other, s, p)
            own = chip[:2] == (s // columns, s % columns)
            actions[device(chip, here)].append((start - (LEAD if own else 0), not own, s * pieces + p, way, there))
            arrived[device(other, there)].add(s * pieces + p)
    plans = []
    for d in range(devices):
        slots, waited = [], set()
        for _, relay, piece, way, there in sorted(actions[d]):
            spot = None
            for j in range(len(slots) - 1, -1, -1):
                if slots[j][0] == piece:
                    spot = j
                    break
                if way in slots[j][2]:
                    break
            if spot is None:
                slots.append((piece, relay and piece not in waited, {}))
                spot = len(slots) - 1
                if relay:
                    waited.add(piece)
            slots[spot][2][way] = there
        leaves = arrived[d] - waited
        plans.append((slots, leaves))
    return plans


def used_ways(plans):
    used = {way for slots, _ in plans for _, _, sends in slots for way in sends}
    pairs = {1: 2, 2: 1, 3: 3, 4: 3}
    return sorted(used | {0 if w == 0 else pairs.get(w, w + 1 if w % 2 else w - 1) for w in used})


def gather_kernel(blocks, replicas, sections, pieces, plans, features_ref, tiles_ref, all_ref, held_ref,
                  table_ref, recv_sem, send_sem, own_sem, held_sem):
    blk, rep = lax.axis_index("blk"), lax.axis_index("rep")
    columns, planes, _, _ = chip_grid(blocks, replicas)
    floors = blocks // columns
    rows = features_ref.shape[0]
    size = rows // pieces
    z, x = lax.div(blk, columns), lax.rem(blk, columns)
    y, me = lax.div(rep, 2), lax.rem(rep, 2)
    is_blk = [blk == b for b in range(blocks)]
    is_rep = [rep == r for r in range(replicas)]

    def choose(options, tests):
        value = jnp.int32(options[0])
        for option, test in zip(options[1:], tests[1:]):
            value = jnp.where(test, option, value)
        return value

    def pick(values):
        if len(set(values)) == 1:
            return jnp.int32(values[0])
        picked = []
        for b in range(blocks):
            row = values[b * replicas:(b + 1) * replicas]
            picked.append(row[0] if len(set(row)) == 1 else choose(row, is_rep))
        return choose(picked, is_blk)

    def target(way, c):
        if way == 0:
            return (z * columns + (columns - 1 - x), y * 2 + c)
        if way in (3, 4):
            return (blk, (1 - y if planes == 2 else y + (1 if way == 3 else -1)) * 2 + c)
        far = 1 if way < 3 else (way - 1) // 2
        return (blk + (far if way % 2 else -far) * columns, y * 2 + c)

    exists = {}
    for way in used_ways(plans):
        if way == 0 or (way == 3 and planes == 2):
            exists[way] = None
        elif way in (3, 4):
            exists[way] = y < planes - 1 if way == 3 else y > 0
        else:
            far = 1 if way < 3 else (way - 1) // 2
            exists[way] = z < floors - far if way % 2 else z >= far

    own = pltpu.make_async_copy(features_ref, all_ref.at[blk], own_sem)
    own.start()
    barrier = pltpu.get_barrier_semaphore()
    count = jnp.int32(0)
    for way, test in exists.items():
        def greet(way=way):
            for c in range(2):
                pl.semaphore_signal(barrier, inc=1, device_id=target(way, c), device_id_type=MESH)
        if test is None:
            greet()
            count = count + 2
        else:
            pl.when(test)(greet)
            count = count + jnp.where(test, 2, 0)
    steps = max(len(slots) for slots, _ in plans)
    ways = sorted(exists)
    shift = pieces.bit_length() - 1
    for j in range(steps):
        values = []
        for slots, _ in plans:
            piece, relay, sends = slots[j] if j < len(slots) else (0, False, {})
            values.append((piece * 2 + int(relay) << 2 * len(ways)) + sum(2 + sends[w] << 2 * k for k, w in enumerate(ways) if w in sends))
        table_ref[j] = pick(values)
    run = min(pieces, 16)
    words = [(i, first) for i in range(sections) for first in range(0, pieces, run)]
    for n, (i, first) in enumerate(words):
        values = []
        for d, (_, leaves) in enumerate(plans):
            s = (d // replicas - d % replicas * sections - i) % blocks
            values.append(sum(1 << p for p in range(run) if s * pieces + first + p in leaves))
        table_ref[steps + n] = pick(values)
    pl.semaphore_wait(barrier, count)

    def block(piece):
        return all_ref.at[piece >> shift, pl.ds(pl.multiple_of((piece & (pieces - 1)) * size, size), size)]

    def copy(piece, way, c, j):
        return pltpu.make_async_remote_copy(
            src_ref=block(piece), dst_ref=block(piece), send_sem=send_sem.at[j, ways.index(way)],
            recv_sem=recv_sem.at[piece], device_id=target(way, c), device_id_type=MESH)

    def unpack(j):
        value = table_ref[j]
        return value >> (2 * len(ways) + 1), (value >> (2 * len(ways))) & 1 == 1, [
            (way, (value >> (2 * k + 1)) & 1 == 1, (value >> (2 * k)) & 1) for k, way in enumerate(ways)]

    own.wait()
    held = pltpu.make_async_copy(tiles_ref, held_ref, held_sem)
    held.start()

    def step(j, carry):
        piece, relay, sends = unpack(j)
        pl.when(relay)(lambda: copy(piece, 0, 0, j).wait_recv())
        for way, test, c in sends:
            pl.when(test)(lambda way=way, c=c: copy(piece, way, c, j).start())
        return carry

    def drain(j, carry):
        piece, _, sends = unpack(j)
        for way, test, c in sends:
            pl.when(test)(lambda way=way, c=c: copy(piece, way, c, j).wait_send())
        return carry

    lax.fori_loop(0, steps, step, 0)
    lax.fori_loop(0, steps * 3 // 4, drain, 0)
    for n, (i, first) in enumerate(words):
        source = lax.rem(blk - rep * sections - i + blocks, blocks)
        mask = table_ref[steps + n]

        def leaf(p, carry, start=source * pieces + first, mask=mask):
            pl.when((mask >> p) & 1 == 1)(lambda: copy(start + p, 0, 0, 0).wait_recv())
            return carry

        lax.fori_loop(0, run, leaf, 0)
    lax.fori_loop(steps * 3 // 4, steps, drain, 0)
    held.wait()


def gather_sources(features, tile_values, blocks, replicas):
    sections = tile_values.shape[1]
    rows, width = features.shape
    pieces = PIECES
    while rows % (16 * pieces):
        pieces //= 2
    plans = plan_gather(blocks, replicas, sections, pieces, HOP, max(2, PASSES // (blocks * replicas)))
    steps = max(len(slots) for slots, _ in plans)
    ways = len(used_ways(plans))
    vmem = pl.BlockSpec(memory_space=pltpu.VMEM)
    hbm = pl.BlockSpec(memory_space=pltpu.HBM)
    dma = pltpu.SemaphoreType.DMA
    return pl.pallas_call(
        functools.partial(gather_kernel, blocks, replicas, sections, pieces, plans),
        out_shape=(
            jax.ShapeDtypeStruct((blocks, rows, width), features.dtype),
            jax.ShapeDtypeStruct(tile_values.shape, tile_values.dtype),
        ),
        in_specs=[hbm, hbm],
        out_specs=(vmem, vmem),
        scratch_shapes=[
            pltpu.SMEM((steps + sections * pl.cdiv(pieces, 16),), jnp.int32), dma((blocks * pieces,)), dma((steps, ways)), dma(()), dma(())
        ],
        compiler_params=pltpu.CompilerParams(collective_id=1, has_side_effects=True, vmem_limit_bytes=2 * GRANT),
        cost_estimate=pl.CostEstimate(
            flops=0, bytes_accessed=96 * rows * width * features.dtype.itemsize, transcendentals=0
        ),
        name="gather_sources",
    )(pltpu.with_memory_space_constraint(features, pltpu.HBM), tile_values)


def sections_kernel(group, place_ref, count_ref, source_ref, tiles_ref, acc_ref):
    sections, slots, tile = tiles_ref.shape[1:4]
    blocks, row_tiles = source_ref.shape[0], source_ref.shape[1] // tile
    blk, rep = lax.axis_index("blk"), lax.axis_index("rep")
    acc_ref[...] = jnp.zeros_like(acc_ref)
    for section in range(sections):
        source = lax.rem(blk - rep * sections - section + blocks, blocks)
        count = count_ref[0, section]

        def body(g, carry, size=group, first=0, section=section, source=source, count=count):
            for u in range(size):
                k = first + g * size + u
                place = place_ref[0, section, k]
                column, target = lax.rem(place, row_tiles), lax.div(place, row_tiles)
                piece = source_ref[source, pl.ds(pl.multiple_of(column * tile, tile), tile), :]
                product = jnp.dot(tiles_ref[0, section, k], piece, preferred_element_type=jnp.float32)
                rows = pl.ds(pl.multiple_of(target * tile, tile), tile)
                acc_ref[rows, :] += jnp.where(k < count, product, 0.0)
            return carry

        half = group // 2 if group % 2 == 0 else group
        full = lax.div(count + group - half - 1, group)
        lax.fori_loop(0, full, body, 0)
        if half < group:
            left = count - full * group
            lax.fori_loop(0, jnp.where(left > 0, 1, 0), functools.partial(body, size=half, first=full * group), 0)


def section_sums(sources, tile_values, tile_place, tile_count):
    slots = tile_values.shape[2]
    rows, width = sources.shape[1:]
    vmem = pl.BlockSpec(memory_space=pltpu.VMEM)
    smem = pl.BlockSpec(memory_space=pltpu.SMEM)
    return pl.pallas_call(
        functools.partial(sections_kernel, largest_divisor(slots, GROUP)),
        out_shape=jax.ShapeDtypeStruct((rows, width), jnp.float32),
        in_specs=[smem, smem, vmem, vmem],
        out_specs=vmem,
        compiler_params=pltpu.CompilerParams(vmem_limit_bytes=2 * GRANT),
        name="section_sums",
    )(tile_place, tile_count, sources, tile_values)


def swap_kernel(sizes, part_ref, weight_ref, bias_ref, act_ref, agg_ref, core_in, send_buf, recv_buf,
                s1, r1, s2, r2, s3, r3):
    blk, rep = lax.axis_index("blk"), lax.axis_index("rep")
    core, chip = lax.rem(rep, 2), lax.div(rep, 2)
    half = part_ref.shape[0] // 2
    other, across = chip * 2 + (1 - core), (1 - chip) * 2 + core
    chunks = len(sizes)
    spans = [pl.ds(sum(sizes[:ch]), sizes[ch]) for ch in range(chunks)]

    def place(which, ch):
        return pl.ds(pl.multiple_of(which * half + sum(sizes[:ch]), min(sizes)), sizes[ch])

    def finish(which, ch):
        span = place(which, ch)
        output = jnp.dot(agg_ref[span, :], weight_ref[...], preferred_element_type=jnp.float32) + bias_ref[...]
        act_ref[span, :] = jnp.maximum(output, 0.0).astype(act_ref.dtype)

    barrier = pltpu.get_barrier_semaphore()
    for target in (other, across):
        pl.semaphore_signal(barrier, inc=1, device_id=(blk, target), device_id_type=MESH)
    pl.semaphore_wait(barrier, 2)

    stage1, stage2, stage3 = [], [], []
    for ch, span in enumerate(spans):
        stage1.append(pltpu.make_async_remote_copy(
            src_ref=part_ref.at[place(1 - core, ch)], dst_ref=core_in.at[span],
            send_sem=s1.at[ch], recv_sem=r1.at[ch], device_id=(blk, other), device_id_type=MESH))
        stage1[ch].start()
    for ch, span in enumerate(spans):
        stage1[ch].wait_recv()
        send_buf[span, :] = (part_ref[place(core, ch), :] + core_in[span, :]).astype(send_buf.dtype)
        stage2.append(pltpu.make_async_remote_copy(
            src_ref=send_buf.at[span], dst_ref=recv_buf.at[span],
            send_sem=s2.at[ch], recv_sem=r2.at[ch], device_id=(blk, across), device_id_type=MESH))
        stage2[ch].start()
    for ch, span in enumerate(spans):
        stage2[ch].wait_recv()
        mine = place(core, ch)
        total = send_buf[span, :].astype(jnp.float32) + recv_buf[span, :].astype(jnp.float32)
        agg_ref[mine, :] = total.astype(agg_ref.dtype)
        stage3.append(pltpu.make_async_remote_copy(
            src_ref=agg_ref.at[mine], dst_ref=agg_ref.at[mine],
            send_sem=s3.at[ch], recv_sem=r3.at[ch], device_id=(blk, other), device_id_type=MESH))
        stage3[ch].start()
        finish(core, ch)
        if ch:
            stage3[ch - 1].wait_recv()
            finish(1 - core, ch - 1)
    for ch in range(chunks):
        stage1[ch].wait_send()
        stage2[ch].wait_send()
    stage3[chunks - 1].wait_recv()
    finish(1 - core, chunks - 1)
    for ch in range(chunks):
        stage3[ch].wait_send()


def swap_and_activate(part, weight, bias):
    rows, width = part.shape
    hidden = weight.shape[1]
    half = rows // 2
    unit = half // sum(SWAPS)
    sizes = [unit * share for share in SWAPS] if unit * sum(SWAPS) == half and unit % 16 == 0 else [half]
    dma = pltpu.SemaphoreType.DMA((len(sizes),))
    vmem = pl.BlockSpec(memory_space=pltpu.VMEM)
    return pl.pallas_call(
        functools.partial(swap_kernel, sizes),
        out_shape=jax.ShapeDtypeStruct((rows, hidden), jnp.bfloat16),
        in_specs=[vmem, vmem, vmem],
        out_specs=vmem,
        scratch_shapes=[
            pltpu.VMEM((rows, width), jnp.bfloat16),
            pltpu.VMEM((half, width), jnp.float32),
            pltpu.VMEM((half, width), jnp.bfloat16),
            pltpu.VMEM((half, width), jnp.bfloat16),
        ] + [dma] * 6,
        compiler_params=pltpu.CompilerParams(collective_id=0, has_side_effects=True, vmem_limit_bytes=GRANT),
        name="swap_and_activate",
    )(part, weight, bias[None, :])


def flush_kernel(steps, act_ref, out_ref, sems):
    size = act_ref.shape[0] // steps
    spans = [pl.ds(i * size, size) for i in range(steps)]
    copies = [pltpu.make_async_copy(act_ref.at[span], out_ref.at[span], sems.at[i]) for i, span in enumerate(spans)]
    for copy in copies:
        copy.start()
    for copy in copies:
        copy.wait()


def flush(activations):
    steps = largest_divisor(activations.shape[0] // 16, OUT_STEPS)
    return pl.pallas_call(
        functools.partial(flush_kernel, steps),
        out_shape=jax.ShapeDtypeStruct(activations.shape, activations.dtype),
        in_specs=[pl.BlockSpec(memory_space=pltpu.VMEM)],
        out_specs=pl.BlockSpec(memory_space=pltpu.HBM),
        scratch_shapes=[pltpu.SemaphoreType.DMA((steps,))],
        compiler_params=pltpu.CompilerParams(vmem_limit_bytes=GRANT),
        name="flush",
    )(activations)


def reduce_kernel(chips, chunks, part_ref, agg_ref, core_in, send_buf, recv_buf,
                  s1, r1, s2, r2, s3, r3, s4, r4):
    blk, rep = lax.axis_index("blk"), lax.axis_index("rep")
    core, chip = lax.rem(rep, 2), lax.div(rep, 2)
    rows = part_ref.shape[0]
    half = rows // 2
    size = half // chips // chunks
    other = chip * 2 + (1 - core)

    def peer(d):
        return lax.rem(chip + d, chips)

    def local(piece, ch):
        return pl.ds(pl.multiple_of((piece * chunks + ch) * size, size), size)

    def place(which, piece, ch):
        return pl.ds(pl.multiple_of(which * half + (piece * chunks + ch) * size, size), size)

    barrier = pltpu.get_barrier_semaphore()
    pl.semaphore_signal(barrier, inc=1, device_id=(blk, other), device_id_type=MESH)
    for d in range(1, chips):
        pl.semaphore_signal(barrier, inc=1, device_id=(blk, peer(d) * 2 + core), device_id_type=MESH)
    pl.semaphore_wait(barrier, chips)

    order = [(ch, d) for ch in range(chunks) for d in list(range(1, chips)) + [0]]
    stage1, stage2, stage3, stage4 = {}, {}, {}, {}
    for ch, d in order:
        copy = pltpu.make_async_remote_copy(
            src_ref=part_ref.at[place(1 - core, peer(d), ch)], dst_ref=core_in.at[local(peer(d), ch)],
            send_sem=s1.at[d, ch], recv_sem=r1.at[d, ch], device_id=(blk, other), device_id_type=MESH)
        copy.start()
        stage1[ch, d] = copy
    for ch, d in order:
        if d == 0:
            continue
        stage1[ch, d].wait_recv()
        total = part_ref[place(core, peer(d), ch), :] + core_in[local(peer(d), ch), :]
        send_buf[d - 1, ch] = total.astype(jnp.bfloat16)
        copy = pltpu.make_async_remote_copy(
            src_ref=send_buf.at[d - 1, ch], dst_ref=recv_buf.at[d - 1, ch],
            send_sem=s2.at[d, ch], recv_sem=r2.at[d, ch],
            device_id=(blk, peer(d) * 2 + core), device_id_type=MESH)
        copy.start()
        stage2[ch, d] = copy
    for ch in range(chunks):
        stage1[ch, 0].wait_recv()
        total = part_ref[place(core, chip, ch), :] + core_in[local(chip, ch), :]
        for d in range(1, chips):
            stage2[ch, d].wait_recv()
            total = total + recv_buf[d - 1, ch].astype(jnp.float32)
        mine = place(core, chip, ch)
        agg_ref[mine, :] = total.astype(jnp.bfloat16)
        for d in list(range(1, chips)) + [0]:
            target = other if d == 0 else peer(d) * 2 + core
            copy = pltpu.make_async_remote_copy(
                src_ref=agg_ref.at[mine], dst_ref=agg_ref.at[mine],
                send_sem=s3.at[d, ch], recv_sem=r3.at[d, ch],
                device_id=(blk, target), device_id_type=MESH)
            copy.start()
            stage3[ch, d] = copy
    for ch in range(chunks):
        for d in range(1, chips):
            stage3[ch, d].wait_recv()
            came = place(core, lax.rem(chip + chips - d, chips), ch)
            copy = pltpu.make_async_remote_copy(
                src_ref=agg_ref.at[came], dst_ref=agg_ref.at[came],
                send_sem=s4.at[d, ch], recv_sem=r4.at[d, ch],
                device_id=(blk, other), device_id_type=MESH)
            copy.start()
            stage4[ch, d] = copy
    for ch, d in order:
        stage1[ch, d].wait_send()
        stage3[ch, d].wait_send()
        if d == 0:
            stage3[ch, d].wait_recv()
        else:
            stage2[ch, d].wait_send()
            stage4[ch, d].wait()


def replica_sum(part, replicas):
    rows, width = part.shape
    chips = replicas // 2
    chunks = largest_divisor(rows // 2 // chips // 16, CHUNKS)
    size = rows // 2 // chips // chunks
    dma = pltpu.SemaphoreType.DMA((chips, chunks))
    vmem = pl.BlockSpec(memory_space=pltpu.VMEM)
    return pl.pallas_call(
        functools.partial(reduce_kernel, chips, chunks),
        out_shape=jax.ShapeDtypeStruct((rows, width), jnp.bfloat16),
        in_specs=[vmem],
        out_specs=vmem,
        scratch_shapes=[
            pltpu.VMEM((rows // 2, width), jnp.float32),
            pltpu.VMEM((chips - 1, chunks, size, width), jnp.bfloat16),
            pltpu.VMEM((chips - 1, chunks, size, width), jnp.bfloat16),
        ] + [dma] * 8,
        compiler_params=pltpu.CompilerParams(collective_id=0, has_side_effects=True, vmem_limit_bytes=GRANT),
        name="replica_sum",
    )(part)


def activate_kernel(steps, agg_ref, weight_ref, bias_ref, out_ref, buffer, sems):
    size = agg_ref.shape[0] // steps
    copies = []
    for i in range(steps):
        span = pl.ds(i * size, size)
        output = jnp.dot(agg_ref[span, :], weight_ref[...], preferred_element_type=jnp.float32) + bias_ref[...]
        buffer[span, :] = jnp.maximum(output, 0.0).astype(buffer.dtype)
        copies.append(pltpu.make_async_copy(buffer.at[span], out_ref.at[span], sems.at[i]))
        copies[i].start()
    for copy in copies:
        copy.wait()


def activate(aggregated, weight, bias):
    rows, width = aggregated.shape
    hidden = weight.shape[1]
    steps = largest_divisor(rows // 16, OUT_STEPS)
    vmem = pl.BlockSpec(memory_space=pltpu.VMEM)
    return pl.pallas_call(
        functools.partial(activate_kernel, steps),
        out_shape=jax.ShapeDtypeStruct((rows, hidden), jnp.bfloat16),
        in_specs=[vmem, vmem, vmem],
        out_specs=pl.BlockSpec(memory_space=pltpu.HBM),
        scratch_shapes=[pltpu.VMEM((rows, hidden), jnp.bfloat16), pltpu.SemaphoreType.DMA((steps,))],
        compiler_params=pltpu.CompilerParams(vmem_limit_bytes=GRANT),
        name="activate",
    )(aggregated, weight, bias[None, :])


def shards(blocks, replicas, features, weight, bias, tile_values, tile_place, tile_count):
    sources, held = gather_sources(features, tile_values, blocks, replicas)
    part = section_sums(sources, held, tile_place, tile_count)
    if replicas == 4:
        return flush(swap_and_activate(part, weight, bias))
    return activate(replica_sum(part, replicas), weight, bias)


def solution(mesh):
    in_specs = (
        P("blk", None),
        P(),
        P(),
        P("blk", "rep", None, None, None),
        P("blk", "rep", None),
        P("blk", "rep"),
    )
    body = functools.partial(shards, mesh.shape["blk"], mesh.shape["rep"])
    return jax.shard_map(body, mesh=mesh, in_specs=in_specs, out_specs=P("blk", None), check_vma=False)
```

```python
import functools
import heapq
import random

import jax
import jax.numpy as jnp
from jax import lax
from jax.experimental import pallas as pl
from jax.experimental.pallas import tpu as pltpu
from jax.sharding import PartitionSpec as P

MESH = pl.DeviceIdType.MESH
GROUP = 80
CHUNKS = 4
PIECES = 16
HOP = 8
WAIT = 5
ROUNDS = 40
LEAD = 0
PASSES = 768
SEED = 70599
EXPRESS = 1
URGENCY = 0.25
TOLL = 1.0
SPREAD = 6.0
OUT_STEPS = 2
SWAPS = (1,) * 8
GRANT = 16 * 1024 * 1024


def largest_divisor(number, most):
    return max(d for d in range(1, most + 1) if number % d == 0)


def chip_grid(blocks, replicas):
    columns = 2
    floors, planes = blocks // columns, replicas // 2
    chips = [(z, x, y) for z in range(floors) for x in range(columns) for y in range(planes)]
    ways = {}
    for z, x, y in chips:
        out = [(0, (z, columns - 1 - x, y), [(z, x, y, 0)])]
        out += [(3, (z, x, 1 - y), [(z, x, y, 3)])] if planes == 2 else [
            (3 + (side < 0), (z, x, y + side), [(z, x, y, 3 + (side < 0))])
            for side in (1, -1) if 0 <= y + side < planes]
        for far in range(1, EXPRESS + 1):
            for side in (1, -1):
                if 0 <= z + side * far < floors:
                    first = 1 if far == 1 else 2 * far + 1
                    crossed = [(z + side * k, x, y, 1 + (side < 0)) for k in range(far)]
                    out.append((first + (side < 0), (z + side * far, x, y), crossed))
        ways[z, x, y] = out
    return columns, planes, chips, ways


def plan_trees(blocks, replicas, sections, pieces, hop, passes):
    columns, planes, chips, ways = chip_grid(blocks, replicas)
    order = {chip: i for i, chip in enumerate(chips)}
    core_of = {}
    for b in range(blocks):
        for r in range(replicas):
            for i in range(sections):
                core_of[(b // columns, b % columns, r // 2), (b - r * sections - i) % blocks] = r % 2
    roots = {s: [(s // columns, s % columns, y) for y in range(planes)] for s in range(blocks)}
    wants = {s: [c for c in chips if (c, s) in core_of and c not in roots[s]] for s in range(blocks)}
    busy = {link: 0 for chip in chips for _, _, crossed in ways[chip] for link in crossed}
    load = dict.fromkeys(busy, 0)
    past = dict.fromkeys(busy, 0.0)
    trees, best, mine = {}, None, {}
    keys = [(s, p) for p in range(pieces) for s in range(blocks)]
    turn, draw = list(keys), SEED

    def grow(s, price):
        ready = dict.fromkeys(roots[s], 0)
        left, tree = set(wants[s]), []
        while left:
            cost, came, done = {}, {}, set()
            heap = [(URGENCY * t, t, order[c], c) for c, t in ready.items()]
            heapq.heapify(heap)
            while True:
                c, t, _, chip = heapq.heappop(heap)
                if chip in done:
                    continue
                done.add(chip)
                if chip in left:
                    break
                for way, other, crossed in ways[chip]:
                    if other in ready or other in done:
                        continue
                    taken, toll = 0, 0.0
                    for link in crossed:
                        taken |= busy[link]
                        toll += price[link] + SPREAD * mine.get((s, link), 0) / pieces
                    taken >>= t
                    start = t + (~taken & (taken + 1)).bit_length() - 1
                    there = start + hop + len(crossed) - 1
                    total = c + URGENCY * (there - t) + toll
                    if other not in cost or total < cost[other]:
                        cost[other] = total
                        came[other] = (chip, way, start, crossed, there)
                        heapq.heappush(heap, (total, there, order[other], other))
            path = []
            while chip not in ready:
                path.append(came[chip] + (chip,))
                chip = came[chip][0]
            for chip, way, start, crossed, there, other in reversed(path):
                ready[other] = there
                for link in crossed:
                    busy[link] |= 1 << start
                    load[link] += 1
                    mine[s, link] = mine.get((s, link), 0) + 1
                tree.append((chip, way, start, other, crossed))
                left.discard(other)
        return tree

    for _ in range(passes):
        for key in turn:
            for _, _, start, _, crossed in trees.get(key, ()):
                for link in crossed:
                    busy[link] &= ~(1 << start)
                    load[link] -= 1
                    mine[key[0], link] -= 1
            top = max(max(load.values()), 1)
            trees[key] = grow(key[0], {k: TOLL * (past[k] + (load[k] / top) ** 4) for k in load})
        last = {key: max(start for _, _, start, _, _ in tree) for key, tree in trees.items()}
        span = max(last.values())
        score = (span, sum(v >= span - 1 for v in last.values()), sum(load.values()))
        if best is None or score < best[0]:
            best = (score, {key: list(tree) for key, tree in trees.items()})
        top = max(load.values())
        for k in load:
            past[k] = past[k] * 0.9 + (0.2 if load[k] >= top - pieces * 0.05 else 0.0)
        ranks = []
        for key in keys:
            draw = (draw * 1103515245 + 12345) % (1 << 31)
            ranks.append(((draw >> 8) % 1000 / 125 - last[key], key))
        turn = [key for _, key in sorted(ranks)]
    return best[1], core_of


def list_times(trees, hop, bonus):
    kids, to_go, queues, arrivals = {}, {}, {}, {}
    starts, last, number, slot = {}, dict.fromkeys(trees, 0), 0, 0
    left = sum(len(tree) for tree in trees.values())

    def enqueue(key, i):
        nonlocal number
        chip, way = trees[key][i][:2]
        heapq.heappush(queues.setdefault((chip, way), []), (-(to_go[key][i] * hop + bonus[key]), number, key, i))
        number += 1

    for key, tree in trees.items():
        kids[key], to_go[key] = {}, {}
        for i, (chip, _, _, _, _) in enumerate(tree):
            kids[key].setdefault(chip, []).append(i)
        for i in reversed(range(len(tree))):
            to_go[key][i] = 1 + max([to_go[key][j] for j in kids[key].get(tree[i][3], [])], default=0)
        reached = {other for _, _, _, other, _ in tree}
        for i, (chip, _, _, _, _) in enumerate(tree):
            if chip not in reached:
                enqueue(key, i)
    while left:
        for key, i in arrivals.pop(slot, []):
            for j in kids[key].get(trees[key][i][3], []):
                enqueue(key, j)
        for queue in queues.values():
            if queue:
                _, _, key, i = heapq.heappop(queue)
                starts[key, i] = slot
                arrivals.setdefault(slot + hop, []).append((key, i))
                last[key] = max(last[key], slot + hop)
                left -= 1
        slot += 1
    return starts, last


def retime(trees, hop, rounds):
    draw, bonus, best = random.Random(1), dict.fromkeys(trees, 0.0), None
    for _ in range(rounds):
        starts, last = list_times(trees, hop, bonus)
        span = max(last.values())
        score = (span, sum(v >= span - 1 for v in last.values()))
        if best is None or score < best[0]:
            best = (score, starts)
        for key in bonus:
            late = 1.0 if last[key] >= span - 1 else 0.3 if last[key] >= span - 3 else 0.0
            bonus[key] = bonus[key] * 0.95 + late * draw.random() * 2
    return {
        key: [(chip, way, best[1][key, i], other, crossed) for i, (chip, way, _, other, crossed) in enumerate(tree)]
        for key, tree in trees.items()}


def plan_gather(blocks, replicas, sections, pieces, hop, passes):
    trees, core_of = plan_trees(blocks, replicas, sections, pieces, hop, passes)
    trees = retime(trees, WAIT, ROUNDS)
    columns, planes, chips, _ = chip_grid(blocks, replicas)
    devices = blocks * replicas
    actions = [[] for _ in range(devices)]
    arrived = [set() for _ in range(devices)]

    def core(chip, s, p):
        return core_of.get((chip, s), p % 2) if chip[:2] != (s // columns, s % columns) else p % 2

    def device(chip, c):
        return (chip[0] * columns + chip[1]) * replicas + chip[2] * 2 + c

    for (s, p), tree in sorted(trees.items()):
        for chip, way, start, other, _ in tree:
            here, there = core(chip, s, p), core(other, s, p)
            own = chip[:2] == (s // columns, s % columns)
            actions[device(chip, here)].append((start - (LEAD if own else 0), not own, s * pieces + p, way, there))
            arrived[device(other, there)].add(s * pieces + p)
    plans = []
    for d in range(devices):
        slots, waited = [], set()
        for _, relay, piece, way, there in sorted(actions[d]):
            spot = None
            for j in range(len(slots) - 1, -1, -1):
                if slots[j][0] == piece:
                    spot = j
                    break
                if way in slots[j][2]:
                    break
            if spot is None:
                slots.append((piece, relay and piece not in waited, {}))
                spot = len(slots) - 1
                if relay:
                    waited.add(piece)
            slots[spot][2][way] = there
        leaves = arrived[d] - waited
        plans.append((slots, leaves))
    return plans


def used_ways(plans):
    used = {way for slots, _ in plans for _, _, sends in slots for way in sends}
    pairs = {1: 2, 2: 1, 3: 3, 4: 3}
    return sorted(used | {0 if w == 0 else pairs.get(w, w + 1 if w % 2 else w - 1) for w in used})


def gather_kernel(blocks, replicas, sections, pieces, plans, features_ref, tiles_ref, all_ref, held_ref,
                  table_ref, recv_sem, send_sem, own_sem, held_sem):
    blk, rep = lax.axis_index("blk"), lax.axis_index("rep")
    columns, planes, _, _ = chip_grid(blocks, replicas)
    floors = blocks // columns
    rows = features_ref.shape[0]
    size = rows // pieces
    z, x = lax.div(blk, columns), lax.rem(blk, columns)
    y, me = lax.div(rep, 2), lax.rem(rep, 2)
    is_blk = [blk == b for b in range(blocks)]
    is_rep = [rep == r for r in range(replicas)]

    def choose(options, tests):
        value = jnp.int32(options[0])
        for option, test in zip(options[1:], tests[1:]):
            value = jnp.where(test, option, value)
        return value

    def pick(values):
        if len(set(values)) == 1:
            return jnp.int32(values[0])
        picked = []
        for b in range(blocks):
            row = values[b * replicas:(b + 1) * replicas]
            picked.append(row[0] if len(set(row)) == 1 else choose(row, is_rep))
        return choose(picked, is_blk)

    def target(way, c):
        if way == 0:
            return (z * columns + (columns - 1 - x), y * 2 + c)
        if way in (3, 4):
            return (blk, (1 - y if planes == 2 else y + (1 if way == 3 else -1)) * 2 + c)
        far = 1 if way < 3 else (way - 1) // 2
        return (blk + (far if way % 2 else -far) * columns, y * 2 + c)

    exists = {}
    for way in used_ways(plans):
        if way == 0 or (way == 3 and planes == 2):
            exists[way] = None
        elif way in (3, 4):
            exists[way] = y < planes - 1 if way == 3 else y > 0
        else:
            far = 1 if way < 3 else (way - 1) // 2
            exists[way] = z < floors - far if way % 2 else z >= far

    own = pltpu.make_async_copy(features_ref, all_ref.at[blk], own_sem)
    own.start()
    barrier = pltpu.get_barrier_semaphore()
    count = jnp.int32(0)
    for way, test in exists.items():
        def greet(way=way):
            for c in range(2):
                pl.semaphore_signal(barrier, inc=1, device_id=target(way, c), device_id_type=MESH)
        if test is None:
            greet()
            count = count + 2
        else:
            pl.when(test)(greet)
            count = count + jnp.where(test, 2, 0)
    steps = max(len(slots) for slots, _ in plans)
    ways = sorted(exists)
    shift = pieces.bit_length() - 1
    for j in range(steps):
        values = []
        for slots, _ in plans:
            piece, relay, sends = slots[j] if j < len(slots) else (0, False, {})
            values.append((piece * 2 + int(relay) << 2 * len(ways)) + sum(2 + sends[w] << 2 * k for k, w in enumerate(ways) if w in sends))
        table_ref[j] = pick(values)
    run = min(pieces, 16)
    words = [(i, first) for i in range(sections) for first in range(0, pieces, run)]
    for n, (i, first) in enumerate(words):
        values = []
        for d, (_, leaves) in enumerate(plans):
            s = (d // replicas - d % replicas * sections - i) % blocks
            values.append(sum(1 << p for p in range(run) if s * pieces + first + p in leaves))
        table_ref[steps + n] = pick(values)
    pl.semaphore_wait(barrier, count)

    def block(piece):
        return all_ref.at[piece >> shift, pl.ds(pl.multiple_of((piece & (pieces - 1)) * size, size), size)]

    def copy(piece, way, c, j):
        return pltpu.make_async_remote_copy(
            src_ref=block(piece), dst_ref=block(piece), send_sem=send_sem.at[j, ways.index(way)],
            recv_sem=recv_sem.at[piece], device_id=target(way, c), device_id_type=MESH)

    def unpack(j):
        value = table_ref[j]
        return value >> (2 * len(ways) + 1), (value >> (2 * len(ways))) & 1 == 1, [
            (way, (value >> (2 * k + 1)) & 1 == 1, (value >> (2 * k)) & 1) for k, way in enumerate(ways)]

    own.wait()
    held = pltpu.make_async_copy(tiles_ref, held_ref, held_sem)
    held.start()

    def step(j, carry):
        piece, relay, sends = unpack(j)
        pl.when(relay)(lambda: copy(piece, 0, 0, j).wait_recv())
        for way, test, c in sends:
            pl.when(test)(lambda way=way, c=c: copy(piece, way, c, j).start())
        return carry

    def drain(j, carry):
        piece, _, sends = unpack(j)
        for way, test, c in sends:
            pl.when(test)(lambda way=way, c=c: copy(piece, way, c, j).wait_send())
        return carry

    lax.fori_loop(0, steps, step, 0)
    lax.fori_loop(0, steps * 3 // 4, drain, 0)
    for n, (i, first) in enumerate(words):
        source = lax.rem(blk - rep * sections - i + blocks, blocks)
        mask = table_ref[steps + n]

        def leaf(p, carry, start=source * pieces + first, mask=mask):
            pl.when((mask >> p) & 1 == 1)(lambda: copy(start + p, 0, 0, 0).wait_recv())
            return carry

        lax.fori_loop(0, run, leaf, 0)
    lax.fori_loop(steps * 3 // 4, steps, drain, 0)
    held.wait()


def gather_sources(features, tile_values, blocks, replicas):
    sections = tile_values.shape[1]
    rows, width = features.shape
    pieces = PIECES
    while rows % (16 * pieces):
        pieces //= 2
    plans = plan_gather(blocks, replicas, sections, pieces, HOP, max(2, PASSES // (blocks * replicas)))
    steps = max(len(slots) for slots, _ in plans)
    ways = len(used_ways(plans))
    vmem = pl.BlockSpec(memory_space=pltpu.VMEM)
    hbm = pl.BlockSpec(memory_space=pltpu.HBM)
    dma = pltpu.SemaphoreType.DMA
    return pl.pallas_call(
        functools.partial(gather_kernel, blocks, replicas, sections, pieces, plans),
        out_shape=(
            jax.ShapeDtypeStruct((blocks, rows, width), features.dtype),
            jax.ShapeDtypeStruct(tile_values.shape, tile_values.dtype),
        ),
        in_specs=[hbm, hbm],
        out_specs=(vmem, vmem),
        scratch_shapes=[
            pltpu.SMEM((steps + sections * pl.cdiv(pieces, 16),), jnp.int32), dma((blocks * pieces,)), dma((steps, ways)), dma(()), dma(())
        ],
        compiler_params=pltpu.CompilerParams(collective_id=1, has_side_effects=True, vmem_limit_bytes=2 * GRANT),
        cost_estimate=pl.CostEstimate(
            flops=0, bytes_accessed=96 * rows * width * features.dtype.itemsize, transcendentals=0
        ),
        name="gather_sources",
    )(pltpu.with_memory_space_constraint(features, pltpu.HBM), tile_values)


def sections_kernel(group, place_ref, count_ref, source_ref, tiles_ref, acc_ref):
    sections, slots, tile = tiles_ref.shape[1:4]
    blocks, row_tiles = source_ref.shape[0], source_ref.shape[1] // tile
    blk, rep = lax.axis_index("blk"), lax.axis_index("rep")
    acc_ref[...] = jnp.zeros_like(acc_ref)
    for section in range(sections):
        source = lax.rem(blk - rep * sections - section + blocks, blocks)
        count = count_ref[0, section]

        def body(g, carry, size=group, first=0, section=section, source=source, count=count):
            for u in range(size):
                k = first + g * size + u
                place = place_ref[0, section, k]
                column, target = lax.rem(place, row_tiles), lax.div(place, row_tiles)
                piece = source_ref[source, pl.ds(pl.multiple_of(column * tile, tile), tile), :]
                product = jnp.dot(tiles_ref[0, section, k], piece, preferred_element_type=jnp.float32)
                rows = pl.ds(pl.multiple_of(target * tile, tile), tile)
                acc_ref[rows, :] += jnp.where(k < count, product, 0.0)
            return carry

        half = group // 2 if group % 2 == 0 else group
        full = lax.div(count + group - half - 1, group)
        lax.fori_loop(0, full, body, 0)
        if half < group:
            left = count - full * group
            lax.fori_loop(0, jnp.where(left > 0, 1, 0), functools.partial(body, size=half, first=full * group), 0)


def section_sums(sources, tile_values, tile_place, tile_count):
    slots = tile_values.shape[2]
    rows, width = sources.shape[1:]
    vmem = pl.BlockSpec(memory_space=pltpu.VMEM)
    smem = pl.BlockSpec(memory_space=pltpu.SMEM)
    return pl.pallas_call(
        functools.partial(sections_kernel, largest_divisor(slots, GROUP)),
        out_shape=jax.ShapeDtypeStruct((rows, width), jnp.float32),
        in_specs=[smem, smem, vmem, vmem],
        out_specs=vmem,
        compiler_params=pltpu.CompilerParams(vmem_limit_bytes=2 * GRANT),
        name="section_sums",
    )(tile_place, tile_count, sources, tile_values)


def swap_kernel(sizes, part_ref, weight_ref, bias_ref, act_ref, agg_ref, core_in, send_buf, recv_buf,
                s1, r1, s2, r2, s3, r3):
    blk, rep = lax.axis_index("blk"), lax.axis_index("rep")
    core, chip = lax.rem(rep, 2), lax.div(rep, 2)
    half = part_ref.shape[0] // 2
    other, across = chip * 2 + (1 - core), (1 - chip) * 2 + core
    chunks = len(sizes)
    spans = [pl.ds(sum(sizes[:ch]), sizes[ch]) for ch in range(chunks)]

    def place(which, ch):
        return pl.ds(pl.multiple_of(which * half + sum(sizes[:ch]), min(sizes)), sizes[ch])

    def finish(which, ch):
        span = place(which, ch)
        output = jnp.dot(agg_ref[span, :], weight_ref[...], preferred_element_type=jnp.float32) + bias_ref[...]
        act_ref[span, :] = jnp.maximum(output, 0.0).astype(act_ref.dtype)

    barrier = pltpu.get_barrier_semaphore()
    for target in (other, across):
        pl.semaphore_signal(barrier, inc=1, device_id=(blk, target), device_id_type=MESH)
    pl.semaphore_wait(barrier, 2)

    stage1, stage2, stage3 = [], [], []
    for ch, span in enumerate(spans):
        stage1.append(pltpu.make_async_remote_copy(
            src_ref=part_ref.at[place(1 - core, ch)], dst_ref=core_in.at[span],
            send_sem=s1.at[ch], recv_sem=r1.at[ch], device_id=(blk, other), device_id_type=MESH))
        stage1[ch].start()
    for ch, span in enumerate(spans):
        stage1[ch].wait_recv()
        send_buf[span, :] = (part_ref[place(core, ch), :] + core_in[span, :]).astype(send_buf.dtype)
        stage2.append(pltpu.make_async_remote_copy(
            src_ref=send_buf.at[span], dst_ref=recv_buf.at[span],
            send_sem=s2.at[ch], recv_sem=r2.at[ch], device_id=(blk, across), device_id_type=MESH))
        stage2[ch].start()
    for ch, span in enumerate(spans):
        stage2[ch].wait_recv()
        mine = place(core, ch)
        total = send_buf[span, :].astype(jnp.float32) + recv_buf[span, :].astype(jnp.float32)
        agg_ref[mine, :] = total.astype(agg_ref.dtype)
        stage3.append(pltpu.make_async_remote_copy(
            src_ref=agg_ref.at[mine], dst_ref=agg_ref.at[mine],
            send_sem=s3.at[ch], recv_sem=r3.at[ch], device_id=(blk, other), device_id_type=MESH))
        stage3[ch].start()
        finish(core, ch)
        if ch:
            stage3[ch - 1].wait_recv()
            finish(1 - core, ch - 1)
    for ch in range(chunks):
        stage1[ch].wait_send()
        stage2[ch].wait_send()
    stage3[chunks - 1].wait_recv()
    finish(1 - core, chunks - 1)
    for ch in range(chunks):
        stage3[ch].wait_send()


def swap_and_activate(part, weight, bias):
    rows, width = part.shape
    hidden = weight.shape[1]
    half = rows // 2
    unit = half // sum(SWAPS)
    sizes = [unit * share for share in SWAPS] if unit * sum(SWAPS) == half and unit % 16 == 0 else [half]
    dma = pltpu.SemaphoreType.DMA((len(sizes),))
    vmem = pl.BlockSpec(memory_space=pltpu.VMEM)
    return pl.pallas_call(
        functools.partial(swap_kernel, sizes),
        out_shape=jax.ShapeDtypeStruct((rows, hidden), jnp.bfloat16),
        in_specs=[vmem, vmem, vmem],
        out_specs=vmem,
        scratch_shapes=[
            pltpu.VMEM((rows, width), jnp.bfloat16),
            pltpu.VMEM((half, width), jnp.float32),
            pltpu.VMEM((half, width), jnp.bfloat16),
            pltpu.VMEM((half, width), jnp.bfloat16),
        ] + [dma] * 6,
        compiler_params=pltpu.CompilerParams(collective_id=0, has_side_effects=True, vmem_limit_bytes=GRANT),
        name="swap_and_activate",
    )(part, weight, bias[None, :])


def flush_kernel(steps, act_ref, out_ref, sems):
    size = act_ref.shape[0] // steps
    spans = [pl.ds(i * size, size) for i in range(steps)]
    copies = [pltpu.make_async_copy(act_ref.at[span], out_ref.at[span], sems.at[i]) for i, span in enumerate(spans)]
    for copy in copies:
        copy.start()
    for copy in copies:
        copy.wait()


def flush(activations):
    steps = largest_divisor(activations.shape[0] // 16, OUT_STEPS)
    return pl.pallas_call(
        functools.partial(flush_kernel, steps),
        out_shape=jax.ShapeDtypeStruct(activations.shape, activations.dtype),
        in_specs=[pl.BlockSpec(memory_space=pltpu.VMEM)],
        out_specs=pl.BlockSpec(memory_space=pltpu.HBM),
        scratch_shapes=[pltpu.SemaphoreType.DMA((steps,))],
        compiler_params=pltpu.CompilerParams(vmem_limit_bytes=GRANT),
        name="flush",
    )(activations)


def reduce_kernel(chips, chunks, part_ref, agg_ref, core_in, send_buf, recv_buf,
                  s1, r1, s2, r2, s3, r3, s4, r4):
    blk, rep = lax.axis_index("blk"), lax.axis_index("rep")
    core, chip = lax.rem(rep, 2), lax.div(rep, 2)
    rows = part_ref.shape[0]
    half = rows // 2
    size = half // chips // chunks
    other = chip * 2 + (1 - core)

    def peer(d):
        return lax.rem(chip + d, chips)

    def local(piece, ch):
        return pl.ds(pl.multiple_of((piece * chunks + ch) * size, size), size)

    def place(which, piece, ch):
        return pl.ds(pl.multiple_of(which * half + (piece * chunks + ch) * size, size), size)

    barrier = pltpu.get_barrier_semaphore()
    pl.semaphore_signal(barrier, inc=1, device_id=(blk, other), device_id_type=MESH)
    for d in range(1, chips):
        pl.semaphore_signal(barrier, inc=1, device_id=(blk, peer(d) * 2 + core), device_id_type=MESH)
    pl.semaphore_wait(barrier, chips)

    order = [(ch, d) for ch in range(chunks) for d in list(range(1, chips)) + [0]]
    stage1, stage2, stage3, stage4 = {}, {}, {}, {}
    for ch, d in order:
        copy = pltpu.make_async_remote_copy(
            src_ref=part_ref.at[place(1 - core, peer(d), ch)], dst_ref=core_in.at[local(peer(d), ch)],
            send_sem=s1.at[d, ch], recv_sem=r1.at[d, ch], device_id=(blk, other), device_id_type=MESH)
        copy.start()
        stage1[ch, d] = copy
    for ch, d in order:
        if d == 0:
            continue
        stage1[ch, d].wait_recv()
        total = part_ref[place(core, peer(d), ch), :] + core_in[local(peer(d), ch), :]
        send_buf[d - 1, ch] = total.astype(jnp.bfloat16)
        copy = pltpu.make_async_remote_copy(
            src_ref=send_buf.at[d - 1, ch], dst_ref=recv_buf.at[d - 1, ch],
            send_sem=s2.at[d, ch], recv_sem=r2.at[d, ch],
            device_id=(blk, peer(d) * 2 + core), device_id_type=MESH)
        copy.start()
        stage2[ch, d] = copy
    for ch in range(chunks):
        stage1[ch, 0].wait_recv()
        total = part_ref[place(core, chip, ch), :] + core_in[local(chip, ch), :]
        for d in range(1, chips):
            stage2[ch, d].wait_recv()
            total = total + recv_buf[d - 1, ch].astype(jnp.float32)
        mine = place(core, chip, ch)
        agg_ref[mine, :] = total.astype(jnp.bfloat16)
        for d in list(range(1, chips)) + [0]:
            target = other if d == 0 else peer(d) * 2 + core
            copy = pltpu.make_async_remote_copy(
                src_ref=agg_ref.at[mine], dst_ref=agg_ref.at[mine],
                send_sem=s3.at[d, ch], recv_sem=r3.at[d, ch],
                device_id=(blk, target), device_id_type=MESH)
            copy.start()
            stage3[ch, d] = copy
    for ch in range(chunks):
        for d in range(1, chips):
            stage3[ch, d].wait_recv()
            came = place(core, lax.rem(chip + chips - d, chips), ch)
            copy = pltpu.make_async_remote_copy(
                src_ref=agg_ref.at[came], dst_ref=agg_ref.at[came],
                send_sem=s4.at[d, ch], recv_sem=r4.at[d, ch],
                device_id=(blk, other), device_id_type=MESH)
            copy.start()
            stage4[ch, d] = copy
    for ch, d in order:
        stage1[ch, d].wait_send()
        stage3[ch, d].wait_send()
        if d == 0:
            stage3[ch, d].wait_recv()
        else:
            stage2[ch, d].wait_send()
            stage4[ch, d].wait()


def replica_sum(part, replicas):
    rows, width = part.shape
    chips = replicas // 2
    chunks = largest_divisor(rows // 2 // chips // 16, CHUNKS)
    size = rows // 2 // chips // chunks
    dma = pltpu.SemaphoreType.DMA((chips, chunks))
    vmem = pl.BlockSpec(memory_space=pltpu.VMEM)
    return pl.pallas_call(
        functools.partial(reduce_kernel, chips, chunks),
        out_shape=jax.ShapeDtypeStruct((rows, width), jnp.bfloat16),
        in_specs=[vmem],
        out_specs=vmem,
        scratch_shapes=[
            pltpu.VMEM((rows // 2, width), jnp.float32),
            pltpu.VMEM((chips - 1, chunks, size, width), jnp.bfloat16),
            pltpu.VMEM((chips - 1, chunks, size, width), jnp.bfloat16),
        ] + [dma] * 8,
        compiler_params=pltpu.CompilerParams(collective_id=0, has_side_effects=True, vmem_limit_bytes=GRANT),
        name="replica_sum",
    )(part)


def activate_kernel(steps, agg_ref, weight_ref, bias_ref, out_ref, buffer, sems):
    size = agg_ref.shape[0] // steps
    copies = []
    for i in range(steps):
        span = pl.ds(i * size, size)
        output = jnp.dot(agg_ref[span, :], weight_ref[...], preferred_element_type=jnp.float32) + bias_ref[...]
        buffer[span, :] = jnp.maximum(output, 0.0).astype(buffer.dtype)
        copies.append(pltpu.make_async_copy(buffer.at[span], out_ref.at[span], sems.at[i]))
        copies[i].start()
    for copy in copies:
        copy.wait()


def activate(aggregated, weight, bias):
    rows, width = aggregated.shape
    hidden = weight.shape[1]
    steps = largest_divisor(rows // 16, OUT_STEPS)
    vmem = pl.BlockSpec(memory_space=pltpu.VMEM)
    return pl.pallas_call(
        functools.partial(activate_kernel, steps),
        out_shape=jax.ShapeDtypeStruct((rows, hidden), jnp.bfloat16),
        in_specs=[vmem, vmem, vmem],
        out_specs=pl.BlockSpec(memory_space=pltpu.HBM),
        scratch_shapes=[pltpu.VMEM((rows, hidden), jnp.bfloat16), pltpu.SemaphoreType.DMA((steps,))],
        compiler_params=pltpu.CompilerParams(vmem_limit_bytes=GRANT),
        name="activate",
    )(aggregated, weight, bias[None, :])


def shards(blocks, replicas, features, weight, bias, tile_values, tile_place, tile_count):
    sources, held = gather_sources(features, tile_values, blocks, replicas)
    part = section_sums(sources, held, tile_place, tile_count)
    if replicas == 4:
        return flush(swap_and_activate(part, weight, bias))
    return activate(replica_sum(part, replicas), weight, bias)


def solution(mesh):
    in_specs = (
        P("blk", None),
        P(),
        P(),
        P("blk", "rep", None, None, None),
        P("blk", "rep", None),
        P("blk", "rep"),
    )
    body = functools.partial(shards, mesh.shape["blk"], mesh.shape["rep"])
    return jax.shard_map(body, mesh=mesh, in_specs=in_specs, out_specs=P("blk", None), check_vma=False)
```

```python
import functools
import heapq
import random

import jax
import jax.numpy as jnp
from jax import lax
from jax.experimental import pallas as pl
from jax.experimental.pallas import tpu as pltpu
from jax.sharding import PartitionSpec as P

MESH = pl.DeviceIdType.MESH
GROUP = 80
CHUNKS = 4
PIECES = 16
HOP = 7
WAIT = 5
ROUNDS = 40
LEAD = 0
PASSES = 768
SEED = 36660
EXPRESS = 1
URGENCY = 0.2
TOLL = 1.0
SPREAD = 4.0
OUT_STEPS = 8
SWAPS = (1,) * 8
GRANT = 16 * 1024 * 1024


def largest_divisor(number, most):
    return max(d for d in range(1, most + 1) if number % d == 0)


def chip_grid(blocks, replicas):
    columns = 2
    floors, planes = blocks // columns, replicas // 2
    chips = [(z, x, y) for z in range(floors) for x in range(columns) for y in range(planes)]
    ways = {}
    for z, x, y in chips:
        out = [(0, (z, columns - 1 - x, y), [(z, x, y, 0)])]
        out += [(3, (z, x, 1 - y), [(z, x, y, 3)])] if planes == 2 else [
            (3 + (side < 0), (z, x, y + side), [(z, x, y, 3 + (side < 0))])
            for side in (1, -1) if 0 <= y + side < planes]
        for far in range(1, EXPRESS + 1):
            for side in (1, -1):
                if 0 <= z + side * far < floors:
                    first = 1 if far == 1 else 2 * far + 1
                    crossed = [(z + side * k, x, y, 1 + (side < 0)) for k in range(far)]
                    out.append((first + (side < 0), (z + side * far, x, y), crossed))
        ways[z, x, y] = out
    return columns, planes, chips, ways


def plan_trees(blocks, replicas, sections, pieces, hop, passes):
    columns, planes, chips, ways = chip_grid(blocks, replicas)
    order = {chip: i for i, chip in enumerate(chips)}
    core_of = {}
    for b in range(blocks):
        for r in range(replicas):
            for i in range(sections):
                core_of[(b // columns, b % columns, r // 2), (b - r * sections - i) % blocks] = r % 2
    roots = {s: [(s // columns, s % columns, y) for y in range(planes)] for s in range(blocks)}
    wants = {s: [c for c in chips if (c, s) in core_of and c not in roots[s]] for s in range(blocks)}
    busy = {link: 0 for chip in chips for _, _, crossed in ways[chip] for link in crossed}
    load = dict.fromkeys(busy, 0)
    past = dict.fromkeys(busy, 0.0)
    trees, best, mine = {}, None, {}
    keys = [(s, p) for p in range(pieces) for s in range(blocks)]
    turn, draw = list(keys), SEED

    def grow(s, price):
        ready = dict.fromkeys(roots[s], 0)
        left, tree = set(wants[s]), []
        while left:
            cost, came, done = {}, {}, set()
            heap = [(URGENCY * t, t, order[c], c) for c, t in ready.items()]
            heapq.heapify(heap)
            while True:
                c, t, _, chip = heapq.heappop(heap)
                if chip in done:
                    continue
                done.add(chip)
                if chip in left:
                    break
                for way, other, crossed in ways[chip]:
                    if other in ready or other in done:
                        continue
                    taken, toll = 0, 0.0
                    for link in crossed:
                        taken |= busy[link]
                        toll += price[link] + SPREAD * mine.get((s, link), 0) / pieces
                    taken >>= t
                    start = t + (~taken & (taken + 1)).bit_length() - 1
                    there = start + hop + len(crossed) - 1
                    total = c + URGENCY * (there - t) + toll
                    if other not in cost or total < cost[other]:
                        cost[other] = total
                        came[other] = (chip, way, start, crossed, there)
                        heapq.heappush(heap, (total, there, order[other], other))
            path = []
            while chip not in ready:
                path.append(came[chip] + (chip,))
                chip = came[chip][0]
            for chip, way, start, crossed, there, other in reversed(path):
                ready[other] = there
                for link in crossed:
                    busy[link] |= 1 << start
                    load[link] += 1
                    mine[s, link] = mine.get((s, link), 0) + 1
                tree.append((chip, way, start, other, crossed))
                left.discard(other)
        return tree

    for _ in range(passes):
        for key in turn:
            for _, _, start, _, crossed in trees.get(key, ()):
                for link in crossed:
                    busy[link] &= ~(1 << start)
                    load[link] -= 1
                    mine[key[0], link] -= 1
            top = max(max(load.values()), 1)
            trees[key] = grow(key[0], {k: TOLL * (past[k] + (load[k] / top) ** 4) for k in load})
        last = {key: max(start for _, _, start, _, _ in tree) for key, tree in trees.items()}
        span = max(last.values())
        score = (span, sum(v >= span - 1 for v in last.values()), sum(load.values()))
        if best is None or score < best[0]:
            best = (score, {key: list(tree) for key, tree in trees.items()})
        top = max(load.values())
        for k in load:
            past[k] = past[k] * 0.9 + (0.2 if load[k] >= top - pieces * 0.05 else 0.0)
        ranks = []
        for key in keys:
            draw = (draw * 1103515245 + 12345) % (1 << 31)
            ranks.append(((draw >> 8) % 1000 / 125 - last[key], key))
        turn = [key for _, key in sorted(ranks)]
    return best[1], core_of


def list_times(trees, hop, bonus):
    kids, to_go, queues, arrivals = {}, {}, {}, {}
    starts, last, number, slot = {}, dict.fromkeys(trees, 0), 0, 0
    left = sum(len(tree) for tree in trees.values())

    def enqueue(key, i):
        nonlocal number
        chip, way = trees[key][i][:2]
        heapq.heappush(queues.setdefault((chip, way), []), (-(to_go[key][i] * hop + bonus[key]), number, key, i))
        number += 1

    for key, tree in trees.items():
        kids[key], to_go[key] = {}, {}
        for i, (chip, _, _, _, _) in enumerate(tree):
            kids[key].setdefault(chip, []).append(i)
        for i in reversed(range(len(tree))):
            to_go[key][i] = 1 + max([to_go[key][j] for j in kids[key].get(tree[i][3], [])], default=0)
        reached = {other for _, _, _, other, _ in tree}
        for i, (chip, _, _, _, _) in enumerate(tree):
            if chip not in reached:
                enqueue(key, i)
    while left:
        for key, i in arrivals.pop(slot, []):
            for j in kids[key].get(trees[key][i][3], []):
                enqueue(key, j)
        for queue in queues.values():
            if queue:
                _, _, key, i = heapq.heappop(queue)
                starts[key, i] = slot
                arrivals.setdefault(slot + hop, []).append((key, i))
                last[key] = max(last[key], slot + hop)
                left -= 1
        slot += 1
    return starts, last


def retime(trees, hop, rounds):
    draw, bonus, best = random.Random(1), dict.fromkeys(trees, 0.0), None
    for _ in range(rounds):
        starts, last = list_times(trees, hop, bonus)
        span = max(last.values())
        score = (span, sum(v >= span - 1 for v in last.values()))
        if best is None or score < best[0]:
            best = (score, starts)
        for key in bonus:
            late = 1.0 if last[key] >= span - 1 else 0.3 if last[key] >= span - 3 else 0.0
            bonus[key] = bonus[key] * 0.95 + late * draw.random() * 2
    return {
        key: [(chip, way, best[1][key, i], other, crossed) for i, (chip, way, _, other, crossed) in enumerate(tree)]
        for key, tree in trees.items()}


def plan_gather(blocks, replicas, sections, pieces, hop, passes):
    trees, core_of = plan_trees(blocks, replicas, sections, pieces, hop, passes)
    trees = retime(trees, WAIT, ROUNDS)
    columns, planes, chips, _ = chip_grid(blocks, replicas)
    devices = blocks * replicas
    actions = [[] for _ in range(devices)]
    arrived = [set() for _ in range(devices)]

    def core(chip, s, p):
        return core_of.get((chip, s), p % 2) if chip[:2] != (s // columns, s % columns) else p % 2

    def device(chip, c):
        return (chip[0] * columns + chip[1]) * replicas + chip[2] * 2 + c

    for (s, p), tree in sorted(trees.items()):
        for chip, way, start, other, _ in tree:
            here, there = core(chip, s, p), core(other, s, p)
            own = chip[:2] == (s // columns, s % columns)
            actions[device(chip, here)].append((start - (LEAD if own else 0), not own, s * pieces + p, way, there))
            arrived[device(other, there)].add(s * pieces + p)
    plans = []
    for d in range(devices):
        slots, waited = [], set()
        for _, relay, piece, way, there in sorted(actions[d]):
            spot = None
            for j in range(len(slots) - 1, -1, -1):
                if slots[j][0] == piece:
                    spot = j
                    break
                if way in slots[j][2]:
                    break
            if spot is None:
                slots.append((piece, relay and piece not in waited, {}))
                spot = len(slots) - 1
                if relay:
                    waited.add(piece)
            slots[spot][2][way] = there
        leaves = arrived[d] - waited
        plans.append((slots, leaves))
    return plans


def used_ways(plans):
    used = {way for slots, _ in plans for _, _, sends in slots for way in sends}
    pairs = {1: 2, 2: 1, 3: 3, 4: 3}
    return sorted(used | {0 if w == 0 else pairs.get(w, w + 1 if w % 2 else w - 1) for w in used})


def gather_kernel(blocks, replicas, sections, pieces, plans, features_ref, tiles_ref, all_ref, held_ref,
                  table_ref, recv_sem, send_sem, own_sem, held_sem):
    blk, rep = lax.axis_index("blk"), lax.axis_index("rep")
    columns, planes, _, _ = chip_grid(blocks, replicas)
    floors = blocks // columns
    rows = features_ref.shape[0]
    size = rows // pieces
    z, x = lax.div(blk, columns), lax.rem(blk, columns)
    y, me = lax.div(rep, 2), lax.rem(rep, 2)
    is_blk = [blk == b for b in range(blocks)]
    is_rep = [rep == r for r in range(replicas)]

    def choose(options, tests):
        value = jnp.int32(options[0])
        for option, test in zip(options[1:], tests[1:]):
            value = jnp.where(test, option, value)
        return value

    def pick(values):
        if len(set(values)) == 1:
            return jnp.int32(values[0])
        picked = []
        for b in range(blocks):
            row = values[b * replicas:(b + 1) * replicas]
            picked.append(row[0] if len(set(row)) == 1 else choose(row, is_rep))
        return choose(picked, is_blk)

    def target(way, c):
        if way == 0:
            return (z * columns + (columns - 1 - x), y * 2 + c)
        if way in (3, 4):
            return (blk, (1 - y if planes == 2 else y + (1 if way == 3 else -1)) * 2 + c)
        far = 1 if way < 3 else (way - 1) // 2
        return (blk + (far if way % 2 else -far) * columns, y * 2 + c)

    exists = {}
    for way in used_ways(plans):
        if way == 0 or (way == 3 and planes == 2):
            exists[way] = None
        elif way in (3, 4):
            exists[way] = y < planes - 1 if way == 3 else y > 0
        else:
            far = 1 if way < 3 else (way - 1) // 2
            exists[way] = z < floors - far if way % 2 else z >= far

    own = pltpu.make_async_copy(features_ref, all_ref.at[blk], own_sem)
    own.start()
    barrier = pltpu.get_barrier_semaphore()
    count = jnp.int32(0)
    for way, test in exists.items():
        def greet(way=way):
            for c in range(2):
                pl.semaphore_signal(barrier, inc=1, device_id=target(way, c), device_id_type=MESH)
        if test is None:
            greet()
            count = count + 2
        else:
            pl.when(test)(greet)
            count = count + jnp.where(test, 2, 0)
    steps = max(len(slots) for slots, _ in plans)
    ways = sorted(exists)
    shift = pieces.bit_length() - 1
    for j in range(steps):
        values = []
        for slots, _ in plans:
            piece, relay, sends = slots[j] if j < len(slots) else (0, False, {})
            values.append((piece * 2 + int(relay) << 2 * len(ways)) + sum(2 + sends[w] << 2 * k for k, w in enumerate(ways) if w in sends))
        table_ref[j] = pick(values)
    run = min(pieces, 16)
    words = [(i, first) for i in range(sections) for first in range(0, pieces, run)]
    for n, (i, first) in enumerate(words):
        values = []
        for d, (_, leaves) in enumerate(plans):
            s = (d // replicas - d % replicas * sections - i) % blocks
            values.append(sum(1 << p for p in range(run) if s * pieces + first + p in leaves))
        table_ref[steps + n] = pick(values)
    pl.semaphore_wait(barrier, count)

    def block(piece):
        return all_ref.at[piece >> shift, pl.ds(pl.multiple_of((piece & (pieces - 1)) * size, size), size)]

    def copy(piece, way, c, j):
        return pltpu.make_async_remote_copy(
            src_ref=block(piece), dst_ref=block(piece), send_sem=send_sem.at[j, ways.index(way)],
            recv_sem=recv_sem.at[piece], device_id=target(way, c), device_id_type=MESH)

    def unpack(j):
        value = table_ref[j]
        return value >> (2 * len(ways) + 1), (value >> (2 * len(ways))) & 1 == 1, [
            (way, (value >> (2 * k + 1)) & 1 == 1, (value >> (2 * k)) & 1) for k, way in enumerate(ways)]

    own.wait()
    held = pltpu.make_async_copy(tiles_ref, held_ref, held_sem)
    held.start()

    def step(j, carry):
        piece, relay, sends = unpack(j)
        pl.when(relay)(lambda: copy(piece, 0, 0, j).wait_recv())
        for way, test, c in sends:
            pl.when(test)(lambda way=way, c=c: copy(piece, way, c, j).start())
        return carry

    def drain(j, carry):
        piece, _, sends = unpack(j)
        for way, test, c in sends:
            pl.when(test)(lambda way=way, c=c: copy(piece, way, c, j).wait_send())
        return carry

    lax.fori_loop(0, steps, step, 0)
    lax.fori_loop(0, steps, drain, 0)
    for n, (i, first) in enumerate(words):
        source = lax.rem(blk - rep * sections - i + blocks, blocks)
        mask = table_ref[steps + n]

        def leaf(p, carry, start=source * pieces + first, mask=mask):
            pl.when((mask >> p) & 1 == 1)(lambda: copy(start + p, 0, 0, 0).wait_recv())
            return carry

        lax.fori_loop(0, run, leaf, 0)
    held.wait()


def gather_sources(features, tile_values, blocks, replicas):
    sections = tile_values.shape[1]
    rows, width = features.shape
    pieces = PIECES
    while rows % (16 * pieces):
        pieces //= 2
    plans = plan_gather(blocks, replicas, sections, pieces, HOP, max(2, PASSES // (blocks * replicas)))
    steps = max(len(slots) for slots, _ in plans)
    ways = len(used_ways(plans))
    vmem = pl.BlockSpec(memory_space=pltpu.VMEM)
    hbm = pl.BlockSpec(memory_space=pltpu.HBM)
    dma = pltpu.SemaphoreType.DMA
    return pl.pallas_call(
        functools.partial(gather_kernel, blocks, replicas, sections, pieces, plans),
        out_shape=(
            jax.ShapeDtypeStruct((blocks, rows, width), features.dtype),
            jax.ShapeDtypeStruct(tile_values.shape, tile_values.dtype),
        ),
        in_specs=[hbm, hbm],
        out_specs=(vmem, vmem),
        scratch_shapes=[
            pltpu.SMEM((steps + sections * pl.cdiv(pieces, 16),), jnp.int32), dma((blocks * pieces,)), dma((steps, ways)), dma(()), dma(())
        ],
        compiler_params=pltpu.CompilerParams(collective_id=1, has_side_effects=True, vmem_limit_bytes=2 * GRANT),
        cost_estimate=pl.CostEstimate(
            flops=0, bytes_accessed=96 * rows * width * features.dtype.itemsize, transcendentals=0
        ),
        name="gather_sources",
    )(pltpu.with_memory_space_constraint(features, pltpu.HBM), tile_values)


def sections_kernel(group, place_ref, count_ref, source_ref, tiles_ref, acc_ref):
    sections, slots, tile = tiles_ref.shape[1:4]
    blocks, row_tiles = source_ref.shape[0], source_ref.shape[1] // tile
    blk, rep = lax.axis_index("blk"), lax.axis_index("rep")
    acc_ref[...] = jnp.zeros_like(acc_ref)
    for section in range(sections):
        source = lax.rem(blk - rep * sections - section + blocks, blocks)
        count = count_ref[0, section]

        def body(g, carry, size=group, first=0, section=section, source=source, count=count):
            for u in range(size):
                k = first + g * size + u
                place = place_ref[0, section, k]
                column, target = lax.rem(place, row_tiles), lax.div(place, row_tiles)
                piece = source_ref[source, pl.ds(pl.multiple_of(column * tile, tile), tile), :]
                product = jnp.dot(tiles_ref[0, section, k], piece, preferred_element_type=jnp.float32)
                rows = pl.ds(pl.multiple_of(target * tile, tile), tile)
                acc_ref[rows, :] += jnp.where(k < count, product, 0.0)
            return carry

        half = group // 2 if group % 2 == 0 else group
        full = lax.div(count + group - half - 1, group)
        lax.fori_loop(0, full, body, 0)
        if half < group:
            left = count - full * group
            lax.fori_loop(0, jnp.where(left > 0, 1, 0), functools.partial(body, size=half, first=full * group), 0)


def section_sums(sources, tile_values, tile_place, tile_count):
    slots = tile_values.shape[2]
    rows, width = sources.shape[1:]
    vmem = pl.BlockSpec(memory_space=pltpu.VMEM)
    smem = pl.BlockSpec(memory_space=pltpu.SMEM)
    return pl.pallas_call(
        functools.partial(sections_kernel, largest_divisor(slots, GROUP)),
        out_shape=jax.ShapeDtypeStruct((rows, width), jnp.float32),
        in_specs=[smem, smem, vmem, vmem],
        out_specs=vmem,
        compiler_params=pltpu.CompilerParams(vmem_limit_bytes=2 * GRANT),
        name="section_sums",
    )(tile_place, tile_count, sources, tile_values)


def swap_kernel(sizes, part_ref, weight_ref, bias_ref, act_ref, agg_ref, core_in, send_buf, recv_buf,
                s1, r1, s2, r2, s3, r3):
    blk, rep = lax.axis_index("blk"), lax.axis_index("rep")
    core, chip = lax.rem(rep, 2), lax.div(rep, 2)
    half = part_ref.shape[0] // 2
    other, across = chip * 2 + (1 - core), (1 - chip) * 2 + core
    chunks = len(sizes)
    spans = [pl.ds(sum(sizes[:ch]), sizes[ch]) for ch in range(chunks)]

    def place(which, ch):
        return pl.ds(pl.multiple_of(which * half + sum(sizes[:ch]), min(sizes)), sizes[ch])

    def finish(which, ch):
        span = place(which, ch)
        output = jnp.dot(agg_ref[span, :], weight_ref[...], preferred_element_type=jnp.float32) + bias_ref[...]
        act_ref[span, :] = jnp.maximum(output, 0.0).astype(act_ref.dtype)

    barrier = pltpu.get_barrier_semaphore()
    for target in (other, across):
        pl.semaphore_signal(barrier, inc=1, device_id=(blk, target), device_id_type=MESH)
    pl.semaphore_wait(barrier, 2)

    stage1, stage2, stage3 = [], [], []
    for ch, span in enumerate(spans):
        stage1.append(pltpu.make_async_remote_copy(
            src_ref=part_ref.at[place(1 - core, ch)], dst_ref=core_in.at[span],
            send_sem=s1.at[ch], recv_sem=r1.at[ch], device_id=(blk, other), device_id_type=MESH))
        stage1[ch].start()
    for ch, span in enumerate(spans):
        stage1[ch].wait_recv()
        send_buf[span, :] = (part_ref[place(core, ch), :] + core_in[span, :]).astype(send_buf.dtype)
        stage2.append(pltpu.make_async_remote_copy(
            src_ref=send_buf.at[span], dst_ref=recv_buf.at[span],
            send_sem=s2.at[ch], recv_sem=r2.at[ch], device_id=(blk, across), device_id_type=MESH))
        stage2[ch].start()
    for ch, span in enumerate(spans):
        stage2[ch].wait_recv()
        mine = place(core, ch)
        total = send_buf[span, :].astype(jnp.float32) + recv_buf[span, :].astype(jnp.float32)
        agg_ref[mine, :] = total.astype(agg_ref.dtype)
        stage3.append(pltpu.make_async_remote_copy(
            src_ref=agg_ref.at[mine], dst_ref=agg_ref.at[mine],
            send_sem=s3.at[ch], recv_sem=r3.at[ch], device_id=(blk, other), device_id_type=MESH))
        stage3[ch].start()
        finish(core, ch)
        if ch:
            stage3[ch - 1].wait_recv()
            finish(1 - core, ch - 1)
    for ch in range(chunks):
        stage1[ch].wait_send()
        stage2[ch].wait_send()
    stage3[chunks - 1].wait_recv()
    finish(1 - core, chunks - 1)
    for ch in range(chunks):
        stage3[ch].wait_send()


def swap_and_activate(part, weight, bias):
    rows, width = part.shape
    hidden = weight.shape[1]
    half = rows // 2
    unit = half // sum(SWAPS)
    sizes = [unit * share for share in SWAPS] if unit * sum(SWAPS) == half and unit % 16 == 0 else [half]
    dma = pltpu.SemaphoreType.DMA((len(sizes),))
    vmem = pl.BlockSpec(memory_space=pltpu.VMEM)
    return pl.pallas_call(
        functools.partial(swap_kernel, sizes),
        out_shape=jax.ShapeDtypeStruct((rows, hidden), jnp.bfloat16),
        in_specs=[vmem, vmem, vmem],
        out_specs=vmem,
        scratch_shapes=[
            pltpu.VMEM((rows, width), jnp.bfloat16),
            pltpu.VMEM((half, width), jnp.float32),
            pltpu.VMEM((half, width), jnp.bfloat16),
            pltpu.VMEM((half, width), jnp.bfloat16),
        ] + [dma] * 6,
        compiler_params=pltpu.CompilerParams(collective_id=0, has_side_effects=True, vmem_limit_bytes=GRANT),
        name="swap_and_activate",
    )(part, weight, bias[None, :])


def flush_kernel(steps, act_ref, out_ref, sems):
    size = act_ref.shape[0] // steps
    spans = [pl.ds(i * size, size) for i in range(steps)]
    copies = [pltpu.make_async_copy(act_ref.at[span], out_ref.at[span], sems.at[i]) for i, span in enumerate(spans)]
    for copy in copies:
        copy.start()
    for copy in copies:
        copy.wait()


def flush(activations):
    steps = largest_divisor(activations.shape[0] // 16, OUT_STEPS)
    return pl.pallas_call(
        functools.partial(flush_kernel, steps),
        out_shape=jax.ShapeDtypeStruct(activations.shape, activations.dtype),
        in_specs=[pl.BlockSpec(memory_space=pltpu.VMEM)],
        out_specs=pl.BlockSpec(memory_space=pltpu.HBM),
        scratch_shapes=[pltpu.SemaphoreType.DMA((steps,))],
        compiler_params=pltpu.CompilerParams(vmem_limit_bytes=GRANT),
        name="flush",
    )(activations)


def reduce_kernel(chips, chunks, part_ref, agg_ref, core_in, send_buf, recv_buf,
                  s1, r1, s2, r2, s3, r3, s4, r4):
    blk, rep = lax.axis_index("blk"), lax.axis_index("rep")
    core, chip = lax.rem(rep, 2), lax.div(rep, 2)
    rows = part_ref.shape[0]
    half = rows // 2
    size = half // chips // chunks
    other = chip * 2 + (1 - core)

    def peer(d):
        return lax.rem(chip + d, chips)

    def local(piece, ch):
        return pl.ds(pl.multiple_of((piece * chunks + ch) * size, size), size)

    def place(which, piece, ch):
        return pl.ds(pl.multiple_of(which * half + (piece * chunks + ch) * size, size), size)

    barrier = pltpu.get_barrier_semaphore()
    pl.semaphore_signal(barrier, inc=1, device_id=(blk, other), device_id_type=MESH)
    for d in range(1, chips):
        pl.semaphore_signal(barrier, inc=1, device_id=(blk, peer(d) * 2 + core), device_id_type=MESH)
    pl.semaphore_wait(barrier, chips)

    order = [(ch, d) for ch in range(chunks) for d in list(range(1, chips)) + [0]]
    stage1, stage2, stage3, stage4 = {}, {}, {}, {}
    for ch, d in order:
        copy = pltpu.make_async_remote_copy(
            src_ref=part_ref.at[place(1 - core, peer(d), ch)], dst_ref=core_in.at[local(peer(d), ch)],
            send_sem=s1.at[d, ch], recv_sem=r1.at[d, ch], device_id=(blk, other), device_id_type=MESH)
        copy.start()
        stage1[ch, d] = copy
    for ch, d in order:
        if d == 0:
            continue
        stage1[ch, d].wait_recv()
        total = part_ref[place(core, peer(d), ch), :] + core_in[local(peer(d), ch), :]
        send_buf[d - 1, ch] = total.astype(jnp.bfloat16)
        copy = pltpu.make_async_remote_copy(
            src_ref=send_buf.at[d - 1, ch], dst_ref=recv_buf.at[d - 1, ch],
            send_sem=s2.at[d, ch], recv_sem=r2.at[d, ch],
            device_id=(blk, peer(d) * 2 + core), device_id_type=MESH)
        copy.start()
        stage2[ch, d] = copy
    for ch in range(chunks):
        stage1[ch, 0].wait_recv()
        total = part_ref[place(core, chip, ch), :] + core_in[local(chip, ch), :]
        for d in range(1, chips):
            stage2[ch, d].wait_recv()
            total = total + recv_buf[d - 1, ch].astype(jnp.float32)
        mine = place(core, chip, ch)
        agg_ref[mine, :] = total.astype(jnp.bfloat16)
        for d in list(range(1, chips)) + [0]:
            target = other if d == 0 else peer(d) * 2 + core
            copy = pltpu.make_async_remote_copy(
                src_ref=agg_ref.at[mine], dst_ref=agg_ref.at[mine],
                send_sem=s3.at[d, ch], recv_sem=r3.at[d, ch],
                device_id=(blk, target), device_id_type=MESH)
            copy.start()
            stage3[ch, d] = copy
    for ch in range(chunks):
        for d in range(1, chips):
            stage3[ch, d].wait_recv()
            came = place(core, lax.rem(chip + chips - d, chips), ch)
            copy = pltpu.make_async_remote_copy(
                src_ref=agg_ref.at[came], dst_ref=agg_ref.at[came],
                send_sem=s4.at[d, ch], recv_sem=r4.at[d, ch],
                device_id=(blk, other), device_id_type=MESH)
            copy.start()
            stage4[ch, d] = copy
    for ch, d in order:
        stage1[ch, d].wait_send()
        stage3[ch, d].wait_send()
        if d == 0:
            stage3[ch, d].wait_recv()
        else:
            stage2[ch, d].wait_send()
            stage4[ch, d].wait()


def replica_sum(part, replicas):
    rows, width = part.shape
    chips = replicas // 2
    chunks = largest_divisor(rows // 2 // chips // 16, CHUNKS)
    size = rows // 2 // chips // chunks
    dma = pltpu.SemaphoreType.DMA((chips, chunks))
    vmem = pl.BlockSpec(memory_space=pltpu.VMEM)
    return pl.pallas_call(
        functools.partial(reduce_kernel, chips, chunks),
        out_shape=jax.ShapeDtypeStruct((rows, width), jnp.bfloat16),
        in_specs=[vmem],
        out_specs=vmem,
        scratch_shapes=[
            pltpu.VMEM((rows // 2, width), jnp.float32),
            pltpu.VMEM((chips - 1, chunks, size, width), jnp.bfloat16),
            pltpu.VMEM((chips - 1, chunks, size, width), jnp.bfloat16),
        ] + [dma] * 8,
        compiler_params=pltpu.CompilerParams(collective_id=0, has_side_effects=True, vmem_limit_bytes=GRANT),
        name="replica_sum",
    )(part)


def activate_kernel(steps, agg_ref, weight_ref, bias_ref, out_ref, buffer, sems):
    size = agg_ref.shape[0] // steps
    copies = []
    for i in range(steps):
        span = pl.ds(i * size, size)
        output = jnp.dot(agg_ref[span, :], weight_ref[...], preferred_element_type=jnp.float32) + bias_ref[...]
        buffer[span, :] = jnp.maximum(output, 0.0).astype(buffer.dtype)
        copies.append(pltpu.make_async_copy(buffer.at[span], out_ref.at[span], sems.at[i]))
        copies[i].start()
    for copy in copies:
        copy.wait()


def activate(aggregated, weight, bias):
    rows, width = aggregated.shape
    hidden = weight.shape[1]
    steps = largest_divisor(rows // 16, OUT_STEPS)
    vmem = pl.BlockSpec(memory_space=pltpu.VMEM)
    return pl.pallas_call(
        functools.partial(activate_kernel, steps),
        out_shape=jax.ShapeDtypeStruct((rows, hidden), jnp.bfloat16),
        in_specs=[vmem, vmem, vmem],
        out_specs=pl.BlockSpec(memory_space=pltpu.HBM),
        scratch_shapes=[pltpu.VMEM((rows, hidden), jnp.bfloat16), pltpu.SemaphoreType.DMA((steps,))],
        compiler_params=pltpu.CompilerParams(vmem_limit_bytes=GRANT),
        name="activate",
    )(aggregated, weight, bias[None, :])


def shards(blocks, replicas, features, weight, bias, tile_values, tile_place, tile_count):
    sources, held = gather_sources(features, tile_values, blocks, replicas)
    part = section_sums(sources, held, tile_place, tile_count)
    if replicas == 4:
        return flush(swap_and_activate(part, weight, bias))
    return activate(replica_sum(part, replicas), weight, bias)


def solution(mesh):
    in_specs = (
        P("blk", None),
        P(),
        P(),
        P("blk", "rep", None, None, None),
        P("blk", "rep", None),
        P("blk", "rep"),
    )
    body = functools.partial(shards, mesh.shape["blk"], mesh.shape["rep"])
    return jax.shard_map(body, mesh=mesh, in_specs=in_specs, out_specs=P("blk", None), check_vma=False)
```
